32 devices in a mesh: dp: 8 (over z, y), mp: 4 (over x, core).
Axes of the slice: x: 2, y: 2, z: 4, core: 2. Of those that a mesh axis runs over, the one named last changes fastest.
Arguments:
- tokens: bfloat16 [8192, 768], P('dp'), may hold values from -6 to 6
- seg_counts: int32 [16], replicated, may hold values from 1 to 16, 64 in all
- seg_order: int32 [64], replicated, may hold values from 0 to 63, each once
- seg_qkv: bfloat16 [768, 3, 768], P(None, None, 'mp'), may hold values from -0.21875 to 0.21875
- seg_qv_bias: float32 [2, 768], P(None, 'mp'), may hold values from -1.75 to 1.75
- seg_out: bfloat16 [768, 768], P('mp'), may hold values from -0.875 to 0.875
- seg_up: bfloat16 [768, 3072], P(None, 'mp'), may hold values from -0.21875 to 0.21875
- seg_up_bias: float32 [3072], P('mp'), may hold values from -1.75 to 1.75
- seg_down: bfloat16 [3072, 768], P('mp'), may hold values from -0.109375 to 0.109375
- seg_gains: float32 [2, 768], replicated, may hold values from 0.5 to 1.5
- seg_shifts: float32 [4, 768], replicated, may hold values from -1.75 to 1.75
- cls_qkv: bfloat16 [768, 3, 768], P(None, None, 'mp'), may hold values from -0.21875 to 0.21875
- cls_qv_bias: float32 [2, 768], P(None, 'mp'), may hold values from -1.75 to 1.75
- cls_out: bfloat16 [768, 768], P('mp'), may hold values from -0.875 to 0.875
- cls_up: bfloat16 [768, 3072], P(None, 'mp'), may hold values from -0.21875 to 0.21875
- cls_up_bias: float32 [3072], P('mp'), may hold values from -1.75 to 1.75
- cls_down: bfloat16 [3072, 768], P('mp'), may hold values from -0.109375 to 0.109375
- cls_gains: float32 [2, 768], replicated, may hold values from 0.5 to 1.5
- cls_shifts: float32 [4, 768], replicated, may hold values from -1.75 to 1.75
- pos_table: bfloat16 [64, 768], replicated, may hold values from -3 to 3
- cotangent: bfloat16 [8192, 768], P('dp'), may hold values from -6 to 6
Outputs:
- layer_out: bfloat16 [8192, 768], P('dp')
- tokens_grad: float32 [8192, 768], P('dp')
- seg_qkv_grad: float32 [768, 3, 768], P(None, None, 'mp')
- seg_qv_bias_grad: float32 [2, 768], P(None, 'mp')
- seg_out_grad: float32 [768, 768], P('mp')
- seg_up_grad: float32 [768, 3072], P(None, 'mp')
- seg_up_bias_grad: float32 [3072], P('mp')
- seg_down_grad: float32 [3072, 768], P('mp')
- seg_gains_grad: float32 [2, 768], replicated
- seg_shifts_grad: float32 [4, 768], replicated
- cls_qkv_grad: float32 [768, 3, 768], P(None, None, 'mp')
- cls_qv_bias_grad: float32 [2, 768], P(None, 'mp')
- cls_out_grad: float32 [768, 768], P('mp')
- cls_up_grad: float32 [768, 3072], P(None, 'mp')
- cls_up_bias_grad: float32 [3072], P('mp')
- cls_down_grad: float32 [3072, 768], P('mp')
- cls_gains_grad: float32 [2, 768], replicated
- cls_shifts_grad: float32 [4, 768], replicated
- pos_table_grad: float32 [64, 768], replicated
The draws below stay inside these ranges and needn't reach their ends.
Inputs may be any that keep to these rules, and one draw needn't show every extreme that they name: `seg_counts`: the counts sum to 64; the largest is exactly 16. `seg_order`: every segment number appears once.
All inputs are finite; a program needn't handle non-finite values.
Results may differ from the reference program's by a relative error of at most 0.02.
Values may be sent and summed in bfloat16 or wider, within the bound.
No kernel may reach another device: no remote copies, remote signals or barrier semaphores. Data moves between devices by JAX's collectives and lax.ppermute only.
A program may use at most 128 MiB of HBM per device.

```python
import math
import jax
import jax.numpy as jnp
import numpy as np
from jax import lax

D = 768
FF = 3072
HEADS = 12
HEAD = 64
SEG = 128
MAX_SEGS = 64
TOK_DEV = 1024
SEGMENTS = 64
TOKENS = 8192
DOCS = 16
MOST_SEGS = 16
N_DP = 8


def block_levels(own_key, extent, cuts, smallest, top_value):
    level, own = 1.0, jax.random.fold_in(own_key, 6)
    for position, parts in cuts:
        steps = jnp.exp(jax.random.uniform(jax.random.fold_in(own, position), (parts,), jnp.float32, smallest / len(cuts), top_value / len(cuts)))
        level = level * jnp.repeat(steps, extent[position] // parts).reshape([-1 if axis == position else 1 for axis in range(len(extent))])
    return level


def length_profile(number_of, total, most, lean):
    portions = [(1 << 20) // math.isqrt(standing ** lean) + 1 for standing in range(2, number_of + 1)]
    rest, holding = total - most - (number_of - 1), [1] * (number_of - 1)
    while rest > 0:
        movable = [i for i in range(number_of - 1) if holding[i] < most]
        whole, remaining = sum([portions[i] for i in movable]), rest
        for i in movable:
            more = min(most - holding[i], max(1, remaining * portions[i] // whole), rest)
            holding[i] = holding[i] + more
            rest = rest - more
    return np.array([most] + holding)


def ragged(own_key, number_of, total, bound, skew):
    if number_of == 2:
        one = jax.random.randint(own_key, (), max(1, total - bound), min(bound, total - 1) + 1)
        return jnp.stack([one, total - one])
    tallies = jnp.asarray(length_profile(number_of, total, bound, skew), jnp.int32)
    couples = (number_of - 1) // 2
    donor, receiver = tallies[1:1 + 2 * couples:2], tallies[2:2 + 2 * couples:2]
    room = jnp.minimum(donor - 1, bound - receiver)
    moved = jax.random.randint(jax.random.fold_in(own_key, 1), (couples,), 0, 1 << 20) % (room + 1)
    tallies = tallies.at[1:1 + 2 * couples:2].set(donor - moved).at[2:2 + 2 * couples:2].set(receiver + moved)
    return tallies[jax.random.permutation(jax.random.fold_in(own_key, 2), number_of)]


def bell_draw(stream_key, extent, width, most, split=(), kind=jnp.bfloat16):
    loudness = block_levels(stream_key, extent, split, -0.22, 0.18) if split else 1.0
    entries = jax.random.normal(stream_key, extent, jnp.float32) * width * loudness
    return jnp.minimum(jnp.maximum(entries, -most), most).astype(kind)


def setup_inputs(seed: int = 0) -> dict:
    key_list = jax.random.split(jax.random.key(seed), 22)
    return {
        "tokens": bell_draw(key_list[0], (TOKENS, D), 1.0, 6.0, ((0, 8),)),
        "seg_counts": ragged(key_list[1], DOCS, SEGMENTS, MOST_SEGS, 2).astype(jnp.int32),
        "seg_order": jax.random.permutation(key_list[2], SEGMENTS).astype(jnp.int32),
        "seg_qkv": bell_draw(key_list[3], (D, 3, D), D ** -0.5, 0.21875, ((2, 4),)),
        "seg_qv_bias": bell_draw(key_list[4], (2, D), 0.3, 1.75, ((1, 4),), jnp.float32),
        "seg_out": bell_draw(key_list[5], (D, D), (D // 16) ** -0.5, 0.875, ((0, 4),)),
        "seg_up": bell_draw(key_list[6], (D, FF), D ** -0.5, 0.21875, ((1, 4),)),
        "seg_up_bias": bell_draw(key_list[7], (FF,), 0.3, 1.75, ((0, 4),), jnp.float32),
        "seg_down": bell_draw(key_list[8], (FF, D), FF ** -0.5, 0.109375, ((0, 4),)),
        "seg_gains": jnp.clip(1.0 + 0.1 * jax.random.normal(key_list[9], (2, D), jnp.float32), 0.5, 1.5),
        "seg_shifts": bell_draw(key_list[10], (4, D), 0.3, 1.75, (), jnp.float32),
        "cls_qkv": bell_draw(key_list[11], (D, 3, D), D ** -0.5, 0.21875, ((2, 4),)),
        "cls_qv_bias": bell_draw(key_list[12], (2, D), 0.3, 1.75, ((1, 4),), jnp.float32),
        "cls_out": bell_draw(key_list[13], (D, D), (D // 16) ** -0.5, 0.875, ((0, 4),)),
        "cls_up": bell_draw(key_list[14], (D, FF), D ** -0.5, 0.21875, ((1, 4),)),
        "cls_up_bias": bell_draw(key_list[15], (FF,), 0.3, 1.75, ((0, 4),), jnp.float32),
        "cls_down": bell_draw(key_list[16], (FF, D), FF ** -0.5, 0.109375, ((0, 4),)),
        "cls_gains": jnp.clip(1.0 + 0.1 * jax.random.normal(key_list[17], (2, D), jnp.float32), 0.5, 1.5),
        "cls_shifts": bell_draw(key_list[18], (4, D), 0.3, 1.75, (), jnp.float32),
        "pos_table": bell_draw(key_list[19], (MAX_SEGS, D), 0.5, 3.0),
        "cotangent": bell_draw(key_list[20], (TOKENS, D), 1.0, 6.0, ((0, 8),)),
    }


EPSILON = 1e-05

@jax.custom_vjp
def low(v):
    return lax.optimization_barrier(v.astype(jnp.bfloat16)).astype(jnp.float32)

@jax.custom_vjp
def low_back(v):
    return v

def low_keep(v):
    return (low(v), None)

def low_pass(kept, grad):
    return (grad,)

def back_keep(v):
    return (v, None)

def back_low(kept, grad):
    return (low(grad),)
low.defvjp(low_keep, low_pass)
low_back.defvjp(back_keep, back_low)

def layout(seg_counts, seg_order):
    slot_total = seg_order.shape[0]
    doc_ends = jnp.cumsum(seg_counts).astype(jnp.int32)
    doc_starts = (doc_ends - seg_counts).astype(jnp.int32)
    longest = jnp.argmax(seg_counts).astype(jnp.int32)
    doc_index = jnp.arange(seg_counts.shape[0], dtype=jnp.int32)
    chosen = doc_index == longest
    lead_seg = jnp.sum(jnp.where(chosen, doc_starts, 0)).astype(jnp.int32)
    trail_seg = (jnp.sum(jnp.where(chosen, doc_ends, 0)) - 1).astype(jnp.int32)
    slot_index = jnp.arange(slot_total, dtype=jnp.int32)
    lead_slot = jnp.argmax(seg_order == lead_seg).astype(jnp.int32)
    slot_seg = jnp.where(slot_index == 0, lead_seg, jnp.where(slot_index == lead_slot, seg_order[0], seg_order))
    trail_slot = jnp.argmax(slot_seg == trail_seg).astype(jnp.int32)
    slot_seg = jnp.where(slot_index == slot_total - 1, trail_seg, jnp.where(slot_index == trail_slot, slot_seg[slot_total - 1], slot_seg))
    seg_owner = lax.optimization_barrier(jnp.sum((slot_seg[:, None] >= doc_ends[None, :]).astype(jnp.int32), axis=1)).astype(jnp.int32)
    seg_start = lax.optimization_barrier(jnp.sum(jnp.where(seg_owner[:, None] == doc_index[None, :], doc_starts[None, :], 0), axis=1))
    seg_place = (slot_seg - seg_start).astype(jnp.int32)
    return (seg_owner, seg_place)

def layer_norm(value, gain_row, shift_row):
    center = value - lax.optimization_barrier(jnp.mean(value, axis=-1, keepdims=True))
    spread = lax.optimization_barrier(jnp.mean(center * center, axis=-1, keepdims=True))
    return center * lax.rsqrt(spread + EPSILON) * gain_row + shift_row

def softmax_rows(scores):
    shifted = jnp.exp(scores - lax.optimization_barrier(jnp.max(scores, axis=-1, keepdims=True)))
    return shifted / lax.optimization_barrier(jnp.sum(shifted, axis=-1, keepdims=True))

def attend(query_blocks, key_blocks, value_blocks, allowed):
    scores = low_back(jnp.einsum('gqhe,gkhe->ghqk', query_blocks, key_blocks, precision=lax.Precision.HIGHEST) * 0.125)
    if allowed is not None:
        scores = jnp.where(allowed[None, None], scores, -1000000000.0)
    probs = low(softmax_rows(scores))
    return jnp.einsum('ghqk,gkhe->gqhe', probs, value_blocks, precision=lax.Precision.HIGHEST)

def block(value, params, groups, allowed):
    w_qkv, qv_bias, w_out, w_up, up_bias, w_down, gains, shifts = params
    row_count = value.shape[0]
    value_low = low(value)
    mixed_qkv = jnp.dot(value_low, w_qkv.reshape(D, 3 * D), precision=lax.Precision.HIGHEST).reshape(row_count, 3, D)
    query_rows = low(low_back(mixed_qkv[:, 0] + qv_bias[0]))
    key_rows = low(low_back(mixed_qkv[:, 1]))
    value_rows = low(low_back(mixed_qkv[:, 2] + qv_bias[1]))
    block_shape = (groups, row_count // groups, HEADS, HEAD)
    attended = attend(query_rows.reshape(block_shape), key_rows.reshape(block_shape), value_rows.reshape(block_shape), allowed)
    attended = low(low_back(attended.reshape(row_count, D)))
    branch = low_back(jnp.dot(attended, w_out, precision=lax.Precision.HIGHEST))
    hidden = layer_norm(value + branch + shifts[0], gains[0], shifts[1])
    pre_act = low_back(jnp.dot(low(hidden), w_up, precision=lax.Precision.HIGHEST) + up_bias)
    act_low = low(jax.nn.gelu(pre_act, approximate=False))
    mlp_out = low_back(jnp.dot(act_low, w_down, precision=lax.Precision.HIGHEST))
    return layer_norm(hidden + mlp_out + shifts[2], gains[1], shifts[3])

def forward(tokens, seg_params, cls_params, pos_table, seg_owner, seg_place):

    def segment_block(rows_block):
        return block(rows_block, seg_params, TOK_DEV // SEG, None)
    first_out = lax.map(jax.checkpoint(segment_block), tokens.reshape(N_DP, TOK_DEV, D)).reshape(TOKENS, D)
    cls_input = first_out[::SEG] + pos_table[seg_place]
    allowed = seg_owner[:, None] == seg_owner[None, :]
    cls_output = block(cls_input, cls_params, 1, allowed)
    return first_out.at[::SEG].set(cls_output)

def reference(tokens, seg_counts, seg_order, seg_qkv, seg_qv_bias, seg_out, seg_up, seg_up_bias, seg_down, seg_gains, seg_shifts, cls_qkv, cls_qv_bias, cls_out, cls_up, cls_up_bias, cls_down, cls_gains, cls_shifts, pos_table, cotangent):
    seg_owner, seg_place = layout(seg_counts, seg_order)
    seg_params = tuple((item.astype(jnp.float32) for item in (seg_qkv, seg_qv_bias, seg_out, seg_up, seg_up_bias, seg_down, seg_gains, seg_shifts)))
    cls_params = tuple((item.astype(jnp.float32) for item in (cls_qkv, cls_qv_bias, cls_out, cls_up, cls_up_bias, cls_down, cls_gains, cls_shifts)))

    def whole(token_rows, seg_weights, cls_weights, table_rows):
        return forward(token_rows, seg_weights, cls_weights, table_rows, seg_owner, seg_place)
    result, pullback = jax.vjp(whole, tokens.astype(jnp.float32), seg_params, cls_params, pos_table.astype(jnp.float32))
    tokens_grad, seg_grads, cls_grads, pos_grad = pullback(cotangent.astype(jnp.float32))
    return (result.astype(jnp.bfloat16), tokens_grad, seg_grads[0], seg_grads[1], seg_grads[2], seg_grads[3], seg_grads[4], seg_grads[5], seg_grads[6], seg_grads[7], cls_grads[0], cls_grads[1], cls_grads[2], cls_grads[3], cls_grads[4], cls_grads[5], cls_grads[6], cls_grads[7], pos_grad)
```

```python
import jax
import jax.numpy as jnp
from jax import lax
from jax.sharding import PartitionSpec as P

HEAD = 64
SEG = 128
EPSILON = 1e-05
BF = jnp.bfloat16
F32 = jnp.float32


def layout(seg_counts, seg_order):
    slot_total = seg_order.shape[0]
    doc_index = jnp.arange(seg_counts.shape[0], dtype=jnp.int32)
    upto = doc_index[:, None] >= doc_index[None, :]
    doc_ends = jnp.sum(jnp.where(upto, seg_counts[None, :], 0), axis=1)
    doc_starts = doc_ends - seg_counts
    longest = jnp.argmax(seg_counts)
    chosen = doc_index == longest
    lead_seg = jnp.sum(jnp.where(chosen, doc_starts, 0))
    trail_seg = jnp.sum(jnp.where(chosen, doc_ends, 0)) - 1
    slot_index = jnp.arange(slot_total, dtype=jnp.int32)
    slot_seg = jnp.where(
        slot_index == 0, lead_seg, jnp.where(seg_order == lead_seg, seg_order[0], seg_order)
    )
    slot_seg = jnp.where(
        slot_index == slot_total - 1,
        trail_seg,
        jnp.where(slot_seg == trail_seg, slot_seg[slot_total - 1], slot_seg),
    )
    seg_owner = jnp.sum((slot_seg[:, None] >= doc_ends[None, :]).astype(jnp.int32), axis=1)
    seg_start = jnp.sum(
        jnp.where(seg_owner[:, None] == doc_index[None, :], doc_starts[None, :], 0), axis=1
    )
    return (seg_owner, slot_seg - seg_start)


def dot(a, b):
    return jnp.dot(a, b, preferred_element_type=F32)


def dot_t(a, b):
    return lax.dot_general(a, b, (((1,), (1,)), ((), ())), preferred_element_type=F32)


def t_dot(a, b):
    return lax.dot_general(a, b, (((0,), (0,)), ((), ())), preferred_element_type=F32)


def norm_parts(value):
    center = value - jnp.mean(value, axis=-1, keepdims=True)
    rstd = lax.rsqrt(jnp.mean(center * center, axis=-1, keepdims=True) + EPSILON)
    return center * rstd, rstd


def norm_back(grad, normed, rstd, gain):
    gy = grad * gain
    return rstd * (
        gy - jnp.mean(gy, axis=-1, keepdims=True) - normed * jnp.mean(gy * normed, axis=-1, keepdims=True)
    )


def gelu_both(pre):
    phi_cdf = 0.5 * (1.0 + lax.erf(pre * 0.7071067811865476))
    phi_pdf = 0.3989422804014327 * jnp.exp(-0.5 * pre * pre)
    return pre * phi_cdf, phi_cdf + pre * phi_pdf


def heads_of(matrix, groups):
    return matrix.reshape(groups, matrix.shape[0] // groups, matrix.shape[1] // HEAD, HEAD)


def scores_of(query, keys, allowed):
    scores = jnp.einsum("gqhe,gkhe->ghqk", query, keys, preferred_element_type=F32) * 0.125
    if allowed is not None:
        scores = jnp.where(allowed[None, None], scores, -1000000000.0)
    return scores


def attend(query, keys, values, allowed):
    scores = scores_of(query, keys, allowed)
    top = jnp.max(scores, axis=-1, keepdims=True)
    powers = jnp.exp(scores - top)
    probs = powers / jnp.sum(powers, axis=-1, keepdims=True)
    attended = jnp.einsum("ghqk,gkhe->gqhe", probs.astype(BF), values, preferred_element_type=F32)
    return attended.astype(BF)


def attend_back(query, keys, values, grad, allowed):
    scores = scores_of(query, keys, allowed)
    top = jnp.max(scores, axis=-1, keepdims=True)
    powers = jnp.exp(scores - top)
    probs = powers / jnp.sum(powers, axis=-1, keepdims=True)
    d_prob = jnp.einsum("gqhe,gkhe->ghqk", grad, values, preferred_element_type=F32)
    d_scores = (probs * (d_prob - jnp.sum(probs * d_prob, axis=-1, keepdims=True))).astype(BF)
    d_query = jnp.einsum("ghqk,gkhe->gqhe", d_scores, keys, preferred_element_type=F32) * 0.125
    d_keys = jnp.einsum("ghqk,gqhe->gkhe", d_scores, query, preferred_element_type=F32) * 0.125
    d_values = jnp.einsum("ghqk,gqhe->gkhe", probs.astype(BF), grad, preferred_element_type=F32)
    return d_query, d_keys, d_values


def make_shards(n_dp):
    core_pairs = [(i, i ^ 1) for i in range(4)]
    x_pairs = [(i, i ^ 2) for i in range(4)]

    def core_swap(value):
        return lax.ppermute(value, "mp", core_pairs)

    def x_swap(value):
        return lax.ppermute(value, "mp", x_pairs)

    def x_sum_low(partial):
        mine = partial.astype(BF)
        return mine.astype(F32) + x_swap(mine).astype(F32)

    def x_sum(partial):
        return partial + x_swap(partial)

    def shards(
        tokens,
        seg_counts,
        seg_order,
        seg_qkv,
        seg_qv_bias,
        seg_out,
        seg_up,
        seg_up_bias,
        seg_down,
        seg_gains,
        seg_shifts,
        cls_qkv,
        cls_qv_bias,
        cls_out,
        cls_up,
        cls_up_bias,
        cls_down,
        cls_gains,
        cls_shifts,
        pos_table,
        cotangent,
    ):
        core = lax.axis_index("mp") % 2
        dp_index = lax.axis_index("dp")
        first_core = core == 0
        row_count = tokens.shape[0] // 2
        own_segs = row_count // SEG
        slots = seg_order.shape[0]
        width = seg_qkv.shape[2]
        model = tokens.shape[1]

        def paired(value, axis):
            other = core_swap(value)
            return jnp.where(
                first_core,
                jnp.concatenate([value, other], axis=axis),
                jnp.concatenate([other, value], axis=axis),
            )

        def gather_slots(value):
            value = paired(value, 0)
            bit = 1
            while bit < n_dp:
                other = lax.ppermute(value, "dp", [(i, i ^ bit) for i in range(n_dp)])
                value = jnp.where(
                    (dp_index & bit) == 0,
                    jnp.concatenate([value, other], axis=0),
                    jnp.concatenate([other, value], axis=0),
                )
                bit *= 2
            return value

        def own_half(value, axis):
            size = value.shape[axis] // 2
            return lax.dynamic_slice_in_dim(value, core * size, size, axis)

        def other_half(value, axis):
            size = value.shape[axis] // 2
            return lax.dynamic_slice_in_dim(value, (1 - core) * size, size, axis)

        def dp_sum(value, bits):
            for bit in bits:
                rows = value.shape[0] // 2
                side = jnp.where((dp_index & bit) == 0, 0, 1)
                keep = lax.dynamic_slice_in_dim(value, side * rows, rows, 0)
                send = lax.dynamic_slice_in_dim(value, (1 - side) * rows, rows, 0)
                got = lax.ppermute(send, "dp", [(i, i ^ bit) for i in range(n_dp)])
                value = (keep.astype(F32) + got.astype(F32)).astype(BF)
            for bit in reversed(bits):
                got = lax.ppermute(value, "dp", [(i, i ^ bit) for i in range(n_dp)])
                value = jnp.where(
                    (dp_index & bit) == 0,
                    jnp.concatenate([value, got], axis=0),
                    jnp.concatenate([got, value], axis=0),
                )
            return value.astype(F32)

        def core_scatter(value, axis):
            return own_half(value, axis) + core_swap(other_half(value, axis).astype(BF)).astype(F32)

        seg_owner, seg_place = layout(seg_counts, seg_order)
        allowed = seg_owner[:, None] == seg_owner[None, :]
        place_hot = (
            seg_place[:, None] == jnp.arange(pos_table.shape[0], dtype=jnp.int32)[None, :]
        ).astype(BF)

        s_qkv = paired(seg_qkv, 2)
        s_out = paired(seg_out, 0)
        s_up = paired(seg_up, 1)
        s_down = paired(seg_down, 0)
        s_qv_bias = paired(seg_qv_bias, 1)
        s_up_bias = paired(seg_up_bias, 0)
        c_qkv = paired(cls_qkv, 2)
        c_out = paired(cls_out, 0)
        c_up = paired(cls_up, 1)
        c_down = paired(cls_down, 0)
        c_qv_bias = paired(cls_qv_bias, 1)
        c_up_bias = paired(cls_up_bias, 0)
        pair = 2 * width
        s_qkv_flat = s_qkv.reshape(model, 3 * pair)
        c_qkv_flat = c_qkv.reshape(model, 3 * pair)

        rows_low = own_half(tokens, 0)
        mixed = dot(rows_low, s_qkv_flat)
        query = heads_of((mixed[:, :pair] + s_qv_bias[0]).astype(BF), own_segs)
        keys = heads_of(mixed[:, pair : 2 * pair].astype(BF), own_segs)
        values = heads_of((mixed[:, 2 * pair :] + s_qv_bias[1]).astype(BF), own_segs)
        attended = attend(query, keys, values, None).reshape(row_count, pair)
        branch = x_sum_low(dot(attended, s_out))
        resid = rows_low.astype(F32) + branch + seg_shifts[0]

        lead_resid = gather_slots(resid[::SEG])
        lead_attended = gather_slots(attended[::SEG])
        lead_n1, lead_rstd1 = norm_parts(lead_resid)
        lead_hidden = lead_n1 * seg_gains[0] + seg_shifts[1]
        lead_hidden_low = lead_hidden.astype(BF)
        lead_act, lead_slope = gelu_both(dot(lead_hidden_low, s_up) + s_up_bias)
        lead_act_low = lead_act.astype(BF)
        lead_second = lead_hidden + x_sum(dot(lead_act_low, s_down)) + seg_shifts[2]
        lead_n2, lead_rstd2 = norm_parts(lead_second)
        lead_first = lead_n2 * seg_gains[1] + seg_shifts[3]

        n1, rstd1 = norm_parts(resid)
        hidden = n1 * seg_gains[0] + seg_shifts[1]
        hidden_low = hidden.astype(BF)
        act, slope = gelu_both(dot(hidden_low, s_up) + s_up_bias)
        act_low = act.astype(BF)
        second = hidden + x_sum_low(dot(act_low, s_down)) + seg_shifts[2]
        n2, rstd2 = norm_parts(second)
        first = n2 * seg_gains[1] + seg_shifts[3]

        c_value = lead_first + dot(place_hot, pos_table)
        c_low = c_value.astype(BF)
        c_mixed = dot(c_low, c_qkv_flat)
        c_query = heads_of((c_mixed[:, :pair] + c_qv_bias[0]).astype(BF), 1)
        c_keys = heads_of(c_mixed[:, pair : 2 * pair].astype(BF), 1)
        c_values = heads_of((c_mixed[:, 2 * pair :] + c_qv_bias[1]).astype(BF), 1)
        c_attended = attend(c_query, c_keys, c_values, allowed).reshape(slots, pair)
        c_resid = c_value + x_sum(dot(c_attended, c_out)) + cls_shifts[0]
        c_n1, c_rstd1 = norm_parts(c_resid)
        c_hidden = c_n1 * cls_gains[0] + cls_shifts[1]
        c_hidden_low = c_hidden.astype(BF)
        c_act, c_slope = gelu_both(dot(c_hidden_low, c_up) + c_up_bias)
        c_act_low = c_act.astype(BF)
        c_second = c_hidden + x_sum(dot(c_act_low, c_down)) + cls_shifts[2]
        c_n2, c_rstd2 = norm_parts(c_second)
        c_result = c_n2 * cls_gains[1] + cls_shifts[3]

        own_cot = own_half(cotangent, 0).astype(F32)
        c_gy = gather_slots(own_cot[::SEG])
        c_d_second = norm_back(c_gy, c_n2, c_rstd2, cls_gains[1])
        c_d_second_low = c_d_second.astype(BF)
        c_d_pre = (dot_t(c_d_second_low, c_down) * c_slope).astype(BF)
        c_d_hidden = x_sum(dot_t(c_d_pre, c_up)) + c_d_second
        c_d_resid = norm_back(c_d_hidden, c_n1, c_rstd1, cls_gains[0])
        c_d_resid_low = c_d_resid.astype(BF)
        c_d_attended = dot_t(c_d_resid_low, c_out).astype(BF)
        c_dq, c_dk, c_dv = attend_back(c_query, c_keys, c_values, heads_of(c_d_attended, 1), allowed)
        c_d_mixed = jnp.concatenate(
            [part.reshape(slots, pair) for part in (c_dq, c_dk, c_dv)], axis=1
        ).astype(BF)
        c_grad = x_sum(dot_t(c_d_mixed, c_qkv_flat)) + c_d_resid
        own_c_mixed = own_half(c_d_mixed.reshape(slots, 3, pair), 2)
        cls_grads = (
            t_dot(c_low, own_c_mixed.reshape(slots, 3 * width)).reshape(model, 3, width),
            jnp.sum(own_c_mixed.astype(F32), axis=0)[::2],
            t_dot(own_half(c_attended, 1), c_d_resid_low),
            t_dot(c_hidden_low, own_half(c_d_pre, 1)),
            jnp.sum(own_half(c_d_pre, 1).astype(F32), axis=0),
            t_dot(own_half(c_act_low, 1), c_d_second_low),
            jnp.stack([jnp.sum(c_d_hidden * c_n1, axis=0), jnp.sum(c_gy * c_n2, axis=0)]),
            jnp.stack(
                [
                    jnp.sum(c_d_resid, axis=0),
                    jnp.sum(c_d_hidden, axis=0),
                    jnp.sum(c_d_second, axis=0),
                    jnp.sum(c_gy, axis=0),
                ]
            ),
        )
        pos_grad = jnp.dot(place_hot.astype(F32).T, c_grad, precision=lax.Precision.HIGHEST)

        row_index = lax.broadcasted_iota(jnp.int32, (row_count, 1), 0)
        is_lead = (row_index % SEG) == 0
        gy = jnp.where(is_lead, 0.0, own_cot)
        d_second = norm_back(gy, n2, rstd2, seg_gains[1])
        d_second_low = d_second.astype(BF)
        grad_down = t_dot(act_low, d_second_low)
        d_pre = (dot_t(d_second_low, s_down) * slope).astype(BF)
        grad_up = t_dot(hidden_low, d_pre)
        d_hidden = x_sum_low(dot_t(d_pre, s_up)) + d_second
        d_resid = norm_back(d_hidden, n1, rstd1, seg_gains[0])
        d_resid_low = d_resid.astype(BF)
        grad_out = t_dot(attended, d_resid_low)
        d_attended = dot_t(d_resid_low, s_out).astype(BF)
        orders = [1 << k for k in range(n_dp.bit_length() - 1)]
        swapped = [orders[1], orders[0], *orders[2:]]
        grad_down = dp_sum(core_scatter(grad_down, 0).astype(BF), orders)
        grad_up = dp_sum(core_scatter(grad_up, 1).astype(BF), swapped)
        grad_out = dp_sum(core_scatter(grad_out, 0).astype(BF), orders)
        small = jnp.stack(
            [
                jnp.sum(d_hidden * n1, axis=0),
                jnp.sum(gy * n2, axis=0),
                jnp.sum(d_resid, axis=0),
                jnp.sum(d_hidden, axis=0),
                jnp.sum(d_second, axis=0),
                jnp.sum(gy, axis=0),
            ]
        )
        d_pre_sum = jnp.sum(d_pre.astype(F32), axis=0).reshape(-1, model)

        l_gy = c_grad
        l_d_second = norm_back(l_gy, lead_n2, lead_rstd2, seg_gains[1])
        l_d_second_low = l_d_second.astype(BF)
        l_d_pre = (dot_t(l_d_second_low, s_down) * lead_slope).astype(BF)
        l_d_hidden = x_sum(dot_t(l_d_pre, s_up)) + l_d_second
        l_d_resid = norm_back(l_d_hidden, lead_n1, lead_rstd1, seg_gains[0])
        l_d_resid_low = l_d_resid.astype(BF)
        l_d_attended = dot_t(l_d_resid_low, s_out).astype(BF)
        l_small = jnp.stack(
            [
                jnp.sum(l_d_hidden * lead_n1, axis=0),
                jnp.sum(l_gy * lead_n2, axis=0),
                jnp.sum(l_d_resid, axis=0),
                jnp.sum(l_d_hidden, axis=0),
                jnp.sum(l_d_second, axis=0),
                jnp.sum(l_gy, axis=0),
            ]
        )

        own_start = (dp_index * 2 + core) * own_segs

        def with_leads(value, leads):
            mine = lax.dynamic_slice_in_dim(leads, own_start, own_segs, 0)
            spread = jnp.broadcast_to(mine[:, None, :], (own_segs, SEG, mine.shape[1]))
            return jnp.where(is_lead, spread.reshape(row_count, mine.shape[1]), value)

        d_attended = with_leads(d_attended, l_d_attended)
        d_resid = with_leads(d_resid, l_d_resid)
        dq, dk, dv = attend_back(query, keys, values, heads_of(d_attended, own_segs), None)
        d_mixed = jnp.concatenate(
            [part.reshape(row_count, pair) for part in (dq, dk, dv)], axis=1
        ).astype(BF)
        d_rows = x_sum_low(dot_t(d_mixed, s_qkv_flat)) + d_resid
        tokens_grad = paired(d_rows, 0)
        grad_qkv = core_scatter(t_dot(rows_low, d_mixed).reshape(model, 3, pair), 2)
        grad_qkv = dp_sum(grad_qkv.reshape(model, 3 * width).astype(BF), swapped)
        mixed_sum = jnp.sum(d_mixed.astype(F32), axis=0).reshape(3, pair)[::2]
        tail = jnp.concatenate([small, d_pre_sum, mixed_sum.reshape(-1, model)], axis=0)
        tail = tail + core_swap(tail)
        tail = lax.psum(tail, "dp")
        d_pre_total = tail[6 : 6 + d_pre_sum.shape[0]].reshape(-1)
        mixed_total = tail[6 + d_pre_sum.shape[0] :].reshape(2, pair)
        seg_small = tail[:6] + l_small

        seg_grads = (
            grad_qkv.reshape(model, 3, width),
            own_half(mixed_total, 1),
            grad_out + t_dot(own_half(lead_attended, 1), l_d_resid_low),
            grad_up + t_dot(lead_hidden_low, own_half(l_d_pre, 1)),
            own_half(d_pre_total, 0) + jnp.sum(own_half(l_d_pre, 1).astype(F32), axis=0),
            grad_down + t_dot(own_half(lead_act_low, 1), l_d_second_low),
            seg_small[:2],
            seg_small[2:],
        )

        own_result = lax.dynamic_slice_in_dim(c_result, own_start, own_segs, 0)
        spread = jnp.broadcast_to(own_result[:, None, :], (own_segs, SEG, model))
        own_out = jnp.where(is_lead, spread.reshape(row_count, model), first).astype(BF)
        layer_out = paired(own_out, 0)
        return (layer_out, tokens_grad, *seg_grads, *cls_grads, pos_grad)

    return shards


def solution(mesh):
    in_specs = (
        P("dp", None),
        P(),
        P(),
        P(None, None, "mp"),
        P(None, "mp"),
        P("mp", None),
        P(None, "mp"),
        P("mp"),
        P("mp", None),
        P(),
        P(),
        P(None, None, "mp"),
        P(None, "mp"),
        P("mp", None),
        P(None, "mp"),
        P("mp"),
        P("mp", None),
        P(),
        P(),
        P(),
        P("dp", None),
    )
    out_specs = (
        P("dp", None),
        P("dp", None),
        P(None, None, "mp"),
        P(None, "mp"),
        P("mp", None),
        P(None, "mp"),
        P("mp"),
        P("mp", None),
        P(),
        P(),
        P(None, None, "mp"),
        P(None, "mp"),
        P("mp", None),
        P(None, "mp"),
        P("mp"),
        P("mp", None),
        P(),
        P(),
        P(),
    )
    return jax.shard_map(
        make_shards(mesh.shape["dp"]), mesh=mesh, in_specs=in_specs, out_specs=out_specs, check_vma=False
    )
```

```python
import jax
import jax.numpy as jnp
from jax import lax
from jax.experimental import pallas as pl
from jax.experimental.pallas import tpu as pltpu
from jax.sharding import PartitionSpec as P

HEAD = 64
SEG = 128
LANES = 128
EPSILON = 1e-05
BF = jnp.bfloat16
F32 = jnp.float32


def dot(a, b):
    return lax.dot_general(a, b, (((1,), (0,)), ((), ())), preferred_element_type=F32)


def dot_t(a, b):
    return lax.dot_general(a, b, (((1,), (1,)), ((), ())), preferred_element_type=F32)


def t_dot(a, b):
    return lax.dot_general(a, b, (((0,), (0,)), ((), ())), preferred_element_type=F32)


def norm_parts(value):
    center = value - jnp.mean(value, axis=-1, keepdims=True)
    rstd = lax.rsqrt(jnp.mean(center * center, axis=-1, keepdims=True) + EPSILON)
    return center * rstd, rstd


def norm_back(grad, normed, rstd, gain):
    gy = grad * gain
    return rstd * (
        gy
        - jnp.mean(gy, axis=-1, keepdims=True)
        - normed * jnp.mean(gy * normed, axis=-1, keepdims=True)
    )


def gelu_both(pre):
    cdf = 0.5 * (1.0 + lax.erf(pre * 0.7071067811865476))
    pdf = 0.3989422804014327 * jnp.exp(-0.5 * pre * pre)
    return pre * cdf, cdf + pre * pdf


def column_sum(value):
    return jnp.sum(value, axis=0, keepdims=True)


def softmax(scores):
    powers = jnp.exp(scores - jnp.max(scores, axis=-1, keepdims=True))
    return powers * (1.0 / jnp.sum(powers, axis=-1, keepdims=True))


def head_masks(dtype):
    lane = lax.broadcasted_iota(jnp.int32, (1, LANES), 1)
    return [(lane < HEAD).astype(F32).astype(dtype), (lane >= HEAD).astype(F32).astype(dtype)]


def stacked(tile, masks):
    return jnp.concatenate([tile * masks[0], tile * masks[1]], axis=0)


class Outer:
    def __init__(self):
        self.held = {}

    def add(self, *values):
        for value in values:
            self.held[id(value)] = value
        return values

    def __contains__(self, value):
        return self.held.get(id(value)) is value


def call(outer, body, outs, args, name, far=(), scratch=(), vmem=16, stay=()):
    def spec(i, a):
        if i in stay:
            return pl.BlockSpec(memory_space=pltpu.HBM)
        return pl.BlockSpec(memory_space=pltpu.SMEM if a.dtype == jnp.int32 and a.ndim == 1 else pltpu.VMEM)

    results = pl.pallas_call(
        body,
        out_shape=tuple(
            pltpu.HBM(s, d) if i in far else jax.ShapeDtypeStruct(s, d) for i, (s, d) in enumerate(outs)
        ),
        in_specs=[spec(i, a) for i, a in enumerate(args)],
        out_specs=tuple(pl.BlockSpec(memory_space=pltpu.VMEM) for _ in outs),
        scratch_shapes=list(scratch),
        compiler_params=pltpu.CompilerParams(vmem_limit_bytes=vmem * 1024 * 1024),
        name=name,
    )(*[pltpu.with_memory_space_constraint(a, pltpu.HBM) if i in stay or a in outer else a for i, a in enumerate(args)])
    outer.add(*[result for i, result in enumerate(results) if i in far])
    return results


def call_blocks(body, outs, scalars, args, name, grid, rows, kinds, vmem=14):
    def spec(shape, kind):
        if kind == "w":
            return pl.BlockSpec(shape, lambda i, scalars: (0,) * len(shape))
        steps = shape[0] // rows
        return pl.BlockSpec((rows, *shape[1:]), lambda i, scalars: (i % steps, 0))

    return pl.pallas_call(
        body,
        out_shape=tuple(jax.ShapeDtypeStruct(s, d) for s, d in outs),
        grid_spec=pltpu.PrefetchScalarGridSpec(
            num_scalar_prefetch=1,
            grid=(grid,),
            in_specs=[spec(a.shape, k) for k, a in zip(kinds, args, strict=True)],
            out_specs=tuple(spec(s, "m") for s, _ in outs),
        ),
        compiler_params=pltpu.CompilerParams(vmem_limit_bytes=vmem * 1024 * 1024),
        name=name,
    )(scalars, *args)


def tie(value, *others):
    return lax.optimization_barrier((value, *others))[0]


BLOCK = 256


def blocks_of(rows):
    return [slice(at, at + BLOCK) for at in range(0, rows, BLOCK)]


def layout_body(counts_ref, order_ref, owner_row, owner_col, place_row, place_col):
    docs, slots = counts_ref.shape[1], order_ref.shape[1]
    counts = counts_ref[...].astype(F32)
    order = order_ref[...].astype(F32)

    def iotas(a, b):
        return [lax.broadcasted_iota(jnp.int32, (a, b), d).astype(F32) for d in (0, 1)]

    def to_column(row):
        size = row.shape[1]
        r, c = iotas(size, size)
        return jnp.sum(jnp.where(r == c, row, 0.0), axis=1, keepdims=True)

    def to_row(col):
        size = col.shape[0]
        r, c = iotas(size, size)
        return column_sum(jnp.where(r == c, col, 0.0))

    def total(row):
        return jnp.sum(row, axis=1, keepdims=True)

    r, c = iotas(docs, docs)
    ends_col = jnp.sum(jnp.where(c <= r, counts, 0.0), axis=1, keepdims=True)
    ends_row = to_row(ends_col)
    starts_col = ends_col - to_column(counts)
    starts_row = ends_row - counts
    index = lax.broadcasted_iota(jnp.int32, (1, docs), 1).astype(F32)
    top = jnp.max(counts, axis=1, keepdims=True)
    longest = jnp.min(jnp.where(counts == top, index, float(docs)), axis=1, keepdims=True)
    lead = total(jnp.where(index == longest, starts_row, 0.0))
    trail = total(jnp.where(index == longest, ends_row, 0.0)) - 1.0
    slot = lax.broadcasted_iota(jnp.int32, (1, slots), 1).astype(F32)
    head = total(jnp.where(slot == 0.0, order, 0.0))
    held = jnp.where(slot == 0.0, lead, jnp.where(order == lead, head, order))
    last = total(jnp.where(slot == slots - 1.0, held, 0.0))
    held = jnp.where(slot == slots - 1.0, trail, jnp.where(held == trail, last, held))
    owner = column_sum((held >= ends_col).astype(F32))
    r, _ = iotas(docs, slots)
    start = column_sum(jnp.where(r == owner, starts_col, 0.0))
    place = held - start
    owner_row[...] = owner
    owner_col[...] = to_column(owner)
    place_row[...] = place
    place_col[...] = to_column(place)


def pair_weights(core, own_ref, oth_ref, w_ref):
    parts, width = own_ref.shape[0], own_ref.shape[1]
    for part in range(parts):
        base = part * 2 * width
        w_ref[pl.ds(pl.multiple_of(base + core * width, width), width)] = own_ref[part]
        w_ref[pl.ds(pl.multiple_of(base + (1 - core) * width, width), width)] = oth_ref[part]


def pair_bias(core, own_ref, oth_ref):
    own, oth = own_ref[...], oth_ref[...]
    low = jnp.where(core == 0, own, oth)
    return jnp.concatenate([low, jnp.where(core == 0, oth, own)], axis=1)


def seg_attention_body(
    scalars, x_any, cot_any, own_ref, oth_ref, b_own, b_oth, wo_own, wo_oth,
    part_ref, lead_ref, rest_ref, q_ref, k_ref, v_ref, att_ref, w_ref, wo_ref, x_ref,
    cot_ref, x_sem, cot_sem,
):
    rows, pair = q_ref.shape
    model = x_any.shape[1]
    segs, packed = cot_ref.shape[0], cot_ref.shape[1]
    base = pl.multiple_of(scalars[0] * rows, rows)
    x_copy = pltpu.make_async_copy(x_any.at[pl.ds(base, rows)], x_ref, x_sem)
    x_copy.start()
    cot_copies = [
        pltpu.make_async_copy(cot_any.at[pl.ds(base + j * SEG, packed)], cot_ref.at[j], cot_sem.at[j])
        for j in range(segs)
    ]
    for copy in cot_copies:
        copy.start()
    pair_weights(scalars[0], own_ref, oth_ref, w_ref)
    pair_weights(scalars[0], wo_own, wo_oth, wo_ref)
    bias = pair_bias(scalars[0], b_own, b_oth)
    masks = head_masks(BF)
    x_copy.wait()
    for rs in blocks_of(rows):
        x = x_ref[rs]
        q_ref[rs] = (dot_t(x, w_ref[:pair]) + bias[0:1]).astype(BF)
        k_ref[rs] = dot_t(x, w_ref[pair : 2 * pair]).astype(BF)
        v_ref[rs] = (dot_t(x, w_ref[2 * pair :]) + bias[1:2]).astype(BF)
        for row in range(rs.start, rs.stop, SEG):
            ats = [(slice(row, row + SEG), slice(col, col + LANES)) for col in range(0, pair, LANES)]
            scores = [dot_t(stacked(q_ref[at], masks), k_ref[at]) * 0.125 for at in ats]
            probs = [softmax(score).astype(BF) for score in scores]
            both = [jnp.concatenate([p[:SEG], p[SEG:]], axis=1) for p in probs]
            for at, weight in zip(ats, both):
                att_ref[at] = dot(weight, stacked(v_ref[at], masks)).astype(BF)
        part = dot(att_ref[rs], wo_ref[...])
        part_ref[rs] = part.astype(BF)
        for row in range(0, BLOCK, SEG):
            j = (rs.start + row) // SEG
            lead_ref[j : j + 1] = part[row : row + 1]
            rest_ref[j : j + 1, :model] = x[row : row + 1].astype(F32)
    for j, copy in enumerate(cot_copies):
        copy.wait()
        rest_ref[j : j + 1, model:] = cot_ref[j, 0:1].astype(F32)


def seg_mlp_body(
    x_ref, mine_ref, got_ref, gains_ref, shifts_ref, up0, up1, ub0, ub1, down0, down1,
    part_ref, resid_ref, act_ref, slope_ref,
):
    for rs in blocks_of(resid_ref.shape[0]):
        branch = mine_ref[rs].astype(F32) + got_ref[rs].astype(F32)
        resid = x_ref[rs].astype(F32) + branch + shifts_ref[0:1]
        resid_ref[rs] = resid
        normed, _ = norm_parts(resid)
        hidden_low = (normed * gains_ref[0:1] + shifts_ref[1:2]).astype(BF)
        parts = []
        for j, (up, ub, down) in enumerate(((up0, ub0, down0), (up1, ub1, down1))):
            at = (rs, slice(j * up.shape[1], (j + 1) * up.shape[1]))
            act, slope = gelu_both(dot(hidden_low, up[...]) + ub[...])
            low = act.astype(BF)
            act_ref[at] = low
            slope_ref[at] = slope
            parts.append(dot(low, down[...]))
        part_ref[rs] = (parts[0] + parts[1]).astype(BF)


def seg_mlp_back_body(
    scalars, resid_ref, mine_ref, got_ref, cot_any, slope_ref, gains_ref, shifts_ref, up0, up1, down0, down1,
    dsec_low_ref, hidden_ref, dpre_ref, out_ref, dsec_ref, part_ref, sums_ref, dpre_sum_ref,
    cot_ref, cot_sem,
):
    rows = resid_ref.shape[0]
    base = pl.multiple_of(scalars[0] * rows, rows)
    copy = pltpu.make_async_copy(cot_any.at[pl.ds(base, rows)], cot_ref, cot_sem)
    copy.start()
    blocks = blocks_of(resid_ref.shape[0])
    for rs in blocks:
        normed, _ = norm_parts(resid_ref[rs])
        hidden = normed * gains_ref[0:1] + shifts_ref[1:2]
        hidden_ref[rs] = hidden.astype(BF)
        second = hidden + (mine_ref[rs].astype(F32) + got_ref[rs].astype(F32)) + shifts_ref[2:3]
        n2, rstd2 = norm_parts(second)
        out_ref[rs] = (n2 * gains_ref[1:2] + shifts_ref[3:4]).astype(BF)
        lead = lax.broadcasted_iota(jnp.int32, (BLOCK, 1), 0) % SEG == 0
        if rs.start == 0:
            copy.wait()
        gy = jnp.where(lead, 0.0, cot_ref[rs].astype(F32))
        d_second = norm_back(gy, n2, rstd2, gains_ref[1:2])
        dsec_ref[rs] = d_second
        low = d_second.astype(BF)
        dsec_low_ref[rs] = low
        parts, pre_sums = [], []
        for j, (up, down) in enumerate(((up0, down0), (up1, down1))):
            at = (rs, slice(j * up.shape[1], (j + 1) * up.shape[1]))
            d_pre = (dot_t(low, down[...]) * slope_ref[at]).astype(BF)
            dpre_ref[at] = d_pre
            pre_sums.append(column_sum(d_pre.astype(F32)))
            parts.append(dot_t(d_pre, up[...]))
        part_ref[rs] = (parts[0] + parts[1]).astype(BF)
        sums = jnp.concatenate([column_sum(gy * n2), column_sum(d_second), column_sum(gy)], axis=0)
        pre_sums = jnp.concatenate(pre_sums, axis=0)
        if rs.start == 0:
            sums_ref[...] = sums
            dpre_sum_ref[...] = pre_sums
        else:
            sums_ref[...] += sums
            dpre_sum_ref[...] += pre_sums


def mlp_grads_body(act_ref, low_ref, hidden_ref, dpre_ref, down_own, down_oth, up_own, up_oth):
    size = down_own.shape[0]
    low, hidden = low_ref[...], hidden_ref[...]
    down_oth[...] = t_dot(act_ref[:, size:], low).astype(BF)
    up_oth[...] = t_dot(hidden, dpre_ref[:, size:]).astype(BF)
    down_own[...] = t_dot(act_ref[:, :size], low).astype(BF)
    up_own[...] = t_dot(hidden, dpre_ref[:, :size]).astype(BF)


def seg_out_back_body(
    resid_ref, mine_ref, got_ref, dsec_ref, gains_ref, wo_ref,
    dres_ref, datt_ref, sums_ref,
):
    for rs in blocks_of(resid_ref.shape[0]):
        n1, rstd1 = norm_parts(resid_ref[rs])
        d_hidden = (mine_ref[rs].astype(F32) + got_ref[rs].astype(F32)) + dsec_ref[rs]
        d_resid = norm_back(d_hidden, n1, rstd1, gains_ref[0:1])
        dres_ref[rs] = d_resid
        datt_ref[rs] = dot_t(d_resid.astype(BF), wo_ref[...]).astype(BF)
        sums = jnp.concatenate([column_sum(d_hidden * n1), column_sum(d_resid), column_sum(d_hidden)], axis=0)
        if rs.start == 0:
            sums_ref[...] = sums
        else:
            sums_ref[...] += sums


def mlp_rows(hidden_low, up0, up1, ub0, ub1, down0, down1, act_ref, slope_ref, part_ref, half_ref):
    for j, (up, ub, down) in enumerate(((up0, ub0, down0), (up1, ub1, down1))):
        act, slope = gelu_both(dot(hidden_low, up[...]) + ub[...])
        low = act.astype(BF)
        act_ref[j] = low
        slope_ref[j] = slope
        half_ref[j] = dot(low, down[...])
    part_ref[...] = (half_ref[0] + half_ref[1]).astype(BF)


def mlp_rows_back(low, slope_ref, up0, up1, down0, down1, dpre_ref, part_ref, half_ref):
    for j, (up, down) in enumerate(((up0, down0), (up1, down1))):
        d_pre = (dot_t(low, down[...]) * slope_ref[j]).astype(BF)
        dpre_ref[j] = d_pre
        half_ref[j] = dot_t(d_pre, up[...])
    part_ref[...] = (half_ref[0] + half_ref[1]).astype(BF)


def lead_mlp_body(
    message_ref, gains_ref, shifts_ref, up0, up1, ub0, ub1, down0, down1,
    resid_ref, hidden_ref, act_ref, slope_ref, part_ref, half_ref,
):
    model = resid_ref.shape[1]
    resid = message_ref[:, :model].astype(F32) + message_ref[:, model : 2 * model].astype(F32) + shifts_ref[0:1]
    resid_ref[...] = resid
    n1, _ = norm_parts(resid)
    hidden_low = (n1 * gains_ref[0:1] + shifts_ref[1:2]).astype(BF)
    hidden_ref[...] = hidden_low
    mlp_rows(hidden_low, up0, up1, ub0, ub1, down0, down1, act_ref, slope_ref, part_ref, half_ref)


def cls_attention_body(
    scalars, resid_ref, mine_ref, got_ref, sgains_ref, sshifts_ref, owner_row, owner_col, place_col, table_ref,
    own_ref, oth_ref, b_own, b_oth, wo_own, wo_oth,
    second_ref, value_ref, q_ref, k_ref, v_ref, att_ref, part_ref, w_ref, wo_ref,
):
    pair = q_ref.shape[1]
    pair_weights(scalars[0], own_ref, oth_ref, w_ref)
    pair_weights(scalars[0], wo_own, wo_oth, wo_ref)
    bias = pair_bias(scalars[0], b_own, b_oth)
    n1, _ = norm_parts(resid_ref[...])
    hidden = n1 * sgains_ref[0:1] + sshifts_ref[1:2]
    second = hidden + (mine_ref[...].astype(F32) + got_ref[...].astype(F32)) + sshifts_ref[2:3]
    second_ref[...] = second
    n2, _ = norm_parts(second)
    first = n2 * sgains_ref[1:2] + sshifts_ref[3:4]
    slots, places = resid_ref.shape[0], table_ref.shape[0]
    index = lax.broadcasted_iota(jnp.int32, (slots, places), 1).astype(F32)
    hot = (index == place_col[...]).astype(F32).astype(BF)
    value = first + dot(hot, table_ref[...])
    value_ref[...] = value
    low = value.astype(BF)
    q_ref[...] = (dot_t(low, w_ref[:pair]) + bias[0:1]).astype(BF)
    k_ref[...] = dot_t(low, w_ref[pair : 2 * pair]).astype(BF)
    v_ref[...] = (dot_t(low, w_ref[2 * pair :]) + bias[1:2]).astype(BF)
    allowed = owner_row[...] == owner_col[...]
    masks = head_masks(BF)
    for col in range(0, pair, LANES):
        at = slice(col, col + LANES)
        q, k, v = q_ref[:, at], k_ref[:, at], v_ref[:, at]
        tile = None
        for mask in masks:
            scores = jnp.where(allowed, dot_t(q * mask, k) * 0.125, -1000000000.0)
            one = dot(softmax(scores).astype(BF), v * mask)
            tile = one if tile is None else tile + one
        att_ref[:, at] = tile.astype(BF)
    part_ref[...] = dot(att_ref[...], wo_ref[...]).astype(BF)


def cls_mlp_body(
    value_ref, mine_ref, got_ref, gains_ref, shifts_ref, up0, up1, ub0, ub1, down0, down1,
    resid_ref, hidden_ref, act_ref, slope_ref, part_ref, half_ref,
):
    resid = value_ref[...] + (mine_ref[...].astype(F32) + got_ref[...].astype(F32)) + shifts_ref[0:1]
    resid_ref[...] = resid
    n1, _ = norm_parts(resid)
    hidden_low = (n1 * gains_ref[0:1] + shifts_ref[1:2]).astype(BF)
    hidden_ref[...] = hidden_low
    mlp_rows(hidden_low, up0, up1, ub0, ub1, down0, down1, act_ref, slope_ref, part_ref, half_ref)


def cls_mlp_back_body(
    resid_ref, mine_ref, got_ref, message_ref, slope_ref, gains_ref, shifts_ref, up0, up1, down0, down1,
    result_ref, dsec_ref, dpre_ref, part_ref, sums_ref, half_ref,
):
    n1, _ = norm_parts(resid_ref[...])
    hidden = n1 * gains_ref[0:1] + shifts_ref[1:2]
    second = hidden + (mine_ref[...].astype(F32) + got_ref[...].astype(F32)) + shifts_ref[2:3]
    n2, rstd2 = norm_parts(second)
    result_ref[...] = n2 * gains_ref[1:2] + shifts_ref[3:4]
    gy = message_ref[:, 2 * result_ref.shape[1] :].astype(F32)
    d_second = norm_back(gy, n2, rstd2, gains_ref[1:2])
    dsec_ref[...] = d_second
    mlp_rows_back(d_second.astype(BF), slope_ref, up0, up1, down0, down1, dpre_ref, part_ref, half_ref)
    sums_ref[...] = jnp.concatenate([column_sum(gy * n2), column_sum(d_second), column_sum(gy)], axis=0)


def cls_attention_back_body(
    resid_ref, mine_ref, got_ref, dsec_ref, gains_ref, q_ref, k_ref, v_ref, owner_row, owner_col,
    w_ref, wo_ref,
    dres_ref, dres_low_ref, dmix_ref, part_ref, sums_ref,
):
    pair = q_ref.shape[1]
    n1, rstd1 = norm_parts(resid_ref[...])
    d_hidden = (mine_ref[...].astype(F32) + got_ref[...].astype(F32)) + dsec_ref[...]
    d_resid = norm_back(d_hidden, n1, rstd1, gains_ref[0:1])
    dres_ref[...] = d_resid
    low = d_resid.astype(BF)
    dres_low_ref[...] = low
    sums_ref[...] = jnp.concatenate(
        [column_sum(d_hidden * n1), column_sum(d_resid), column_sum(d_hidden)], axis=0
    )
    d_att = dot_t(low, wo_ref[...]).astype(BF)
    allowed = owner_row[...] == owner_col[...]
    masks = head_masks(BF)
    for col in range(0, pair, LANES):
        at = slice(col, col + LANES)
        q, k, v, g = q_ref[:, at], k_ref[:, at], v_ref[:, at], d_att[:, at]
        total = [None] * 3
        for mask in masks:
            qm, gm = q * mask, g * mask
            probs = softmax(jnp.where(allowed, dot_t(qm, k) * 0.125, -1000000000.0))
            d_prob = dot_t(gm, v)
            ds = (probs * (d_prob - jnp.sum(probs * d_prob, axis=-1, keepdims=True))).astype(BF)
            one = [dot(ds, k * mask), t_dot(ds, qm), t_dot(probs.astype(BF), gm)]
            total = [a if b is None else a + b for a, b in zip(one, total)]
        for j, scale in enumerate((0.125, 0.125, 1.0)):
            dmix_ref[:, j * pair + col : j * pair + col + LANES] = (total[j] * scale).astype(BF)
    part_ref[...] = dot(dmix_ref[...], w_ref[...]).astype(BF)


def lead_mlp_back_body(
    mine_ref, got_ref, dres_ref, second_ref, slope_ref, sgains_ref, place_row, up0, up1, down0, down1,
    dsec_ref, dsec_low_ref, dpre_ref, part_ref, sums_ref, pos_ref, half_ref,
):
    gy = (mine_ref[...].astype(F32) + got_ref[...].astype(F32)) + dres_ref[...]
    n2, rstd2 = norm_parts(second_ref[...])
    d_second = norm_back(gy, n2, rstd2, sgains_ref[1:2])
    dsec_ref[...] = d_second
    low = d_second.astype(BF)
    dsec_low_ref[...] = low
    mlp_rows_back(low, slope_ref, up0, up1, down0, down1, dpre_ref, part_ref, half_ref)
    sums_ref[...] = jnp.concatenate([column_sum(gy * n2), column_sum(d_second), column_sum(gy)], axis=0)
    places, slots = pos_ref.shape[0], gy.shape[0]
    index = lax.broadcasted_iota(jnp.int32, (places, slots), 0).astype(F32)
    hot = (index == place_row[...]).astype(F32)
    pos_ref[...] = lax.dot_general(
        hot, gy, (((1,), (0,)), ((), ())), preferred_element_type=F32, precision=lax.Precision.HIGHEST
    )


def seg_attention_back_body(
    scalars, lresid_ref, lmine_ref, lgot_ref, ldsec_ref, gains_ref, wo_ref, w_ref,
    q_ref, k_ref, v_ref, datt_ref, dres_ref,
    part_ref, dres_out, dmix_ref, lsums_ref,
    lead_dres, lead_datt, datt_all,
):
    rows, pair = q_ref.shape
    n1, rstd1 = norm_parts(lresid_ref[...])
    d_hidden = (lmine_ref[...].astype(F32) + lgot_ref[...].astype(F32)) + ldsec_ref[...]
    d_resid = norm_back(d_hidden, n1, rstd1, gains_ref[0:1])
    lead_dres[...] = d_resid
    lead_datt[...] = dot_t(d_resid.astype(BF), wo_ref[...]).astype(BF).astype(F32)
    lsums_ref[...] = jnp.concatenate(
        [column_sum(d_hidden * n1), column_sum(d_resid), column_sum(d_hidden)], axis=0
    )
    masks = head_masks(BF)
    for row in range(0, rows, SEG):
        rs = slice(row, row + SEG)
        slot = scalars[1] + row // SEG
        dres_out[rs] = dres_ref[rs]
        dres_out[row : row + 1] = lead_dres[pl.ds(slot, 1)]
        datt_all[rs] = datt_ref[rs].astype(F32)
        datt_all[row : row + 1] = lead_datt[pl.ds(slot, 1)]
        ats = [(rs, slice(col, col + LANES)) for col in range(0, pair, LANES)]
        qs = [stacked(q_ref[at], masks) for at in ats]
        gs = [stacked(datt_all[at].astype(BF), masks) for at in ats]
        scores = [dot_t(q, k_ref[at]) * 0.125 for q, at in zip(qs, ats)]
        d_probs = [dot_t(g, v_ref[at]) for g, at in zip(gs, ats)]
        probs = [softmax(score) for score in scores]
        d_scores = [
            (p * (d - jnp.sum(p * d, axis=-1, keepdims=True))).astype(BF) for p, d in zip(probs, d_probs)
        ]
        for j, at in enumerate(ats):
            col = j * LANES
            both = jnp.concatenate([d_scores[j][:SEG], d_scores[j][SEG:]], axis=1)
            dmix_ref[rs, col : col + LANES] = (dot(both, stacked(k_ref[at], masks)) * 0.125).astype(BF)
            col += pair
            dmix_ref[rs, col : col + LANES] = (t_dot(d_scores[j], qs[j]) * 0.125).astype(BF)
            col += pair
            dmix_ref[rs, col : col + LANES] = t_dot(probs[j].astype(BF), gs[j]).astype(BF)
        if (row + SEG) % BLOCK == 0:
            at = slice(row + SEG - BLOCK, row + SEG)
            part_ref[at] = dot(dmix_ref[at], w_ref[...]).astype(BF)


def attention_grads_body(
    scalars, dmix_ref, x_ref, att_ref, dres_ref, own_a, own_b, oth_a, oth_b, sums_ref, full_ref
):
    core = scalars[0]
    d_mixed = dmix_ref[...]
    sums_ref[...] = column_sum(d_mixed.astype(F32))
    rows = d_mixed.shape[1]
    full_ref[:rows] = t_dot(d_mixed, x_ref[...]).astype(BF)
    full_ref[rows:] = t_dot(att_ref[...], dres_ref[...].astype(BF)).astype(BF)
    width = own_a.shape[0] // 2
    for part, (own_ref, oth_ref) in enumerate(((own_a, oth_a), (own_a, oth_a), (own_b, oth_b), (own_b, oth_b))):
        at = slice((part % 2) * width, (part % 2 + 1) * width)
        base = part * 2 * width
        own_ref[at] = full_ref[pl.ds(pl.multiple_of(base + core * width, width), width)]
        oth_ref[at] = full_ref[pl.ds(pl.multiple_of(base + (1 - core) * width, width), width)]


def attention_join_body(sides_ref, a_mine, a_got, b_mine, b_got, qkv_ref, out_ref):
    rows = a_mine.shape[0]
    for half_ref, which in ((a_mine, sides_ref[0]), (a_got, 1 - sides_ref[0])):
        qkv_ref[pl.ds(pl.multiple_of(which * rows, rows), rows)] = half_ref[...].astype(F32)
    low = sides_ref[1] == 0
    mine, got = b_mine[...].astype(F32), b_got[...].astype(F32)
    qkv_ref[2 * rows :] = jnp.where(low, mine, got)
    out_ref[...] = jnp.where(low, got, mine)


def sum_split_body(side_ref, a_ref, b_ref, keep_ref, send_ref, sum_ref):
    rows = keep_ref.shape[0]
    side = side_ref[0]
    sum_ref[...] = (a_ref[...].astype(F32) + b_ref[...].astype(F32)).astype(BF)
    keep_ref[...] = sum_ref[pl.ds(pl.multiple_of(side * rows, rows), rows)]
    send_ref[...] = sum_ref[pl.ds(pl.multiple_of((1 - side) * rows, rows), rows)]


def sum_body(a_ref, b_ref, out_ref):
    out_ref[...] = (a_ref[...].astype(F32) + b_ref[...].astype(F32)).astype(BF)


def join_body(side_ref, a_ref, b_ref, out_ref):
    rows = a_ref.shape[0]
    side = side_ref[0]
    out_ref[pl.ds(pl.multiple_of(side * rows, rows), rows)] = a_ref[...].astype(out_ref.dtype)
    out_ref[pl.ds(pl.multiple_of((1 - side) * rows, rows), rows)] = b_ref[...].astype(out_ref.dtype)


def layer_out_body(scalars, mine_ref, got_ref, result_mine, result_got, out_ref):
    step = pl.program_id(0)
    rows = out_ref.shape[0]
    steps = pl.num_programs(0) // 2
    value = jnp.where(step // steps == scalars[0], mine_ref[...].astype(F32), got_ref[...].astype(F32))
    row = lax.broadcasted_iota(jnp.int32, (rows, 1), 0)
    for j in range(rows // SEG):
        slot = scalars[2] + step * (rows // SEG) + j
        result = jnp.where(scalars[0] == 0, result_mine[pl.ds(slot, 1)], result_got[pl.ds(slot, 1)])
        value = jnp.where(row == j * SEG, result, value)
    out_ref[...] = value.astype(BF)


def tokens_grad_body(scalars, mine_ref, got_ref, out_ref):
    steps = pl.num_programs(0) // 2
    own = pl.program_id(0) // steps == scalars[0]

    @pl.when(own)
    def _():
        out_ref[...] = mine_ref[...]

    @pl.when(jnp.logical_not(own))
    def _():
        out_ref[...] = got_ref[...]


def tail_rows_body(a_ref, b_ref, mixed_ref, pre_ref, out_ref):
    pair = mixed_ref.shape[1] // 3
    out_ref[0:3] = a_ref[...]
    out_ref[3:6] = b_ref[...]
    out_ref[6:7] = jnp.zeros_like(out_ref[6:7])
    out_ref[6:7, :pair] = mixed_ref[:, :pair]
    out_ref[7:8] = jnp.zeros_like(out_ref[7:8])
    out_ref[7:8, :pair] = mixed_ref[:, 2 * pair :]
    out_ref[8:10] = pre_ref[...]


def tail_cores_body(mine_ref, got_ref, out_ref):
    out_ref[0:8] = mine_ref[0:8] + got_ref[0:8]
    out_ref[8:9] = mine_ref[8:9] + got_ref[9:10]


def finish_body(
    scalars, tail_ref, ub_ref, la_mine, lb_mine, ca_mine, cb_mine, pos_mine, la_got, lb_got, ca_got, cb_got, pos_got,
    gains_ref, shifts_ref, qv_ref, up_ref, cgains_ref, cshifts_ref, pos_ref,
):
    low = scalars[0] == 0

    def chosen(mine, got):
        return jnp.where(low, mine[...], got[...])

    def rows_of(a, b):
        return jnp.concatenate([b[0:1], a[0:1]], axis=0), jnp.concatenate([b[1:3], a[1:3]], axis=0)

    tail = tail_ref[...]
    la, lb = chosen(la_mine, la_got), chosen(lb_mine, lb_got)
    gains_ref[...], shifts_ref[...] = rows_of(tail[0:3] + la, tail[3:6] + lb)
    cgains_ref[...], cshifts_ref[...] = rows_of(chosen(ca_mine, ca_got), chosen(cb_mine, cb_got))
    pos_ref[...] = chosen(pos_mine, pos_got)
    width = qv_ref.shape[1]
    both = tail[6:8, : 2 * width]
    qv_ref[...] = jnp.where(low, both[:, :width], both[:, width:])
    up_ref[...] = tail[8:9] + ub_ref[...]


def add_rows_body(mine_ref, got_ref, dres_ref, out_ref):
    out_ref[...] = (mine_ref[...].astype(F32) + got_ref[...].astype(F32)) + dres_ref[...]


def row_grads_body(mix_ref, low_ref, att_ref, dres_ref, hidden_ref, dpre_ref, act_ref, dsec_ref,
                   qkv_out, bias_out, out_out, up_out, ub_out, down_out):
    qkv_out[...] = t_dot(mix_ref[...], low_ref[...].astype(BF))
    bias_out[...] = column_sum(mix_ref[...].astype(F32))
    out_out[...] = t_dot(att_ref[...], dres_ref[...])
    up_out[...] = t_dot(hidden_ref[...], dpre_ref[0])
    ub_out[...] = column_sum(dpre_ref[0].astype(F32))
    down_out[...] = t_dot(act_ref[0], dsec_ref[...].astype(BF))


def add_grads_body(sides_ref, hidden_ref, dpre_ref, act_ref, dsec_ref, down_a, down_b, up_a, up_b,
                   down_out, up_out, ub_out):
    for j, (a_ref, b_ref, out_ref) in enumerate(((down_a, down_b, down_out), (up_a, up_b, up_out))):
        rows = a_ref.shape[0]
        side = sides_ref[j]
        if j == 0:
            out_ref[...] = t_dot(act_ref[0], dsec_ref[...])
        else:
            out_ref[...] = t_dot(hidden_ref[...], dpre_ref[0])
        at = pl.ds(pl.multiple_of(side * rows, rows), rows)
        out_ref[at] = out_ref[at] + a_ref[...].astype(F32)
        at = pl.ds(pl.multiple_of((1 - side) * rows, rows), rows)
        out_ref[at] = out_ref[at] + b_ref[...].astype(F32)
    ub_out[...] = column_sum(dpre_ref[0].astype(F32))


def make_shards(n_dp):
    core_pairs = [(i, i ^ 1) for i in range(4)]
    x_pairs = [(i, i ^ 2) for i in range(4)]
    bits = [1 << k for k in range(n_dp.bit_length() - 1)]
    swapped = [bits[1], bits[0], *bits[2:]]

    def core_swap(value):
        return lax.ppermute(value, "mp", core_pairs)

    def x_swap(value):
        return lax.ppermute(value, "mp", x_pairs)

    def dp_swap(value, bit):
        return lax.ppermute(value, "dp", [(i, i ^ bit) for i in range(n_dp)])

    def shards(
        tokens,
        seg_counts,
        seg_order,
        seg_qkv,
        seg_qv_bias,
        seg_out,
        seg_up,
        seg_up_bias,
        seg_down,
        seg_gains,
        seg_shifts,
        cls_qkv,
        cls_qv_bias,
        cls_out,
        cls_up,
        cls_up_bias,
        cls_down,
        cls_gains,
        cls_shifts,
        pos_table,
        cotangent,
    ):
        outer = Outer()

        def run(*args, **options):
            if slots > 64:
                options["vmem"] = 56
            return call(outer, *args, **options)

        def tied(value, *others):
            result = tie(value, *others)
            if value in outer:
                outer.add(result)
            return result

        core = lax.axis_index("mp") % 2
        dp_index = lax.axis_index("dp")
        rows = tokens.shape[0] // 2
        own_segs = rows // SEG
        slots = seg_order.shape[0]
        width = seg_qkv.shape[2]
        pair = 2 * width
        model = tokens.shape[1]
        ff = seg_down.shape[0]
        places = pos_table.shape[0]

        def ordered(low_side, mine, other, axis):
            return jnp.where(
                low_side,
                jnp.concatenate([mine, other], axis=axis),
                jnp.concatenate([other, mine], axis=axis),
            )

        def paired(value, axis):
            return ordered(core == 0, value, core_swap(value), axis)

        def gather_slots(value, last_after):
            value = paired(value, 0)
            for bit in bits:
                if bit == bits[-1]:
                    before = value
                    value = tied(value, last_after)
                value = ordered((dp_index & bit) == 0, value, dp_swap(value, bit), 0)
            return value, before

        def half(value, which, axis):
            size = value.shape[axis] // 2
            return lax.dynamic_slice_in_dim(value, which * size, size, axis)

        def own_half(value, axis):
            return half(value, core, axis)

        def side_of(bit):
            return jnp.where((dp_index & bit) == 0, 0, 1).astype(jnp.int32).reshape(1)

        def split_sum(a, b, bit):
            size = a.shape[0] // 2
            if size % 16 == 0:
                return run(
                    sum_split_body,
                    [((size, model), BF)] * 2,
                    (side_of(bit), a, b),
                    "sum_split",
                    far=(0,),
                    scratch=[pltpu.VMEM(a.shape, BF)],
                )
            value = (a.astype(F32) + b.astype(F32)).astype(BF)
            side = side_of(bit)[0]
            return half(value, side, 0), half(value, 1 - side, 0)

        def joined(mine, got, bit, dtype=BF):
            if mine.shape[0] % 16 == 0:
                return run(
                    join_body,
                    [((2 * mine.shape[0], model), dtype)],
                    (side_of(bit), mine, got),
                    "join",
                )[0]
            return ordered((dp_index & bit) == 0, mine, got, 0).astype(dtype)

        outer.add(seg_gains, seg_shifts, cls_gains, cls_shifts, pos_table)
        scalars = jnp.stack([core, (dp_index * 2 + core) * own_segs, dp_index * 2 * own_segs]).astype(jnp.int32)

        def weights(qkv, qv_bias, out, up, up_bias, down):
            flat = jnp.transpose(qkv, (1, 2, 0))
            bias = up_bias.reshape(1, ff)
            outs = out.reshape(1, width, model)
            heads = (flat, core_swap(flat), qv_bias, core_swap(qv_bias), outs, core_swap(outs))
            hidden = (up, core_swap(up), down, core_swap(down), bias, core_swap(bias))
            outer.add(*heads, *hidden)
            return heads, hidden

        s_heads, (s_up0, s_up1, s_down0, s_down1, *s_ub) = weights(
            seg_qkv, seg_qv_bias, seg_out, seg_up, seg_up_bias, seg_down
        )
        c_heads, (c_up0, c_up1, c_down0, c_down1, *c_ub) = weights(
            cls_qkv, cls_qv_bias, cls_out, cls_up, cls_up_bias, cls_down
        )

        part1, lead_part, lead_rest, q, k, v, att, s_qkv, s_out, x = run(
            seg_attention_body,
            [((rows, model), BF), ((own_segs, model), F32), ((own_segs, 2 * model), F32)]
            + [((rows, pair), BF)] * 4
            + [((3 * pair, model), BF), ((pair, model), BF), ((rows, model), BF)],
            (scalars, tokens, cotangent, *s_heads),
            "seg_attention",
            far=(0, 3, 4, 5, 6, 7, 8, 9),
            scratch=[
                pltpu.VMEM((own_segs, 16, model), BF),
                pltpu.SemaphoreType.DMA,
                pltpu.SemaphoreType.DMA((own_segs,)),
            ],
            vmem=18,
            stay=(1, 2),
        )
        lead_sum = lead_part + x_swap(lead_part)
        got1 = x_swap(part1)
        message, before_last = gather_slots(jnp.concatenate([lead_sum.astype(BF), lead_rest.astype(BF)], axis=1), got1)

        mlp_weights = (s_up0, s_up1, s_down0, s_down1)
        l_resid, l_hidden, l_act, l_slope, l_part = run(
            lead_mlp_body,
            [((slots, model), F32), ((slots, model), BF), ((2, slots, ff), BF), ((2, slots, ff), F32),
             ((slots, model), BF)],
            (message, seg_gains, seg_shifts, s_up0, s_up1, *s_ub, s_down0, s_down1),
            "lead_mlp",
            far=(0, 1, 2, 3),
            scratch=[pltpu.VMEM((2, slots, model), F32)],
        )
        got_l1 = x_swap(l_part)
        owner_row, owner_col, place_row, place_col = run(
            layout_body,
            [((1, slots), F32), ((slots, 1), F32), ((1, slots), F32), ((slots, 1), F32)],
            (seg_counts.reshape(1, -1), seg_order.reshape(1, -1)),
            "layout",
            far=(0, 1, 2, 3),
        )
        part2, resid, act, slope = run(
            seg_mlp_body,
            [((rows, model), BF), ((rows, model), F32), ((rows, 2 * ff), BF), ((rows, 2 * ff), F32)],
            (x, tied(part1, before_last), got1, seg_gains, seg_shifts, s_up0, s_up1, *s_ub, s_down0, s_down1),
            "seg_mlp",
            far=(0, 1, 2),
            vmem=18,
        )
        l_second, c_value, c_q, c_k, c_v, c_att, c_part1, c_qkv, c_out = run(
            cls_attention_body,
            [((slots, model), F32)] * 2
            + [((slots, pair), BF)] * 4
            + [((slots, model), BF), ((3 * pair, model), BF), ((pair, model), BF)],
            (scalars, l_resid, l_part, got_l1, seg_gains, seg_shifts, owner_row, owner_col, place_col,
             pos_table, *c_heads),
            "cls_attention",
            far=(0, 1, 2, 3, 4, 5, 7, 8),
        )
        d_second_low, hidden_low, d_pre, first_low, d_second, part3, sums_a, d_pre_sum = run(
            seg_mlp_back_body,
            [((rows, model), BF), ((rows, model), BF), ((rows, 2 * ff), BF), ((rows, model), BF),
             ((rows, model), F32), ((rows, model), BF), ((3, model), F32), ((2, ff), F32)],
            (scalars, resid, tied(part2, l_part), x_swap(part2), cotangent, slope, seg_gains, seg_shifts, *mlp_weights),
            "seg_mlp_back",
            far=(3, 4, 5, 6, 7),
            scratch=[pltpu.VMEM((rows, model), BF), pltpu.SemaphoreType.DMA],
            stay=(4,),
            vmem=18,
        )
        g_down, g_down_oth, g_up, g_up_oth = run(
            mlp_grads_body,
            [((ff, model), BF), ((ff, model), BF), ((model, ff), BF), ((model, ff), BF)],
            (tied(act, got_l1), d_second_low, hidden_low, d_pre),
            "seg_mlp_grads",
            far=(0, 2),
        )
        got_down, got_up = core_swap(g_down_oth), core_swap(g_up_oth)
        got3 = x_swap(part3)
        keep_down, send_down = split_sum(tied(g_down, c_part1), got_down, bits[0])
        keep_up, send_up = split_sum(tied(g_up, c_part1), got_up, swapped[0])
        got_c1 = tied(x_swap(c_part1), send_down, send_up, got3)
        c_resid, c_hidden, c_act, c_slope, c_part2 = run(
            cls_mlp_body,
            [((slots, model), F32), ((slots, model), BF), ((2, slots, ff), BF), ((2, slots, ff), F32),
             ((slots, model), BF)],
            (c_value, c_part1, got_c1, cls_gains, cls_shifts, c_up0, c_up1, *c_ub, c_down0, c_down1),
            "cls_mlp",
            far=(0, 1, 2, 3),
            scratch=[pltpu.VMEM((2, slots, model), F32)],
        )

        keep_down, send_down = split_sum(tied(keep_down, c_part2), dp_swap(send_down, bits[0]), bits[1])
        keep_up, send_up = split_sum(tied(keep_up, c_part2), dp_swap(send_up, swapped[0]), swapped[1])
        c_result, c_d_second, c_d_pre, c_part3, c_sums_a = run(
            cls_mlp_back_body,
            [((slots, model), F32), ((slots, model), F32), ((2, slots, ff), BF), ((slots, model), BF),
             ((3, model), F32)],
            (c_resid, c_part2, tied(x_swap(c_part2), send_down, send_up), message, c_slope, cls_gains, cls_shifts, c_up0, c_up1, c_down0, c_down1),
            "cls_mlp_back",
            far=(0, 1, 2, 4),
            scratch=[pltpu.VMEM((2, slots, model), F32)],
        )
        for step in range(2, len(bits)):
            keep_down, send_down = split_sum(tied(keep_down, c_part3), dp_swap(send_down, bits[step - 1]), bits[step])
            keep_up, send_up = split_sum(tied(keep_up, c_part3), dp_swap(send_up, swapped[step - 1]), swapped[step])
        c_d_resid, c_d_resid_low, c_d_mixed, c_part4, c_sums_b = run(
            cls_attention_back_body,
            [((slots, model), F32), ((slots, model), BF), ((slots, 3 * pair), BF), ((slots, model), BF),
             ((3, model), F32)],
            (c_resid, c_part3, tied(x_swap(c_part3), send_down, send_up), c_d_second, cls_gains, c_q, c_k, c_v, owner_row, owner_col,
             c_qkv, c_out),
            "cls_attention_back",
            far=(0, 1, 2, 4),
        )

        l_d_second, l_d_second_low, l_d_pre, l_part3, l_sums_a, pos_grad = run(
            lead_mlp_back_body,
            [((slots, model), F32), ((slots, model), BF), ((2, slots, ff), BF), ((slots, model), BF),
             ((3, model), F32), ((places, model), F32)],
            (c_part4, x_swap(c_part4), c_d_resid, l_second, l_slope, seg_gains, place_row, *mlp_weights),
            "lead_mlp_back",
            far=(0, 1, 2, 4, 5),
            scratch=[pltpu.VMEM((2, slots, model), F32)],
        )
        d_resid, d_att, sums_b = run(
            seg_out_back_body,
            [((rows, model), F32), ((rows, pair), BF), ((3, model), F32)],
            (resid, part3, tied(got3, l_part3), d_second, seg_gains, s_out),
            "seg_out_back",
            far=(2,),
        )
        down = run(sum_body, [(keep_down.shape, BF)], (tied(keep_down, l_part3), dp_swap(send_down, bits[-1])), "sum")[0]
        up = run(sum_body, [(keep_up.shape, BF)], (tied(keep_up, l_part3), dp_swap(send_up, swapped[-1])), "sum")[0]
        part4, d_resid, d_mixed, l_sums_b = run(
            seg_attention_back_body,
            [((rows, model), BF), ((rows, model), F32), ((rows, 3 * pair), BF), ((3, model), F32)],
            (scalars, l_resid, l_part3, tied(x_swap(l_part3), down, up), l_d_second, seg_gains, s_out, s_qkv, q, k, v, d_att, d_resid),
            "seg_attention_back",
            far=(1, 3),
            scratch=(pltpu.VMEM((slots, model), F32), pltpu.VMEM((slots, pair), F32), pltpu.VMEM((rows, pair), F32)),
            vmem=18,
        )
        got4 = x_swap(part4)
        spread = list(range(len(bits) - 1, 0, -1))
        first = spread[0]
        down = joined(tied(down, part4), dp_swap(down, bits[first]), bits[first])
        up = joined(tied(up, part4), dp_swap(up, swapped[first]), swapped[first])
        own_a, own_b, oth_a, oth_b, mixed_sum = run(
            attention_grads_body,
            [((2 * width, model), BF)] * 4 + [((1, 3 * pair), F32)],
            (scalars, d_mixed, tied(x, down, up), att, d_resid),
            "seg_attention_grads",
            far=(0, 1, 4),
            scratch=[pltpu.VMEM((8 * width, model), BF)],
        )
        keep_a, send_a = split_sum(own_a, core_swap(oth_a), bits[0])
        keep_b, send_b = split_sum(own_b, core_swap(oth_b), swapped[0])
        own_c_mixed = own_half(tied(c_d_mixed, send_a, send_b).reshape(slots, 3, pair), 2).reshape(slots, 3 * width)
        cg_qkv, cg_bias, cg_out, cg_up, cg_ub, cg_down = run(
            row_grads_body,
            [((3 * width, model), F32), ((1, 3 * width), F32), ((width, model), F32), ((model, ff), F32),
             ((1, ff), F32), ((ff, model), F32)],
            (own_c_mixed, c_value, own_half(c_att, 1), c_d_resid_low, c_hidden, c_d_pre, c_act, c_d_second),
            "cls_grads",
        )
        layer_out = call_blocks(
            layer_out_body,
            [((2 * rows, model), BF)],
            scalars,
            (tied(first_low, send_a, send_b), core_swap(first_low), c_result, core_swap(c_result)),
            "layer_out",
            2 * rows // BLOCK,
            BLOCK,
            "mmww",
        )[0]
        tail = run(
            tail_rows_body,
            [((10, model), F32)],
            (sums_a, sums_b, mixed_sum, d_pre_sum),
            "tail_rows",
        )[0]
        tail = run(tail_cores_body, [((9, model), F32)], (tail, core_swap(tail)), "tail_cores")[0]
        for step, (bit_a, bit_b) in enumerate(zip(bits, swapped)):
            if step > 0:
                keep_a, send_a = split_sum(*a_next, bit_a)
                keep_b, send_b = split_sum(*b_next, bit_b)
            if step == 1:
                d_rows = run(add_rows_body, [((rows, model), F32)], (part4, tied(got4, send_a, send_b), d_resid), "add_rows")[0]
                tokens_grad = call_blocks(
                    tokens_grad_body,
                    [((2 * rows, model), F32)],
                    scalars,
                    (d_rows, core_swap(d_rows)),
                    "tokens_grad",
                    2 * rows // BLOCK,
                    BLOCK,
                    "mm",
                )[0]
            others = [tail]
            if step == 0:
                others += [cg_bias, layer_out]
            if step + 1 < len(spread):
                at = spread[step + 1]
                down = joined(down, dp_swap(down, bits[at]), bits[at])
                up = joined(up, dp_swap(up, swapped[at]), swapped[at])
                others += [down, up]
            got_a, got_b = dp_swap(send_a, bit_a), dp_swap(send_b, bit_b)
            a_next, b_next = (keep_a, tied(got_a, *others)), (keep_b, got_b)
            tail = tail + dp_swap(tail, bits[step])
        value_a = run(sum_body, [(a_next[0].shape, BF)], a_next, "sum")[0]
        value_b = run(sum_body, [(b_next[0].shape, BF)], b_next, "sum")[0]
        sides = jnp.concatenate([side_of(bits[0]), side_of(swapped[0])])
        grad_down, grad_up, l_up_bias = run(
            add_grads_body,
            [((ff, model), F32), ((model, ff), F32), ((1, ff), F32)],
            (sides, l_hidden, l_d_pre, l_act, l_d_second_low,
             down, dp_swap(down, bits[0]), up, dp_swap(up, swapped[0])),
            "seg_add_grads",
        )
        for step in spread:
            got_a, got_b = dp_swap(value_a, bits[step]), dp_swap(value_b, swapped[step])
            if step == spread[0]:
                got_a = tied(got_a, tail, tokens_grad)
            if step == spread[-1]:
                got_a = tied(got_a, l_up_bias)
            value_a, value_b = joined(value_a, got_a, bits[step]), joined(value_b, got_b, swapped[step])
        a_parts = (value_a, dp_swap(value_a, bits[0]))
        b_parts = (value_b, dp_swap(value_b, swapped[0]))
        g_qkv, g_out = run(
            attention_join_body,
            [((3 * width, model), F32), ((width, model), F32)],
            (sides, *a_parts, *b_parts),
            "seg_attention_join",
        )
        lead_sums = (l_sums_a, l_sums_b, c_sums_a, c_sums_b, pos_grad)
        m_gains, m_shifts, qv_total, up_total, cls_gains_grad, cls_shifts_grad, pos_grad = run(
            finish_body,
            [((2, model), F32), ((4, model), F32), ((2, width), F32), ((1, ff), F32), ((2, model), F32),
             ((4, model), F32), ((places, model), F32)],
            (scalars, tail, l_up_bias, *lead_sums, *[core_swap(part) for part in lead_sums]),
            "finish",
        )

        def unflatten(flat):
            return jnp.transpose(flat.reshape(3, width, model), (2, 0, 1))

        seg_grads = (
            unflatten(g_qkv),
            qv_total,
            g_out,
            grad_up,
            up_total[0],
            grad_down,
            m_gains,
            m_shifts,
        )
        cls_grads = (
            unflatten(cg_qkv),
            cg_bias.reshape(3, width)[::2],
            cg_out,
            cg_up,
            cg_ub[0],
            cg_down,
            cls_gains_grad,
            cls_shifts_grad,
        )
        return (layer_out, tokens_grad, *seg_grads, *cls_grads, pos_grad)

    return shards


def solution(mesh):
    in_specs = (
        P("dp", None),
        P(),
        P(),
        P(None, None, "mp"),
        P(None, "mp"),
        P("mp", None),
        P(None, "mp"),
        P("mp"),
        P("mp", None),
        P(),
        P(),
        P(None, None, "mp"),
        P(None, "mp"),
        P("mp", None),
        P(None, "mp"),
        P("mp"),
        P("mp", None),
        P(),
        P(),
        P(),
        P("dp", None),
    )
    out_specs = (
        P("dp", None),
        P("dp", None),
        P(None, None, "mp"),
        P(None, "mp"),
        P("mp", None),
        P(None, "mp"),
        P("mp"),
        P("mp", None),
        P(),
        P(),
        P(None, None, "mp"),
        P(None, "mp"),
        P("mp", None),
        P(None, "mp"),
        P("mp"),
        P("mp", None),
        P(),
        P(),
        P(),
    )
    return jax.shard_map(
        make_shards(mesh.shape["dp"]), mesh=mesh, in_specs=in_specs, out_specs=out_specs, check_vma=False
    )
```

```python
import functools

import jax
import jax.numpy as jnp
from jax import lax
from jax.experimental import pallas as pl
from jax.experimental.pallas import tpu as pltpu
from jax.sharding import PartitionSpec as P

HEAD = 64
SEG = 128
LANES = 128
EPSILON = 1e-05
BF = jnp.bfloat16
F32 = jnp.float32


def dot(a, b):
    return lax.dot_general(a, b, (((1,), (0,)), ((), ())), preferred_element_type=F32)


def dot_t(a, b):
    return lax.dot_general(a, b, (((1,), (1,)), ((), ())), preferred_element_type=F32)


def t_dot(a, b):
    return lax.dot_general(a, b, (((0,), (0,)), ((), ())), preferred_element_type=F32)


def norm_parts(value):
    center = value - jnp.mean(value, axis=-1, keepdims=True)
    rstd = lax.rsqrt(jnp.mean(center * center, axis=-1, keepdims=True) + EPSILON)
    return center * rstd, rstd


def norm_back(grad, normed, rstd, gain):
    gy = grad * gain
    return rstd * (
        gy
        - jnp.mean(gy, axis=-1, keepdims=True)
        - normed * jnp.mean(gy * normed, axis=-1, keepdims=True)
    )


def gelu_both(pre):
    cdf = 0.5 * (1.0 + lax.erf(pre * 0.7071067811865476))
    pdf = 0.3989422804014327 * jnp.exp(-0.5 * pre * pre)
    return pre * cdf, cdf + pre * pdf


def column_sum(value):
    return jnp.sum(value, axis=0, keepdims=True)


def softmax(scores):
    powers = jnp.exp(scores - jnp.max(scores, axis=-1, keepdims=True))
    return powers * (1.0 / jnp.sum(powers, axis=-1, keepdims=True))


def head_masks(dtype):
    lane = lax.broadcasted_iota(jnp.int32, (1, LANES), 1)
    return [(lane < HEAD).astype(F32).astype(dtype), (lane >= HEAD).astype(F32).astype(dtype)]


def stacked(tile, masks):
    return jnp.concatenate([tile * masks[0], tile * masks[1]], axis=0)


class Outer:
    def __init__(self):
        self.held = {}

    def add(self, *values):
        for value in values:
            self.held[id(value)] = value
        return values

    def __contains__(self, value):
        return self.held.get(id(value)) is value


def call(outer, body, outs, args, name, far=(), scratch=(), vmem=16, stay=()):
    def spec(i, a):
        if i in stay:
            return pl.BlockSpec(memory_space=pltpu.HBM)
        return pl.BlockSpec(memory_space=pltpu.SMEM if a.dtype == jnp.int32 and a.ndim == 1 else pltpu.VMEM)

    results = pl.pallas_call(
        body,
        out_shape=tuple(
            pltpu.HBM(s, d) if i in far else jax.ShapeDtypeStruct(s, d) for i, (s, d) in enumerate(outs)
        ),
        in_specs=[spec(i, a) for i, a in enumerate(args)],
        out_specs=tuple(pl.BlockSpec(memory_space=pltpu.VMEM) for _ in outs),
        scratch_shapes=list(scratch),
        compiler_params=pltpu.CompilerParams(vmem_limit_bytes=vmem * 1024 * 1024),
        name=name,
    )(*[pltpu.with_memory_space_constraint(a, pltpu.HBM) if i in stay or a in outer else a for i, a in enumerate(args)])
    outer.add(*[result for i, result in enumerate(results) if i in far])
    return results


def call_blocks(body, outs, scalars, args, name, grid, rows, kinds, vmem=14):
    def spec(shape, kind):
        if kind == "w":
            return pl.BlockSpec(shape, lambda i, scalars: (0,) * len(shape))
        steps = shape[0] // rows
        return pl.BlockSpec((rows, *shape[1:]), lambda i, scalars: (i % steps, 0))

    return pl.pallas_call(
        body,
        out_shape=tuple(jax.ShapeDtypeStruct(s, d) for s, d in outs),
        grid_spec=pltpu.PrefetchScalarGridSpec(
            num_scalar_prefetch=1,
            grid=(grid,),
            in_specs=[spec(a.shape, k) for k, a in zip(kinds, args, strict=True)],
            out_specs=tuple(spec(s, "m") for s, _ in outs),
        ),
        compiler_params=pltpu.CompilerParams(vmem_limit_bytes=vmem * 1024 * 1024),
        name=name,
    )(scalars, *args)


def tie(value, *others):
    return lax.optimization_barrier((value, *others))[0]


BLOCK = 256


def blocks_of(rows):
    return [slice(at, at + BLOCK) for at in range(0, rows, BLOCK)]


def layout_body(counts_ref, order_ref, owner_row, owner_col, place_row, place_col):
    docs, slots = counts_ref.shape[1], order_ref.shape[1]
    counts = counts_ref[...].astype(F32)
    order = order_ref[...].astype(F32)

    def iotas(a, b):
        return [lax.broadcasted_iota(jnp.int32, (a, b), d).astype(F32) for d in (0, 1)]

    def to_column(row):
        size = row.shape[1]
        r, c = iotas(size, size)
        return jnp.sum(jnp.where(r == c, row, 0.0), axis=1, keepdims=True)

    def to_row(col):
        size = col.shape[0]
        r, c = iotas(size, size)
        return column_sum(jnp.where(r == c, col, 0.0))

    def total(row):
        return jnp.sum(row, axis=1, keepdims=True)

    r, c = iotas(docs, docs)
    ends_col = jnp.sum(jnp.where(c <= r, counts, 0.0), axis=1, keepdims=True)
    ends_row = to_row(ends_col)
    starts_col = ends_col - to_column(counts)
    starts_row = ends_row - counts
    index = lax.broadcasted_iota(jnp.int32, (1, docs), 1).astype(F32)
    top = jnp.max(counts, axis=1, keepdims=True)
    longest = jnp.min(jnp.where(counts == top, index, float(docs)), axis=1, keepdims=True)
    lead = total(jnp.where(index == longest, starts_row, 0.0))
    trail = total(jnp.where(index == longest, ends_row, 0.0)) - 1.0
    slot = lax.broadcasted_iota(jnp.int32, (1, slots), 1).astype(F32)
    head = total(jnp.where(slot == 0.0, order, 0.0))
    held = jnp.where(slot == 0.0, lead, jnp.where(order == lead, head, order))
    last = total(jnp.where(slot == slots - 1.0, held, 0.0))
    held = jnp.where(slot == slots - 1.0, trail, jnp.where(held == trail, last, held))
    owner = column_sum((held >= ends_col).astype(F32))
    r, _ = iotas(docs, slots)
    start = column_sum(jnp.where(r == owner, starts_col, 0.0))
    place = held - start
    owner_row[...] = owner
    owner_col[...] = to_column(owner)
    place_row[...] = place
    place_col[...] = to_column(place)


def pair_weights(core, own_ref, oth_ref, w_ref):
    parts, width = own_ref.shape[0], own_ref.shape[1]
    for part in range(parts):
        base = part * 2 * width
        w_ref[pl.ds(pl.multiple_of(base + core * width, width), width)] = own_ref[part]
        w_ref[pl.ds(pl.multiple_of(base + (1 - core) * width, width), width)] = oth_ref[part]


def pair_bias(core, own_ref, oth_ref):
    own, oth = own_ref[...], oth_ref[...]
    low = jnp.where(core == 0, own, oth)
    return jnp.concatenate([low, jnp.where(core == 0, oth, own)], axis=1)


def seg_attention_body(
    scalars, x_any, cot_any, own_ref, oth_ref, b_own, b_oth, wo_own, wo_oth,
    part_ref, lead_ref, rest_ref, q_ref, k_ref, v_ref, att_ref,
    w_ref, wo_ref, x_ref, cot_ref, x_sem, cot_sem,
):
    rows, pair = q_ref.shape
    model = x_any.shape[1]
    segs, packed = cot_ref.shape[0], cot_ref.shape[1]
    base = pl.multiple_of(scalars[0] * rows, rows)
    x_copy = pltpu.make_async_copy(x_any.at[pl.ds(base, rows)], x_ref, x_sem)
    x_copy.start()
    cot_copies = [
        pltpu.make_async_copy(cot_any.at[pl.ds(base + j * SEG, packed)], cot_ref.at[j], cot_sem.at[j])
        for j in range(segs)
    ]
    for copy in cot_copies:
        copy.start()
    pair_weights(scalars[0], own_ref, oth_ref, w_ref)
    pair_weights(scalars[0], wo_own, wo_oth, wo_ref)
    bias = pair_bias(scalars[0], b_own, b_oth)
    masks = head_masks(BF)
    x_copy.wait()
    for rs in blocks_of(rows):
        x = x_ref[rs]
        q_ref[rs] = (dot_t(x, w_ref[:pair]) + bias[0:1]).astype(BF)
        k_ref[rs] = dot_t(x, w_ref[pair : 2 * pair]).astype(BF)
        v_ref[rs] = (dot_t(x, w_ref[2 * pair :]) + bias[1:2]).astype(BF)
        for row in range(rs.start, rs.stop, SEG):
            ats = [(slice(row, row + SEG), slice(col, col + LANES)) for col in range(0, pair, LANES)]
            scores = [dot_t(stacked(q_ref[at], masks), k_ref[at]) * 0.125 for at in ats]
            probs = [softmax(score).astype(BF) for score in scores]
            both = [jnp.concatenate([p[:SEG], p[SEG:]], axis=1) for p in probs]
            for at, weight in zip(ats, both):
                att_ref[at] = dot(weight, stacked(v_ref[at], masks)).astype(BF)
        part = dot(att_ref[rs], wo_ref[...])
        part_ref[rs] = part.astype(BF)
        for row in range(0, BLOCK, SEG):
            j = (rs.start + row) // SEG
            lead_ref[j : j + 1] = part[row : row + 1]
            rest_ref[j : j + 1, :model] = x[row : row + 1].astype(F32)
    for j, copy in enumerate(cot_copies):
        copy.wait()
        rest_ref[j : j + 1, model:] = cot_ref[j, 0:1].astype(F32)


def own_copy(scalars, source, target, sem):
    rows = target.shape[0]
    copy = pltpu.make_async_copy(source.at[pl.ds(pl.multiple_of(scalars[0] * rows, rows), rows)], target, sem)
    copy.start()
    return copy


def seg_mlp_body(
    scalars, x_any, mine_ref, got_ref, gains_ref, shifts_ref, up0, up1, ub0, ub1, down0, down1,
    part_ref, resid_ref, act_ref, slope_ref,
    x_ref, x_sem,
):
    own_copy(scalars, x_any, x_ref, x_sem).wait()
    for rs in blocks_of(resid_ref.shape[0]):
        branch = mine_ref[rs].astype(F32) + got_ref[rs].astype(F32)
        resid = x_ref[rs].astype(F32) + branch + shifts_ref[0:1]
        resid_ref[rs] = resid
        normed, _ = norm_parts(resid)
        hidden_low = (normed * gains_ref[0:1] + shifts_ref[1:2]).astype(BF)
        parts = []
        for j, (up, ub, down) in enumerate(((up0, ub0, down0), (up1, ub1, down1))):
            at = (rs, slice(j * up.shape[1], (j + 1) * up.shape[1]))
            act, slope = gelu_both(dot(hidden_low, up[...]) + ub[...])
            low = act.astype(BF)
            act_ref[at] = low
            slope_ref[at] = slope
            parts.append(dot(low, down[...]))
        part_ref[rs] = (parts[0] + parts[1]).astype(BF)


def seg_mlp_back_body(
    scalars, resid_ref, mine_ref, got_ref, cot_any, slope_ref, act_ref, gains_ref, shifts_ref, up0, up1, down0, down1,
    dsec_low_ref, hidden_ref, dpre_ref, out_ref, dsec_ref, part_ref, sums_ref, dpre_sum_ref, down_ref, up_ref,
    cot_ref, cot_sem,
):
    copy = own_copy(scalars, cot_any, cot_ref, cot_sem)
    blocks = blocks_of(resid_ref.shape[0])
    for rs in blocks:
        normed, _ = norm_parts(resid_ref[rs])
        hidden = normed * gains_ref[0:1] + shifts_ref[1:2]
        hidden_ref[rs] = hidden.astype(BF)
        second = hidden + (mine_ref[rs].astype(F32) + got_ref[rs].astype(F32)) + shifts_ref[2:3]
        n2, rstd2 = norm_parts(second)
        out_ref[rs] = (n2 * gains_ref[1:2] + shifts_ref[3:4]).astype(BF)
        lead = lax.broadcasted_iota(jnp.int32, (BLOCK, 1), 0) % SEG == 0
        if rs.start == 0:
            copy.wait()
        gy = jnp.where(lead, 0.0, cot_ref[rs].astype(F32))
        d_second = norm_back(gy, n2, rstd2, gains_ref[1:2])
        dsec_ref[rs] = d_second
        low = d_second.astype(BF)
        dsec_low_ref[rs] = low
        parts, pre_sums = [], []
        for j, (up, down) in enumerate(((up0, down0), (up1, down1))):
            at = (rs, slice(j * up.shape[1], (j + 1) * up.shape[1]))
            d_pre = (dot_t(low, down[...]) * slope_ref[at]).astype(BF)
            dpre_ref[at] = d_pre
            pre_sums.append(column_sum(d_pre.astype(F32)))
            parts.append(dot_t(d_pre, up[...]))
        part_ref[rs] = (parts[0] + parts[1]).astype(BF)
        sums = jnp.concatenate([column_sum(gy * n2), column_sum(d_second), column_sum(gy)], axis=0)
        pre_sums = jnp.concatenate(pre_sums, axis=0)
        if rs.start == 0:
            sums_ref[...] = sums
            dpre_sum_ref[...] = pre_sums
        else:
            sums_ref[...] += sums
            dpre_sum_ref[...] += pre_sums
    size = down_ref.shape[0]
    down_ref[...] = t_dot(act_ref[:, size:], dsec_low_ref[...]).astype(BF)
    up_ref[...] = t_dot(hidden_ref[...], dpre_ref[:, size:]).astype(BF)


def cut(side, value_ref, keep_ref, send_ref):
    rows = keep_ref.shape[0]
    keep_ref[...] = value_ref[pl.ds(pl.multiple_of(side * rows, rows), rows)]
    send_ref[...] = value_ref[pl.ds(pl.multiple_of((1 - side) * rows, rows), rows)]


def own_mlp_grads_body(
    sides_ref, act_ref, low_ref, hidden_ref, dpre_ref, got_down, got_up,
    keep_down, send_down, keep_up, send_up, down_ref, up_ref,
):
    size = down_ref.shape[0]
    down_ref[...] = (t_dot(act_ref[:, :size], low_ref[...]) + got_down[...].astype(F32)).astype(BF)
    cut(sides_ref[0], down_ref, keep_down, send_down)
    up_ref[...] = (t_dot(hidden_ref[...], dpre_ref[:, :size]) + got_up[...].astype(F32)).astype(BF)
    cut(sides_ref[1], up_ref, keep_up, send_up)


def add_cut(sides_ref, at, first, second):
    for j, (a_ref, b_ref, keep_ref, send_ref, sum_ref) in enumerate((first, second)):
        sum_ref[...] = (a_ref[...].astype(F32) + b_ref[...].astype(F32)).astype(BF)
        cut(sides_ref[at + j], sum_ref, keep_ref, send_ref)


def seg_out_back_body(
    scalars, resid_ref, mine_ref, got_ref, dsec_ref, gains_ref, wo_own, wo_oth,
    dres_ref, datt_ref, sums_ref,
    wo_ref,
):
    pair_weights(scalars[0], wo_own, wo_oth, wo_ref)
    for rs in blocks_of(resid_ref.shape[0]):
        n1, rstd1 = norm_parts(resid_ref[rs])
        d_hidden = (mine_ref[rs].astype(F32) + got_ref[rs].astype(F32)) + dsec_ref[rs]
        d_resid = norm_back(d_hidden, n1, rstd1, gains_ref[0:1])
        dres_ref[rs] = d_resid
        datt_ref[rs] = dot_t(d_resid.astype(BF), wo_ref[...]).astype(BF)
        sums = jnp.concatenate([column_sum(d_hidden * n1), column_sum(d_resid), column_sum(d_hidden)], axis=0)
        if rs.start == 0:
            sums_ref[...] = sums
        else:
            sums_ref[...] += sums


def mlp_rows(hidden_low, up0, up1, ub0, ub1, down0, down1, act_ref, slope_ref, part_ref, half_ref):
    for j, (up, ub, down) in enumerate(((up0, ub0, down0), (up1, ub1, down1))):
        act, slope = gelu_both(dot(hidden_low, up[...]) + ub[...])
        low = act.astype(BF)
        act_ref[j] = low
        slope_ref[j] = slope
        half_ref[j] = dot(low, down[...])
    part_ref[...] = (half_ref[0] + half_ref[1]).astype(BF)


def mlp_rows_back(low, slope_ref, up0, up1, down0, down1, dpre_ref, part_ref, half_ref):
    for j, (up, down) in enumerate(((up0, down0), (up1, down1))):
        d_pre = (dot_t(low, down[...]) * slope_ref[j]).astype(BF)
        dpre_ref[j] = d_pre
        half_ref[j] = dot_t(d_pre, up[...])
    part_ref[...] = (half_ref[0] + half_ref[1]).astype(BF)


def lead_mlp_body(
    message_ref, gains_ref, shifts_ref, up0, up1, ub0, ub1, down0, down1,
    resid_ref, hidden_ref, act_ref, slope_ref, part_ref, half_ref,
):
    model = resid_ref.shape[1]
    resid = message_ref[:, :model].astype(F32) + message_ref[:, model : 2 * model].astype(F32) + shifts_ref[0:1]
    resid_ref[...] = resid
    n1, _ = norm_parts(resid)
    hidden_low = (n1 * gains_ref[0:1] + shifts_ref[1:2]).astype(BF)
    hidden_ref[...] = hidden_low
    mlp_rows(hidden_low, up0, up1, ub0, ub1, down0, down1, act_ref, slope_ref, part_ref, half_ref)


def cls_attention_body(
    scalars, resid_ref, mine_ref, got_ref, sgains_ref, sshifts_ref, owner_row, owner_col, place_col, table_ref,
    own_ref, oth_ref, b_own, b_oth, wo_own, wo_oth,
    second_ref, value_ref, q_ref, k_ref, v_ref, att_ref, part_ref,
    w_ref, wo_ref,
):
    pair = q_ref.shape[1]
    pair_weights(scalars[0], own_ref, oth_ref, w_ref)
    pair_weights(scalars[0], wo_own, wo_oth, wo_ref)
    bias = pair_bias(scalars[0], b_own, b_oth)
    n1, _ = norm_parts(resid_ref[...])
    hidden = n1 * sgains_ref[0:1] + sshifts_ref[1:2]
    second = hidden + (mine_ref[...].astype(F32) + got_ref[...].astype(F32)) + sshifts_ref[2:3]
    second_ref[...] = second
    n2, _ = norm_parts(second)
    first = n2 * sgains_ref[1:2] + sshifts_ref[3:4]
    slots, places = resid_ref.shape[0], table_ref.shape[0]
    index = lax.broadcasted_iota(jnp.int32, (slots, places), 1).astype(F32)
    hot = (index == place_col[...]).astype(F32).astype(BF)
    value = first + dot(hot, table_ref[...])
    value_ref[...] = value
    low = value.astype(BF)
    q_ref[...] = (dot_t(low, w_ref[:pair]) + bias[0:1]).astype(BF)
    k_ref[...] = dot_t(low, w_ref[pair : 2 * pair]).astype(BF)
    v_ref[...] = (dot_t(low, w_ref[2 * pair :]) + bias[1:2]).astype(BF)
    allowed = owner_row[...] == owner_col[...]
    masks = head_masks(BF)
    for col in range(0, pair, LANES):
        at = slice(col, col + LANES)
        q, k, v = q_ref[:, at], k_ref[:, at], v_ref[:, at]
        tile = None
        for mask in masks:
            scores = jnp.where(allowed, dot_t(q * mask, k) * 0.125, -1000000000.0)
            one = dot(softmax(scores).astype(BF), v * mask)
            tile = one if tile is None else tile + one
        att_ref[:, at] = tile.astype(BF)
    part_ref[...] = dot(att_ref[...], wo_ref[...]).astype(BF)


def cls_mlp_body(
    value_ref, mine_ref, got_ref, gains_ref, shifts_ref, up0, up1, ub0, ub1, down0, down1,
    resid_ref, hidden_ref, act_ref, slope_ref, part_ref, half_ref,
):
    resid = value_ref[...] + (mine_ref[...].astype(F32) + got_ref[...].astype(F32)) + shifts_ref[0:1]
    resid_ref[...] = resid
    n1, _ = norm_parts(resid)
    hidden_low = (n1 * gains_ref[0:1] + shifts_ref[1:2]).astype(BF)
    hidden_ref[...] = hidden_low
    mlp_rows(hidden_low, up0, up1, ub0, ub1, down0, down1, act_ref, slope_ref, part_ref, half_ref)


def cls_mlp_back_body(
    resid_ref, mine_ref, got_ref, message_ref, slope_ref, gains_ref, shifts_ref, up0, up1, down0, down1,
    sides_ref, kept_down, came_down, kept_up, came_up,
    result_ref, dsec_ref, dpre_ref, part_ref, sums_ref, keep_down, send_down, keep_up, send_up,
    half_ref, down_ref, up_ref,
):
    add_cut(sides_ref, 2, (kept_down, came_down, keep_down, send_down, down_ref), (kept_up, came_up, keep_up, send_up, up_ref))
    n1, _ = norm_parts(resid_ref[...])
    hidden = n1 * gains_ref[0:1] + shifts_ref[1:2]
    second = hidden + (mine_ref[...].astype(F32) + got_ref[...].astype(F32)) + shifts_ref[2:3]
    n2, rstd2 = norm_parts(second)
    result_ref[...] = n2 * gains_ref[1:2] + shifts_ref[3:4]
    gy = message_ref[:, 2 * result_ref.shape[1] :].astype(F32)
    d_second = norm_back(gy, n2, rstd2, gains_ref[1:2])
    dsec_ref[...] = d_second
    mlp_rows_back(d_second.astype(BF), slope_ref, up0, up1, down0, down1, dpre_ref, part_ref, half_ref)
    sums_ref[...] = jnp.concatenate([column_sum(gy * n2), column_sum(d_second), column_sum(gy)], axis=0)


def cls_attention_back_body(
    scalars, resid_ref, mine_ref, got_ref, dsec_ref, gains_ref, q_ref, k_ref, v_ref, owner_row, owner_col,
    own_ref, oth_ref, wo_own, wo_oth,
    dres_ref, dres_low_ref, dmix_ref, part_ref, sums_ref,
    w_ref, wo_ref,
):
    pair = q_ref.shape[1]
    pair_weights(scalars[0], own_ref, oth_ref, w_ref)
    pair_weights(scalars[0], wo_own, wo_oth, wo_ref)
    n1, rstd1 = norm_parts(resid_ref[...])
    d_hidden = (mine_ref[...].astype(F32) + got_ref[...].astype(F32)) + dsec_ref[...]
    d_resid = norm_back(d_hidden, n1, rstd1, gains_ref[0:1])
    dres_ref[...] = d_resid
    low = d_resid.astype(BF)
    dres_low_ref[...] = low
    sums_ref[...] = jnp.concatenate(
        [column_sum(d_hidden * n1), column_sum(d_resid), column_sum(d_hidden)], axis=0
    )
    d_att = dot_t(low, wo_ref[...]).astype(BF)
    allowed = owner_row[...] == owner_col[...]
    masks = head_masks(BF)
    for col in range(0, pair, LANES):
        at = slice(col, col + LANES)
        q, k, v, g = q_ref[:, at], k_ref[:, at], v_ref[:, at], d_att[:, at]
        total = [None] * 3
        for mask in masks:
            qm, gm = q * mask, g * mask
            probs = softmax(jnp.where(allowed, dot_t(qm, k) * 0.125, -1000000000.0))
            d_prob = dot_t(gm, v)
            ds = (probs * (d_prob - jnp.sum(probs * d_prob, axis=-1, keepdims=True))).astype(BF)
            one = [dot(ds, k * mask), t_dot(ds, qm), t_dot(probs.astype(BF), gm)]
            total = [a if b is None else a + b for a, b in zip(one, total)]
        for j, scale in enumerate((0.125, 0.125, 1.0)):
            dmix_ref[:, j * pair + col : j * pair + col + LANES] = (total[j] * scale).astype(BF)
    part_ref[...] = dot(dmix_ref[...], w_ref[...]).astype(BF)


def lead_mlp_back_body(
    mine_ref, got_ref, dres_ref, second_ref, slope_ref, sgains_ref, place_row, up0, up1, down0, down1,
    sides_ref, kept_down, came_down, kept_up, came_up,
    dsec_ref, dsec_low_ref, dpre_ref, part_ref, sums_ref, pos_ref, keep_ref, send_ref,
    half_ref, down_ref, up_ref,
):
    cut_last(sides_ref[4], (kept_down, came_down, down_ref), (kept_up, came_up, up_ref), keep_ref, send_ref)
    gy = (mine_ref[...].astype(F32) + got_ref[...].astype(F32)) + dres_ref[...]
    n2, rstd2 = norm_parts(second_ref[...])
    d_second = norm_back(gy, n2, rstd2, sgains_ref[1:2])
    dsec_ref[...] = d_second
    low = d_second.astype(BF)
    dsec_low_ref[...] = low
    mlp_rows_back(low, slope_ref, up0, up1, down0, down1, dpre_ref, part_ref, half_ref)
    sums_ref[...] = jnp.concatenate([column_sum(gy * n2), column_sum(d_second), column_sum(gy)], axis=0)
    places, slots = pos_ref.shape[0], gy.shape[0]
    index = lax.broadcasted_iota(jnp.int32, (places, slots), 0).astype(F32)
    hot = (index == place_row[...]).astype(F32)
    pos_ref[...] = lax.dot_general(
        hot, gy, (((1,), (0,)), ((), ())), preferred_element_type=F32, precision=lax.Precision.HIGHEST
    )


def seg_attention_back_body(
    scalars, lresid_ref, lmine_ref, lgot_ref, ldsec_ref, gains_ref, wo_own, wo_oth, own_ref, oth_ref,
    q_ref, k_ref, v_ref, datt_ref, dres_ref, sums_a, sums_b, dpre_sums,
    part_ref, dres_out, dmix_ref, lsums_ref, rows_ref,
    lead_dres, lead_datt, datt_all, w_ref, wo_ref,
):
    rows, pair = q_ref.shape
    pair_weights(scalars[0], own_ref, oth_ref, w_ref)
    pair_weights(scalars[0], wo_own, wo_oth, wo_ref)
    n1, rstd1 = norm_parts(lresid_ref[...])
    d_hidden = (lmine_ref[...].astype(F32) + lgot_ref[...].astype(F32)) + ldsec_ref[...]
    d_resid = norm_back(d_hidden, n1, rstd1, gains_ref[0:1])
    lead_dres[...] = d_resid
    lead_datt[...] = dot_t(d_resid.astype(BF), wo_ref[...]).astype(BF).astype(F32)
    lsums_ref[...] = jnp.concatenate(
        [column_sum(d_hidden * n1), column_sum(d_resid), column_sum(d_hidden)], axis=0
    )
    masks = head_masks(BF)
    for row in range(0, rows, SEG):
        rs = slice(row, row + SEG)
        slot = scalars[1] + row // SEG
        dres_out[rs] = dres_ref[rs]
        dres_out[row : row + 1] = lead_dres[pl.ds(slot, 1)]
        datt_all[rs] = datt_ref[rs].astype(F32)
        datt_all[row : row + 1] = lead_datt[pl.ds(slot, 1)]
        ats = [(rs, slice(col, col + LANES)) for col in range(0, pair, LANES)]
        qs = [stacked(q_ref[at], masks) for at in ats]
        gs = [stacked(datt_all[at].astype(BF), masks) for at in ats]
        scores = [dot_t(q, k_ref[at]) * 0.125 for q, at in zip(qs, ats)]
        d_probs = [dot_t(g, v_ref[at]) for g, at in zip(gs, ats)]
        probs = [softmax(score) for score in scores]
        d_scores = [
            (p * (d - jnp.sum(p * d, axis=-1, keepdims=True))).astype(BF) for p, d in zip(probs, d_probs)
        ]
        for j, at in enumerate(ats):
            col = j * LANES
            both = jnp.concatenate([d_scores[j][:SEG], d_scores[j][SEG:]], axis=1)
            dmix_ref[rs, col : col + LANES] = (dot(both, stacked(k_ref[at], masks)) * 0.125).astype(BF)
            col += pair
            dmix_ref[rs, col : col + LANES] = (t_dot(d_scores[j], qs[j]) * 0.125).astype(BF)
            col += pair
            dmix_ref[rs, col : col + LANES] = t_dot(probs[j].astype(BF), gs[j]).astype(BF)
        if (row + SEG) % BLOCK == 0:
            at = slice(row + SEG - BLOCK, row + SEG)
            part_ref[at] = dot(dmix_ref[at], w_ref[...]).astype(BF)
    mixed = column_sum(dmix_ref[...].astype(F32))
    rows_ref[0:3] = sums_a[...]
    rows_ref[3:6] = sums_b[...]
    rows_ref[6:8] = jnp.zeros_like(rows_ref[6:8])
    rows_ref[6:7, :pair] = mixed[:, :pair]
    rows_ref[7:8, :pair] = mixed[:, 2 * pair :]
    rows_ref[8:10] = dpre_sums[...]


def attention_grads_body(
    scalars, dmix_ref, x_any, att_ref, dres_ref, kept_ref, came_ref,
    oth_a, oth_b, value_ref, own_a, own_b,
    full_ref, x_ref, x_sem,
):
    copy = own_copy(scalars, x_any, x_ref, x_sem)
    sum_body(kept_ref, came_ref, value_ref)
    core = scalars[0]
    d_mixed = dmix_ref[...]
    rows = d_mixed.shape[1]
    full_ref[rows:] = t_dot(att_ref[...], dres_ref[...].astype(BF)).astype(BF)
    copy.wait()
    full_ref[:rows] = t_dot(d_mixed, x_ref[...]).astype(BF)
    width = own_a.shape[0] // 2
    for part, (own_ref, oth_ref) in enumerate(((own_a, oth_a), (own_a, oth_a), (own_b, oth_b), (own_b, oth_b))):
        at = slice((part % 2) * width, (part % 2 + 1) * width)
        base = part * 2 * width
        own_ref[at] = full_ref[pl.ds(pl.multiple_of(base + core * width, width), width)]
        oth_ref[at] = full_ref[pl.ds(pl.multiple_of(base + (1 - core) * width, width), width)]


def two_cuts_body(at, sides_ref, a_mine, a_got, b_mine, b_got, keep_a, send_a, keep_b, send_b, a_ref, b_ref):
    add_cut(sides_ref, at, (a_mine, a_got, keep_a, send_a, a_ref), (b_mine, b_got, keep_b, send_b, b_ref))


def cut_last(side, first, second, keep_ref, send_ref):
    rows = keep_ref.shape[0] // 2
    for j, (mine, got, sum_ref) in enumerate((first, second)):
        sum_ref[...] = (mine[...].astype(F32) + got[...].astype(F32)).astype(BF)
        keep_ref[j * rows : (j + 1) * rows] = sum_ref[pl.ds(pl.multiple_of(side * rows, rows), rows)]
        send_ref[j * rows : (j + 1) * rows] = sum_ref[pl.ds(pl.multiple_of((1 - side) * rows, rows), rows)]


def last_cut_body(at, sides_ref, a_mine, a_got, b_mine, b_got, keep_ref, send_ref, a_ref, b_ref):
    cut_last(sides_ref[at], (a_mine, a_got, a_ref), (b_mine, b_got, b_ref), keep_ref, send_ref)


def last_cut_join_body(
    at, step, sides_ref, a_mine, a_got, b_mine, b_got, c_mine, c_got, d_mine, d_got,
    keep_ref, send_ref, c_ref, d_ref, a_ref, b_ref,
):
    cut_last(sides_ref[at], (a_mine, a_got, a_ref), (b_mine, b_got, b_ref), keep_ref, send_ref)
    join(sides_ref[step], c_mine, c_got, c_ref)
    join(sides_ref[step + 1], d_mine, d_got, d_ref)


def parts_join(side, mine_ref, got_ref, a_ref, b_ref):
    rows = mine_ref.shape[0] // 2
    for j, out_ref in enumerate((a_ref, b_ref)):
        out_ref[pl.ds(pl.multiple_of(side * rows, rows), rows)] = mine_ref[j * rows : (j + 1) * rows]
        out_ref[pl.ds(pl.multiple_of((1 - side) * rows, rows), rows)] = got_ref[j * rows : (j + 1) * rows]


def first_join_body(at, sides_ref, mine_ref, got_ref, a_ref, b_ref):
    parts_join(sides_ref[at], mine_ref, got_ref, a_ref, b_ref)


def cut_first_join_body(
    at, step, sides_ref, a_mine, a_got, b_mine, b_got, mine_ref, got_ref,
    keep_a, send_a, keep_b, send_b, c_ref, d_ref, a_ref, b_ref,
):
    add_cut(sides_ref, at, (a_mine, a_got, keep_a, send_a, a_ref), (b_mine, b_got, keep_b, send_b, b_ref))
    parts_join(sides_ref[step], mine_ref, got_ref, c_ref, d_ref)


def sum_body(a_ref, b_ref, out_ref):
    out_ref[...] = (a_ref[...].astype(F32) + b_ref[...].astype(F32)).astype(BF)


def join(side, a_ref, b_ref, out_ref):
    rows = a_ref.shape[0]
    out_ref[pl.ds(pl.multiple_of(side * rows, rows), rows)] = a_ref[...]
    out_ref[pl.ds(pl.multiple_of((1 - side) * rows, rows), rows)] = b_ref[...]


def two_joins_body(at, sides_ref, a_mine, a_got, b_mine, b_got, a_ref, b_ref):
    join(sides_ref[at], a_mine, a_got, a_ref)
    join(sides_ref[at + 1], b_mine, b_got, b_ref)


def attention_join_body(sides_ref, a_mine, a_got, b_mine, b_got, qkv_ref, out_ref):
    rows = a_mine.shape[0]
    for half_ref, which in ((a_mine, sides_ref[0]), (a_got, 1 - sides_ref[0])):
        qkv_ref[pl.ds(pl.multiple_of(which * rows, rows), rows)] = half_ref[...].astype(F32)
    low = sides_ref[1] == 0
    mine, got = b_mine[...].astype(F32), b_got[...].astype(F32)
    qkv_ref[2 * rows :] = jnp.where(low, mine, got)
    out_ref[...] = jnp.where(low, got, mine)


def layer_out_body(scalars, mine_ref, got_ref, result_mine, result_got, out_ref):
    step = pl.program_id(0)
    rows = out_ref.shape[0]
    steps = pl.num_programs(0) // 2
    value = jnp.where(step // steps == scalars[0], mine_ref[...].astype(F32), got_ref[...].astype(F32))
    row = lax.broadcasted_iota(jnp.int32, (rows, 1), 0)
    for j in range(rows // SEG):
        slot = scalars[2] + step * (rows // SEG) + j
        result = jnp.where(scalars[0] == 0, result_mine[pl.ds(slot, 1)], result_got[pl.ds(slot, 1)])
        value = jnp.where(row == j * SEG, result, value)
    out_ref[...] = value.astype(BF)


def tokens_grad_body(scalars, mine_ref, got_ref, out_ref):
    steps = pl.num_programs(0) // 2
    own = pl.program_id(0) // steps == scalars[0]

    @pl.when(own)
    def _():
        out_ref[...] = mine_ref[...]

    @pl.when(jnp.logical_not(own))
    def _():
        out_ref[...] = got_ref[...]


def tail_cores_body(mine_ref, got_ref, out_ref):
    out_ref[0:8] = mine_ref[0:8] + got_ref[0:8]
    out_ref[8:9] = mine_ref[8:9] + got_ref[9:10]


def finish_body(
    scalars, tail_ref, ub_ref, la_mine, lb_mine, ca_mine, cb_mine, pos_mine, la_got, lb_got, ca_got, cb_got, pos_got,
    gains_ref, shifts_ref, qv_ref, up_ref, cgains_ref, cshifts_ref, pos_ref,
):
    low = scalars[0] == 0

    def chosen(mine, got):
        return jnp.where(low, mine[...], got[...])

    def rows_of(a, b):
        return jnp.concatenate([b[0:1], a[0:1]], axis=0), jnp.concatenate([b[1:3], a[1:3]], axis=0)

    tail = tail_ref[...]
    la, lb = chosen(la_mine, la_got), chosen(lb_mine, lb_got)
    gains_ref[...], shifts_ref[...] = rows_of(tail[0:3] + la, tail[3:6] + lb)
    cgains_ref[...], cshifts_ref[...] = rows_of(chosen(ca_mine, ca_got), chosen(cb_mine, cb_got))
    pos_ref[...] = chosen(pos_mine, pos_got)
    width = qv_ref.shape[1]
    both = tail[6:8, : 2 * width]
    qv_ref[...] = jnp.where(low, both[:, :width], both[:, width:])
    up_ref[...] = tail[8:9] + ub_ref[...]


def add_rows_body(mine_ref, got_ref, dres_ref, out_ref):
    out_ref[...] = (mine_ref[...].astype(F32) + got_ref[...].astype(F32)) + dres_ref[...]


def cls_grads_body(
    scalars, mix_ref, low_ref, att_ref, dres_ref, hidden_ref, dpre_ref, act_ref, dsec_ref,
    qkv_out, bias_out, out_out, up_out, ub_out, down_out,
    full_ref,
):
    core = scalars[0]
    width = out_out.shape[0]
    pair = 2 * width

    def own(base):
        return full_ref[pl.ds(pl.multiple_of(base + core * width, width), width)]

    full_ref[...] = t_dot(mix_ref[...], low_ref[...].astype(BF))
    for part in range(3):
        qkv_out[part * width : (part + 1) * width] = own(part * pair)
    full_ref[:pair] = t_dot(att_ref[...], dres_ref[...])
    out_out[...] = own(0)
    sums = column_sum(mix_ref[...].astype(F32))
    for row, base in enumerate((0, 2 * pair)):
        bias_out[row : row + 1] = jnp.where(core == 0, sums[:, base : base + width], sums[:, base + width : base + pair])
    up_out[...] = t_dot(hidden_ref[...], dpre_ref[0])
    ub_out[...] = column_sum(dpre_ref[0].astype(F32))
    down_out[...] = t_dot(act_ref[0], dsec_ref[...].astype(BF))


def add_grads_body(sides_ref, hidden_ref, dpre_ref, act_ref, dsec_ref, down_a, down_b, up_a, up_b,
                   down_out, up_out, ub_out):
    for j, (a_ref, b_ref, out_ref) in enumerate(((down_a, down_b, down_out), (up_a, up_b, up_out))):
        rows = a_ref.shape[0]
        side = sides_ref[j]
        if j == 0:
            out_ref[...] = t_dot(act_ref[0], dsec_ref[...])
        else:
            out_ref[...] = t_dot(hidden_ref[...], dpre_ref[0])
        at = pl.ds(pl.multiple_of(side * rows, rows), rows)
        out_ref[at] = out_ref[at] + a_ref[...].astype(F32)
        at = pl.ds(pl.multiple_of((1 - side) * rows, rows), rows)
        out_ref[at] = out_ref[at] + b_ref[...].astype(F32)
    ub_out[...] = column_sum(dpre_ref[0].astype(F32))


def make_shards(n_dp):
    core_pairs = [(i, i ^ 1) for i in range(4)]
    x_pairs = [(i, i ^ 2) for i in range(4)]
    bits = [1 << k for k in range(n_dp.bit_length() - 1)]
    swapped = [bits[1], bits[0], *bits[2:]]

    def core_swap(value):
        return lax.ppermute(value, "mp", core_pairs)

    def x_swap(value):
        return lax.ppermute(value, "mp", x_pairs)

    def dp_swap(value, bit):
        return lax.ppermute(value, "dp", [(i, i ^ bit) for i in range(n_dp)])

    def shards(
        tokens,
        seg_counts,
        seg_order,
        seg_qkv,
        seg_qv_bias,
        seg_out,
        seg_up,
        seg_up_bias,
        seg_down,
        seg_gains,
        seg_shifts,
        cls_qkv,
        cls_qv_bias,
        cls_out,
        cls_up,
        cls_up_bias,
        cls_down,
        cls_gains,
        cls_shifts,
        pos_table,
        cotangent,
    ):
        outer = Outer()

        def run(*args, **options):
            if slots > 64:
                options["vmem"] = 56
            return call(outer, *args, **options)

        def tied(value, *others):
            result = tie(value, *others)
            if value in outer:
                outer.add(result)
            return result

        core = lax.axis_index("mp") % 2
        dp_index = lax.axis_index("dp")
        rows = tokens.shape[0] // 2
        own_segs = rows // SEG
        slots = seg_order.shape[0]
        width = seg_qkv.shape[2]
        pair = 2 * width
        model = tokens.shape[1]
        ff = seg_down.shape[0]
        places = pos_table.shape[0]

        def ordered(low_side, mine, other, axis):
            return jnp.where(
                low_side,
                jnp.concatenate([mine, other], axis=axis),
                jnp.concatenate([other, mine], axis=axis),
            )

        def paired(value, axis):
            return ordered(core == 0, value, core_swap(value), axis)

        def gather_slots(value, last_after):
            value = paired(value, 0)
            for bit in bits:
                if bit == bits[1]:
                    before = value
                    value = tied(value, last_after)
                value = ordered((dp_index & bit) == 0, value, dp_swap(value, bit), 0)
            return value, before

        def half(value, which, axis):
            size = value.shape[axis] // 2
            return lax.dynamic_slice_in_dim(value, which * size, size, axis)

        def own_half(value, axis):
            return half(value, core, axis)

        def side_of(bit):
            return jnp.where((dp_index & bit) == 0, 0, 1).astype(jnp.int32).reshape(1)

        def two_cuts(step, a, a_got, b, b_got):
            size = a.shape[0] // 2
            if size % 16 == 0:
                return run(
                    functools.partial(two_cuts_body, 2 * step),
                    [((size, model), BF)] * 4,
                    (sides, a, a_got, b, b_got),
                    "two_cuts",
                    far=(0, 2),
                    scratch=[pltpu.VMEM(a.shape, BF), pltpu.VMEM(b.shape, BF)],
                )
            out = []
            for mine, got, bit in ((a, a_got, bits[step]), (b, b_got, swapped[step])):
                value = (mine.astype(F32) + got.astype(F32)).astype(BF)
                side = side_of(bit)[0]
                out += [half(value, side, 0), half(value, 1 - side, 0)]
            return out

        last = len(bits) - 1

        def last_cut(a, a_got, b, b_got):
            size = a.shape[0] // 2
            if size % 16 == 0:
                return run(
                    functools.partial(last_cut_body, 2 * last),
                    [((2 * size, model), BF)] * 2,
                    (sides, a, a_got, b, b_got),
                    "last_cut",
                    far=(0,),
                    scratch=[pltpu.VMEM(a.shape, BF), pltpu.VMEM(b.shape, BF)],
                )
            keep_a, send_a, keep_b, send_b = two_cuts(last, a, a_got, b, b_got)
            return jnp.concatenate([keep_a, keep_b], axis=0), jnp.concatenate([send_a, send_b], axis=0)

        def last_sum(keep, send):
            return run(sum_body, [(keep.shape, BF)], (keep, dp_swap(send, bits[-1])), "last_sum")[0]

        def first_join(value, got):
            rows = value.shape[0] // 2
            if rows % 16 == 0:
                return run(
                    functools.partial(first_join_body, 2 * last),
                    [((2 * rows, model), BF)] * 2,
                    (sides, value, got),
                    "first_join",
                )
            low = (dp_index & bits[-1]) == 0
            return ordered(low, value[:rows], got[:rows], 0), ordered(low, value[rows:], got[rows:], 0)

        def two_joins(step, a, a_got, b, b_got):
            if a.shape[0] % 16 == 0:
                return run(
                    functools.partial(two_joins_body, 2 * step),
                    [((2 * a.shape[0], model), BF), ((2 * b.shape[0], model), BF)],
                    (sides, a, a_got, b, b_got),
                    "two_joins",
                )
            return (
                ordered((dp_index & bits[step]) == 0, a, a_got, 0),
                ordered((dp_index & swapped[step]) == 0, b, b_got, 0),
            )

        sides = jnp.concatenate([side_of(bit) for two in zip(bits, swapped) for bit in two])
        outer.add(seg_gains, seg_shifts, cls_gains, cls_shifts, pos_table)
        scalars = jnp.stack([core, (dp_index * 2 + core) * own_segs, dp_index * 2 * own_segs]).astype(jnp.int32)

        def weights(qkv, qv_bias, out, up, up_bias, down):
            flat = jnp.transpose(qkv, (1, 2, 0))
            bias = up_bias.reshape(1, ff)
            outs = out.reshape(1, width, model)
            heads = (flat, core_swap(flat), qv_bias, core_swap(qv_bias), outs, core_swap(outs))
            hidden = (up, core_swap(up), down, core_swap(down), bias, core_swap(bias))
            outer.add(heads[0], heads[4], *hidden)
            return heads, hidden

        s_heads, (s_up0, s_up1, s_down0, s_down1, *s_ub) = weights(
            seg_qkv, seg_qv_bias, seg_out, seg_up, seg_up_bias, seg_down
        )
        c_heads, (c_up0, c_up1, c_down0, c_down1, *c_ub) = weights(
            cls_qkv, cls_qv_bias, cls_out, cls_up, cls_up_bias, cls_down
        )

        c_swapped = (c_heads[1], c_heads[3], c_heads[5], c_up1, c_down1, c_ub[1])
        part1, lead_part, lead_rest, q, k, v, att = run(
            seg_attention_body,
            [((rows, model), BF), ((own_segs, model), F32), ((own_segs, 2 * model), F32)]
            + [((rows, pair), BF)] * 4,
            (scalars, tokens, cotangent, tied(s_heads[0], s_ub[1]), *s_heads[1:]),
            "seg_attention",
            far=(0, 3, 4, 5, 6),
            scratch=[
                pltpu.VMEM((3 * pair, model), BF),
                pltpu.VMEM((pair, model), BF),
                pltpu.VMEM((rows, model), BF),
                pltpu.VMEM((own_segs, 16, model), BF),
                pltpu.SemaphoreType.DMA,
                pltpu.SemaphoreType.DMA((own_segs,)),
            ],
            vmem=18,
            stay=(1, 2),
        )
        lead_sum = lead_part + x_swap(lead_part)
        got1 = x_swap(part1)
        message, before_last = gather_slots(jnp.concatenate([lead_sum.astype(BF), lead_rest.astype(BF)], axis=1), got1)

        owner_row, owner_col, place_row, place_col = run(
            layout_body,
            [((1, slots), F32), ((slots, 1), F32), ((1, slots), F32), ((slots, 1), F32)],
            (seg_counts.reshape(1, -1), seg_order.reshape(1, -1)),
            "layout",
            far=(0, 1, 2, 3),
        )
        mlp_weights = (s_up0, s_up1, s_down0, s_down1)
        l_resid, l_hidden, l_act, l_slope, l_part = run(
            lead_mlp_body,
            [((slots, model), F32), ((slots, model), BF), ((2, slots, ff), BF), ((2, slots, ff), F32),
             ((slots, model), BF)],
            (tied(message, owner_row, *c_swapped), seg_gains, seg_shifts, s_up0, s_up1, *s_ub, s_down0, s_down1),
            "lead_mlp",
            far=(0, 1, 2, 3),
            scratch=[pltpu.VMEM((2, slots, model), F32)],
        )
        got_l1 = x_swap(l_part)

        part2, resid, act, slope = run(
            seg_mlp_body,
            [((rows, model), BF), ((rows, model), F32), ((rows, 2 * ff), BF), ((rows, 2 * ff), F32)],
            (scalars, tokens, tied(part1, before_last), got1, seg_gains, seg_shifts, s_up0, s_up1, *s_ub, s_down0, s_down1),
            "seg_mlp",
            far=(0, 1, 2, 3),
            scratch=[pltpu.VMEM((rows, model), BF), pltpu.SemaphoreType.DMA],
            stay=(1,),
            vmem=18,
        )
        l_second, c_value, c_q, c_k, c_v, c_att, c_part1 = run(
            cls_attention_body,
            [((slots, model), F32)] * 2
            + [((slots, pair), BF)] * 4
            + [((slots, model), BF)],
            (scalars, l_resid, l_part, got_l1, seg_gains, seg_shifts, owner_row, owner_col, place_col,
             pos_table, *c_heads),
            "cls_attention",
            far=(0, 1, 2, 3, 4, 5),
            scratch=[pltpu.VMEM((3 * pair, model), BF), pltpu.VMEM((pair, model), BF)],
        )
        got2 = x_swap(part2)
        outer.add(got2)
        d_second_low, hidden_low, d_pre, first_low, d_second, part3, sums_a, d_pre_sum, down_oth, up_oth = run(
            seg_mlp_back_body,
            [((rows, model), BF), ((rows, model), BF), ((rows, 2 * ff), BF), ((rows, model), BF),
             ((rows, model), F32), ((rows, model), BF), ((3, model), F32), ((2, ff), F32),
             ((ff, model), BF), ((model, ff), BF)],
            (scalars, resid, tied(part2, l_part), got2, cotangent, slope, tied(act, got_l1), seg_gains,
             seg_shifts, *mlp_weights),
            "seg_mlp_back",
            far=(0, 1, 2, 3, 4, 5, 6, 7),
            scratch=[pltpu.VMEM((rows, model), BF), pltpu.SemaphoreType.DMA],
            stay=(4,),
            vmem=24,
        )
        got3 = x_swap(part3)
        keep_down, send_down, keep_up, send_up = run(
            own_mlp_grads_body,
            [((ff // 2, model), BF)] * 2 + [((model // 2, ff), BF)] * 2,
            (sides, tied(act, c_part1), d_second_low, hidden_low, d_pre, core_swap(down_oth), core_swap(up_oth)),
            "seg_own_mlp_grads",
            far=(0, 2),
            scratch=[pltpu.VMEM((ff, model), BF), pltpu.VMEM((model, ff), BF)],
        )
        got_c1 = tied(x_swap(c_part1), send_down, send_up, got3)
        c_resid, c_hidden, c_act, c_slope, c_part2 = run(
            cls_mlp_body,
            [((slots, model), F32), ((slots, model), BF), ((2, slots, ff), BF), ((2, slots, ff), F32),
             ((slots, model), BF)],
            (c_value, c_part1, got_c1, cls_gains, cls_shifts, c_up0, c_up1, *c_ub, c_down0, c_down1),
            "cls_mlp",
            far=(0, 1, 2, 3),
            scratch=[pltpu.VMEM((2, slots, model), F32)],
        )

        quarter = ff // 4
        c_result, c_d_second, c_d_pre, c_part3, c_sums_a, keep_down, send_down, keep_up, send_up = run(
            cls_mlp_back_body,
            [((slots, model), F32), ((slots, model), F32), ((2, slots, ff), BF), ((slots, model), BF),
             ((3, model), F32)] + [((quarter, model), BF)] * 4,
            (c_resid, c_part2, x_swap(c_part2), message, c_slope, cls_gains, cls_shifts, c_up0, c_up1, c_down0, c_down1,
             sides, keep_down, dp_swap(send_down, bits[0]), keep_up, dp_swap(send_up, swapped[0])),
            "cls_mlp_back",
            far=(0, 1, 2, 4, 5, 7),
            scratch=[pltpu.VMEM((2, slots, model), F32)] + [pltpu.VMEM((2 * quarter, model), BF)] * 2,
        )
        c_d_resid, c_d_resid_low, c_d_mixed, c_part4, c_sums_b = run(
            cls_attention_back_body,
            [((slots, model), F32), ((slots, model), BF), ((slots, 3 * pair), BF), ((slots, model), BF),
             ((3, model), F32)],
            (scalars, c_resid, c_part3, x_swap(c_part3), c_d_second, cls_gains, c_q, c_k, c_v,
             owner_row, owner_col, c_heads[0], c_heads[1], c_heads[4], c_heads[5]),
            "cls_attention_back",
            far=(0, 1, 2, 4),
            scratch=[pltpu.VMEM((3 * pair, model), BF), pltpu.VMEM((pair, model), BF)],
        )

        for step in range(2, last):
            keep_down, send_down, keep_up, send_up = two_cuts(
                step, keep_down, dp_swap(send_down, bits[step - 1]), keep_up, dp_swap(send_up, swapped[step - 1])
            )
        fused = last == 2
        kept = (keep_down, dp_swap(send_down, bits[last - 1]), keep_up, dp_swap(send_up, swapped[last - 1]))
        if not fused:
            keep_mlp, send_mlp = last_cut(*kept)
            kept = (down_oth[:32], down_oth[:32], down_oth[:32], down_oth[:32])
        eighth = kept[0].shape[0] // 2
        l_d_second, l_d_second_low, l_d_pre, l_part3, l_sums_a, pos_grad, *cuts = run(
            lead_mlp_back_body,
            [((slots, model), F32), ((slots, model), BF), ((2, slots, ff), BF), ((slots, model), BF),
             ((3, model), F32), ((places, model), F32)] + [((2 * eighth, model), BF)] * 2,
            (c_part4, x_swap(c_part4), c_d_resid, l_second, l_slope, seg_gains, place_row,
             *mlp_weights, sides, *kept),
            "lead_mlp_back",
            far=(0, 1, 2, 4, 5, 6),
            scratch=[pltpu.VMEM((2, slots, model), F32)] + [pltpu.VMEM((2 * eighth, model), BF)] * 2,
        )
        if fused:
            keep_mlp, send_mlp = cuts
        d_resid, d_att, sums_b = run(
            seg_out_back_body,
            [((rows, model), F32), ((rows, pair), BF), ((3, model), F32)],
            (scalars, resid, part3, tied(got3, l_part3), d_second, seg_gains, s_heads[4], s_heads[5]),
            "seg_out_back",
            far=(2,),
            scratch=[pltpu.VMEM((pair, model), BF)],
        )
        part4, d_resid, d_mixed, l_sums_b, tail = run(
            seg_attention_back_body,
            [((rows, model), BF), ((rows, model), F32), ((rows, 3 * pair), BF), ((3, model), F32), ((10, model), F32)],
            (scalars, l_resid, l_part3, x_swap(l_part3), l_d_second, seg_gains, s_heads[4], s_heads[5],
             s_heads[0], s_heads[1], q, k, v, d_att, d_resid, sums_a, sums_b, d_pre_sum),
            "seg_attention_back",
            far=(1, 3),
            scratch=[
                pltpu.VMEM((slots, model), F32),
                pltpu.VMEM((slots, pair), F32),
                pltpu.VMEM((rows, pair), F32),
                pltpu.VMEM((3 * pair, model), BF),
                pltpu.VMEM((pair, model), BF),
            ],
            vmem=18,
        )
        got4 = x_swap(part4)
        tail = run(tail_cores_body, [((9, model), F32)], (tail, core_swap(tail)), "tail_cores")[0]
        tails = [tail]
        for bit in bits:
            tails.append(tails[-1] + dp_swap(tails[-1], bit))
        tail = tails[-1]
        oth_a, oth_b, value_mlp, own_a, own_b = run(
            attention_grads_body,
            [((2 * width, model), BF)] * 2 + [(keep_mlp.shape, BF)] + [((2 * width, model), BF)] * 2,
            (scalars, d_mixed, tokens, att, d_resid, keep_mlp, dp_swap(send_mlp, bits[-1])),
            "seg_attention_grads",
            far=(3, 4),
            scratch=[pltpu.VMEM((8 * width, model), BF), pltpu.VMEM((rows, model), BF), pltpu.SemaphoreType.DMA],
            stay=(2,),
        )
        keep_a, send_a, keep_b, send_b = two_cuts(0, own_a, core_swap(oth_a), own_b, core_swap(oth_b))
        got_mlp = dp_swap(value_mlp, bits[-1])
        cg_qkv, cg_bias, cg_out, cg_up, cg_ub, cg_down = run(
            cls_grads_body,
            [((3 * width, model), F32), ((2, width), F32), ((width, model), F32), ((model, ff), F32),
             ((1, ff), F32), ((ff, model), F32)],
            (scalars, tied(c_d_mixed, send_a, send_b), c_value, c_att, c_d_resid_low, c_hidden, c_d_pre, c_act, c_d_second),
            "cls_grads",
            scratch=[pltpu.VMEM((3 * pair, model), F32)],
        )
        layer_out = call_blocks(
            layer_out_body,
            [((2 * rows, model), BF)],
            scalars,
            (tied(first_low, send_a, send_b), core_swap(first_low), c_result, core_swap(c_result)),
            "layer_out",
            2 * rows // BLOCK,
            BLOCK,
            "mmww",
        )[0]
        for step in range(last):
            if step > 0:
                if fused:
                    keep_a, send_a, keep_b, send_b, down, up = run(
                        functools.partial(cut_first_join_body, 2 * step, 2 * last),
                        [((width // 2, model), BF)] * 4 + [(value_mlp.shape, BF)] * 2,
                        (sides, *a_next, *b_next, value_mlp, got_mlp),
                        "cut_first_join",
                        far=(0, 2),
                        scratch=[pltpu.VMEM((width, model), BF)] * 2,
                    )
                else:
                    keep_a, send_a, keep_b, send_b = two_cuts(step, *a_next, *b_next)
            if step == 1:
                d_rows = run(add_rows_body, [((rows, model), F32)], (part4, tied(got4, send_a, send_b), d_resid), "add_rows")[0]
                tokens_grad = call_blocks(
                    tokens_grad_body,
                    [((2 * rows, model), F32)],
                    scalars,
                    (d_rows, core_swap(d_rows)),
                    "tokens_grad",
                    2 * rows // BLOCK,
                    BLOCK,
                    "mm",
                )[0]
            others = [tails[step]] + ([cg_bias, layer_out] if step == 0 else [])
            got_a, got_b = dp_swap(send_a, bits[step]), dp_swap(send_b, swapped[step])
            a_next, b_next = (keep_a, tied(got_a, *others)), (keep_b, got_b)
        if fused:
            size = a_next[0].shape[0]
            keep_tail, send_tail, down, up = run(
                functools.partial(last_cut_join_body, 2 * last, 2),
                [((size, model), BF)] * 2 + [((2 * down.shape[0], model), BF)] * 2,
                (sides, *a_next, *b_next, down, dp_swap(down, bits[1]), up, dp_swap(up, swapped[1])),
                "last_cut_join",
                far=(0,),
                scratch=[pltpu.VMEM((size, model), BF)] * 2,
            )
        else:
            keep_tail, send_tail = last_cut(*a_next, *b_next)
            down, up = first_join(value_mlp, got_mlp)
            for at in range(last - 1, 0, -1):
                down, up = two_joins(at, down, dp_swap(down, bits[at]), up, dp_swap(up, swapped[at]))
        value_tail = last_sum(keep_tail, send_tail)
        grad_down, grad_up, l_up_bias = run(
            add_grads_body,
            [((ff, model), F32), ((model, ff), F32), ((1, ff), F32)],
            (sides, l_hidden, l_d_pre, l_act, l_d_second_low,
             down, dp_swap(down, bits[0]), up, dp_swap(up, swapped[0])),
            "seg_add_grads",
        )
        value_a, value_b = first_join(value_tail, tied(dp_swap(value_tail, bits[-1]), tail, tokens_grad))
        for step in range(last - 1, 0, -1):
            got_a, got_b = dp_swap(value_a, bits[step]), dp_swap(value_b, swapped[step])
            if step == 1:
                got_a = tied(got_a, l_up_bias)
            value_a, value_b = two_joins(step, value_a, got_a, value_b, got_b)
        a_parts = (value_a, dp_swap(value_a, bits[0]))
        b_parts = (value_b, dp_swap(value_b, swapped[0]))
        lead_sums = (l_sums_a, l_sums_b, c_sums_a, c_sums_b, pos_grad)
        m_gains, m_shifts, qv_total, up_total, cls_gains_grad, cls_shifts_grad, pos_grad = run(
            finish_body,
            [((2, model), F32), ((4, model), F32), ((2, width), F32), ((1, ff), F32), ((2, model), F32),
             ((4, model), F32), ((places, model), F32)],
            (scalars, tail, l_up_bias, *lead_sums, *[core_swap(part) for part in lead_sums]),
            "finish",
        )

        g_qkv, g_out = run(
            attention_join_body,
            [((3 * width, model), F32), ((width, model), F32)],
            (sides, tied(a_parts[0], m_gains), a_parts[1], *b_parts),
            "seg_attention_join",
        )
        def unflatten(flat):
            return jnp.transpose(flat.reshape(3, width, model), (2, 0, 1))

        seg_grads = (
            unflatten(g_qkv),
            qv_total,
            g_out,
            grad_up,
            up_total[0],
            grad_down,
            m_gains,
            m_shifts,
        )
        cls_grads = (
            unflatten(cg_qkv),
            cg_bias,
            cg_out,
            cg_up,
            cg_ub[0],
            cg_down,
            cls_gains_grad,
            cls_shifts_grad,
        )
        return (layer_out, tokens_grad, *seg_grads, *cls_grads, pos_grad)

    return shards


def solution(mesh):
    in_specs = (
        P("dp", None),
        P(),
        P(),
        P(None, None, "mp"),
        P(None, "mp"),
        P("mp", None),
        P(None, "mp"),
        P("mp"),
        P("mp", None),
        P(),
        P(),
        P(None, None, "mp"),
        P(None, "mp"),
        P("mp", None),
        P(None, "mp"),
        P("mp"),
        P("mp", None),
        P(),
        P(),
        P(),
        P("dp", None),
    )
    out_specs = (
        P("dp", None),
        P("dp", None),
        P(None, None, "mp"),
        P(None, "mp"),
        P("mp", None),
        P(None, "mp"),
        P("mp"),
        P("mp", None),
        P(),
        P(),
        P(None, None, "mp"),
        P(None, "mp"),
        P("mp", None),
        P(None, "mp"),
        P("mp"),
        P("mp", None),
        P(),
        P(),
        P(),
    )
    return jax.shard_map(
        make_shards(mesh.shape["dp"]), mesh=mesh, in_specs=in_specs, out_specs=out_specs, check_vma=False
    )
```

```python
import functools

import jax
import jax.numpy as jnp
from jax import lax
from jax.experimental import pallas as pl
from jax.experimental.pallas import tpu as pltpu
from jax.sharding import PartitionSpec as P

HEAD = 64
SEG = 128
LANES = 128
EPSILON = 1e-05
BF = jnp.bfloat16
F32 = jnp.float32


def dot(a, b):
    return lax.dot_general(a, b, (((1,), (0,)), ((), ())), preferred_element_type=F32)


def dot_t(a, b):
    return lax.dot_general(a, b, (((1,), (1,)), ((), ())), preferred_element_type=F32)


def t_dot(a, b):
    return lax.dot_general(a, b, (((0,), (0,)), ((), ())), preferred_element_type=F32)


def norm_parts(value):
    center = value - jnp.mean(value, axis=-1, keepdims=True)
    rstd = lax.rsqrt(jnp.mean(center * center, axis=-1, keepdims=True) + EPSILON)
    return center * rstd, rstd


def norm_back(grad, normed, rstd, gain):
    gy = grad * gain
    return rstd * (
        gy
        - jnp.mean(gy, axis=-1, keepdims=True)
        - normed * jnp.mean(gy * normed, axis=-1, keepdims=True)
    )


def gelu_both(pre):
    cdf = 0.5 * (1.0 + lax.erf(pre * 0.7071067811865476))
    pdf = 0.3989422804014327 * jnp.exp(-0.5 * pre * pre)
    return pre * cdf, cdf + pre * pdf


def column_sum(value):
    return jnp.sum(value, axis=0, keepdims=True)


def softmax(scores):
    powers = jnp.exp(scores - jnp.max(scores, axis=-1, keepdims=True))
    return powers * (1.0 / jnp.sum(powers, axis=-1, keepdims=True))


def head_masks(dtype):
    lane = lax.broadcasted_iota(jnp.int32, (1, LANES), 1)
    return [(lane < HEAD).astype(F32).astype(dtype), (lane >= HEAD).astype(F32).astype(dtype)]


def stacked(tile, masks):
    return jnp.concatenate([tile * masks[0], tile * masks[1]], axis=0)


class Outer:
    def __init__(self):
        self.held = {}

    def add(self, *values):
        for value in values:
            self.held[id(value)] = value
        return values

    def __contains__(self, value):
        return self.held.get(id(value)) is value


def call(outer, body, outs, args, name, far=(), scratch=(), vmem=16, stay=()):
    def spec(i, a):
        if i in stay:
            return pl.BlockSpec(memory_space=pltpu.HBM)
        return pl.BlockSpec(memory_space=pltpu.SMEM if a.dtype == jnp.int32 and a.ndim == 1 else pltpu.VMEM)

    results = pl.pallas_call(
        body,
        out_shape=tuple(
            pltpu.HBM(s, d) if i in far else jax.ShapeDtypeStruct(s, d) for i, (s, d) in enumerate(outs)
        ),
        in_specs=[spec(i, a) for i, a in enumerate(args)],
        out_specs=tuple(pl.BlockSpec(memory_space=pltpu.VMEM) for _ in outs),
        scratch_shapes=list(scratch),
        compiler_params=pltpu.CompilerParams(vmem_limit_bytes=vmem * 1024 * 1024),
        name=name,
    )(*[pltpu.with_memory_space_constraint(a, pltpu.HBM) if i in stay or a in outer else a for i, a in enumerate(args)])
    outer.add(*[result for i, result in enumerate(results) if i in far])
    return results


def call_blocks(body, outs, scalars, args, name, grid, rows, kinds, vmem=14):
    def spec(shape, kind):
        if kind == "w":
            return pl.BlockSpec(shape, lambda i, scalars: (0,) * len(shape))
        steps = shape[0] // rows
        return pl.BlockSpec((rows, *shape[1:]), lambda i, scalars: (i % steps, 0))

    return pl.pallas_call(
        body,
        out_shape=tuple(jax.ShapeDtypeStruct(s, d) for s, d in outs),
        grid_spec=pltpu.PrefetchScalarGridSpec(
            num_scalar_prefetch=1,
            grid=(grid,),
            in_specs=[spec(a.shape, k) for k, a in zip(kinds, args, strict=True)],
            out_specs=tuple(spec(s, "m") for s, _ in outs),
        ),
        compiler_params=pltpu.CompilerParams(vmem_limit_bytes=vmem * 1024 * 1024),
        name=name,
    )(scalars, *args)


def tie(value, *others):
    return lax.optimization_barrier((value, *others))[0]


BLOCK = 256


def blocks_of(rows):
    return [slice(at, at + BLOCK) for at in range(0, rows, BLOCK)]


def layout_body(counts_ref, order_ref, owner_row, owner_col, place_row, place_col):
    docs, slots = counts_ref.shape[1], order_ref.shape[1]
    counts = counts_ref[...].astype(F32)
    order = order_ref[...].astype(F32)

    def iotas(a, b):
        return [lax.broadcasted_iota(jnp.int32, (a, b), d).astype(F32) for d in (0, 1)]

    def to_column(row):
        size = row.shape[1]
        r, c = iotas(size, size)
        return jnp.sum(jnp.where(r == c, row, 0.0), axis=1, keepdims=True)

    def to_row(col):
        size = col.shape[0]
        r, c = iotas(size, size)
        return column_sum(jnp.where(r == c, col, 0.0))

    def total(row):
        return jnp.sum(row, axis=1, keepdims=True)

    r, c = iotas(docs, docs)
    ends_col = jnp.sum(jnp.where(c <= r, counts, 0.0), axis=1, keepdims=True)
    ends_row = to_row(ends_col)
    starts_col = ends_col - to_column(counts)
    starts_row = ends_row - counts
    index = lax.broadcasted_iota(jnp.int32, (1, docs), 1).astype(F32)
    top = jnp.max(counts, axis=1, keepdims=True)
    longest = jnp.min(jnp.where(counts == top, index, float(docs)), axis=1, keepdims=True)
    lead = total(jnp.where(index == longest, starts_row, 0.0))
    trail = total(jnp.where(index == longest, ends_row, 0.0)) - 1.0
    slot = lax.broadcasted_iota(jnp.int32, (1, slots), 1).astype(F32)
    head = total(jnp.where(slot == 0.0, order, 0.0))
    held = jnp.where(slot == 0.0, lead, jnp.where(order == lead, head, order))
    last = total(jnp.where(slot == slots - 1.0, held, 0.0))
    held = jnp.where(slot == slots - 1.0, trail, jnp.where(held == trail, last, held))
    owner = column_sum((held >= ends_col).astype(F32))
    r, _ = iotas(docs, slots)
    start = column_sum(jnp.where(r == owner, starts_col, 0.0))
    place = held - start
    owner_row[...] = owner
    owner_col[...] = to_column(owner)
    place_row[...] = place
    place_col[...] = to_column(place)


def pair_weights(core, own_ref, oth_ref, w_ref):
    parts, width = own_ref.shape[0], own_ref.shape[1]
    for part in range(parts):
        base = part * 2 * width
        w_ref[pl.ds(pl.multiple_of(base + core * width, width), width)] = own_ref[part]
        w_ref[pl.ds(pl.multiple_of(base + (1 - core) * width, width), width)] = oth_ref[part]


def pair_bias(core, own_ref, oth_ref):
    own, oth = own_ref[...], oth_ref[...]
    low = jnp.where(core == 0, own, oth)
    return jnp.concatenate([low, jnp.where(core == 0, oth, own)], axis=1)


def seg_attention_body(
    scalars, x_any, cot_any, own_ref, oth_ref, b_own, b_oth, wo_own, wo_oth,
    part_ref, lead_ref, rest_ref, q_ref, k_ref, v_ref, att_ref,
    w_ref, wo_ref, x_ref, cot_ref, x_sem, cot_sem,
):
    rows, pair = q_ref.shape
    model = x_any.shape[1]
    segs, packed = cot_ref.shape[0], cot_ref.shape[1]
    base = pl.multiple_of(scalars[0] * rows, rows)
    x_copy = pltpu.make_async_copy(x_any.at[pl.ds(base, rows)], x_ref, x_sem)
    x_copy.start()
    cot_copies = [
        pltpu.make_async_copy(cot_any.at[pl.ds(base + j * SEG, packed)], cot_ref.at[j], cot_sem.at[j])
        for j in range(segs)
    ]
    for copy in cot_copies:
        copy.start()
    pair_weights(scalars[0], own_ref, oth_ref, w_ref)
    pair_weights(scalars[0], wo_own, wo_oth, wo_ref)
    bias = pair_bias(scalars[0], b_own, b_oth)
    masks = head_masks(BF)
    x_copy.wait()
    for rs in blocks_of(rows):
        x = x_ref[rs]
        q_ref[rs] = (dot_t(x, w_ref[:pair]) + bias[0:1]).astype(BF)
        k_ref[rs] = dot_t(x, w_ref[pair : 2 * pair]).astype(BF)
        v_ref[rs] = (dot_t(x, w_ref[2 * pair :]) + bias[1:2]).astype(BF)
        for row in range(rs.start, rs.stop, SEG):
            ats = [(slice(row, row + SEG), slice(col, col + LANES)) for col in range(0, pair, LANES)]
            scores = [dot_t(stacked(q_ref[at], masks), k_ref[at]) * 0.125 for at in ats]
            probs = [softmax(score).astype(BF) for score in scores]
            both = [jnp.concatenate([p[:SEG], p[SEG:]], axis=1) for p in probs]
            for at, weight in zip(ats, both):
                att_ref[at] = dot(weight, stacked(v_ref[at], masks)).astype(BF)
        part = dot(att_ref[rs], wo_ref[...])
        part_ref[rs] = part.astype(BF)
        for row in range(0, BLOCK, SEG):
            j = (rs.start + row) // SEG
            lead_ref[j : j + 1] = part[row : row + 1]
            rest_ref[j : j + 1, :model] = x[row : row + 1].astype(F32)
    for j, copy in enumerate(cot_copies):
        copy.wait()
        rest_ref[j : j + 1, model:] = cot_ref[j, 0:1].astype(F32)


def own_copy(scalars, source, target, sem):
    rows = target.shape[0]
    copy = pltpu.make_async_copy(source.at[pl.ds(pl.multiple_of(scalars[0] * rows, rows), rows)], target, sem)
    copy.start()
    return copy


def seg_mlp_body(
    scalars, x_any, mine_ref, got_ref, gains_ref, shifts_ref, up0, up1, ub0, ub1, down0, down1,
    part_ref, resid_ref, act_ref, slope_ref,
    x_ref, x_sem,
):
    own_copy(scalars, x_any, x_ref, x_sem).wait()
    for rs in blocks_of(resid_ref.shape[0]):
        branch = mine_ref[rs].astype(F32) + got_ref[rs].astype(F32)
        resid = x_ref[rs].astype(F32) + branch + shifts_ref[0:1]
        resid_ref[rs] = resid
        normed, _ = norm_parts(resid)
        hidden_low = (normed * gains_ref[0:1] + shifts_ref[1:2]).astype(BF)
        parts = []
        for j, (up, ub, down) in enumerate(((up0, ub0, down0), (up1, ub1, down1))):
            at = (rs, slice(j * up.shape[1], (j + 1) * up.shape[1]))
            act, slope = gelu_both(dot(hidden_low, up[...]) + ub[...])
            low = act.astype(BF)
            act_ref[at] = low
            slope_ref[at] = slope
            parts.append(dot(low, down[...]))
        part_ref[rs] = (parts[0] + parts[1]).astype(BF)


def seg_mlp_back_body(
    scalars, resid_ref, mine_ref, got_ref, cot_any, slope_ref, act_ref, gains_ref, shifts_ref, up0, up1, down0, down1,
    dsec_low_ref, hidden_ref, dpre_ref, out_ref, dsec_ref, part_ref, sums_ref, dpre_sum_ref, down_ref, up_ref,
    cot_ref, cot_sem,
):
    copy = own_copy(scalars, cot_any, cot_ref, cot_sem)
    blocks = blocks_of(resid_ref.shape[0])
    for rs in blocks:
        normed, _ = norm_parts(resid_ref[rs])
        hidden = normed * gains_ref[0:1] + shifts_ref[1:2]
        hidden_ref[rs] = hidden.astype(BF)
        second = hidden + (mine_ref[rs].astype(F32) + got_ref[rs].astype(F32)) + shifts_ref[2:3]
        n2, rstd2 = norm_parts(second)
        out_ref[rs] = (n2 * gains_ref[1:2] + shifts_ref[3:4]).astype(BF)
        lead = lax.broadcasted_iota(jnp.int32, (BLOCK, 1), 0) % SEG == 0
        if rs.start == 0:
            copy.wait()
        gy = jnp.where(lead, 0.0, cot_ref[rs].astype(F32))
        d_second = norm_back(gy, n2, rstd2, gains_ref[1:2])
        dsec_ref[rs] = d_second
        low = d_second.astype(BF)
        dsec_low_ref[rs] = low
        parts, pre_sums = [], []
        for j, (up, down) in enumerate(((up0, down0), (up1, down1))):
            at = (rs, slice(j * up.shape[1], (j + 1) * up.shape[1]))
            d_pre = (dot_t(low, down[...]) * slope_ref[at]).astype(BF)
            dpre_ref[at] = d_pre
            pre_sums.append(column_sum(d_pre.astype(F32)))
            parts.append(dot_t(d_pre, up[...]))
        part_ref[rs] = (parts[0] + parts[1]).astype(BF)
        sums = jnp.concatenate([column_sum(gy * n2), column_sum(d_second), column_sum(gy)], axis=0)
        pre_sums = jnp.concatenate(pre_sums, axis=0)
        if rs.start == 0:
            sums_ref[...] = sums
            dpre_sum_ref[...] = pre_sums
        else:
            sums_ref[...] += sums
            dpre_sum_ref[...] += pre_sums
    size = down_ref.shape[0]
    down_ref[...] = t_dot(act_ref[:, size:], dsec_low_ref[...]).astype(BF)
    up_ref[...] = t_dot(hidden_ref[...], dpre_ref[:, size:]).astype(BF)


def cut(side, value_ref, keep_ref, send_ref):
    rows = keep_ref.shape[0]
    keep_ref[...] = value_ref[pl.ds(pl.multiple_of(side * rows, rows), rows)]
    send_ref[...] = value_ref[pl.ds(pl.multiple_of((1 - side) * rows, rows), rows)]


def own_mlp_grads_body(
    sides_ref, act_ref, low_ref, hidden_ref, dpre_ref, got_down, got_up,
    keep_down, send_down, keep_up, send_up, down_ref, up_ref,
):
    size = down_ref.shape[0]
    down_ref[...] = (t_dot(act_ref[:, :size], low_ref[...]) + got_down[...].astype(F32)).astype(BF)
    cut(sides_ref[0], down_ref, keep_down, send_down)
    up_ref[...] = (t_dot(hidden_ref[...], dpre_ref[:, :size]) + got_up[...].astype(F32)).astype(BF)
    cut(sides_ref[1], up_ref, keep_up, send_up)


def add_cut(sides_ref, at, first, second):
    for j, (a_ref, b_ref, keep_ref, send_ref, sum_ref) in enumerate((first, second)):
        sum_ref[...] = (a_ref[...].astype(F32) + b_ref[...].astype(F32)).astype(BF)
        cut(sides_ref[at + j], sum_ref, keep_ref, send_ref)


def seg_out_back_body(
    scalars, resid_ref, mine_ref, got_ref, dsec_ref, gains_ref, wo_own, wo_oth,
    dres_ref, datt_ref, sums_ref,
    wo_ref,
):
    pair_weights(scalars[0], wo_own, wo_oth, wo_ref)
    for rs in blocks_of(resid_ref.shape[0]):
        n1, rstd1 = norm_parts(resid_ref[rs])
        d_hidden = (mine_ref[rs].astype(F32) + got_ref[rs].astype(F32)) + dsec_ref[rs]
        d_resid = norm_back(d_hidden, n1, rstd1, gains_ref[0:1])
        dres_ref[rs] = d_resid
        datt_ref[rs] = dot_t(d_resid.astype(BF), wo_ref[...]).astype(BF)
        sums = jnp.concatenate([column_sum(d_hidden * n1), column_sum(d_resid), column_sum(d_hidden)], axis=0)
        if rs.start == 0:
            sums_ref[...] = sums
        else:
            sums_ref[...] += sums


def mlp_rows(hidden_low, up0, up1, ub0, ub1, down0, down1, act_ref, slope_ref, part_ref, half_ref):
    for j, (up, ub, down) in enumerate(((up0, ub0, down0), (up1, ub1, down1))):
        act, slope = gelu_both(dot(hidden_low, up[...]) + ub[...])
        low = act.astype(BF)
        act_ref[j] = low
        slope_ref[j] = slope
        half_ref[j] = dot(low, down[...])
    part_ref[...] = (half_ref[0] + half_ref[1]).astype(BF)


def mlp_rows_back(low, slope_ref, up0, up1, down0, down1, dpre_ref, part_ref, half_ref):
    for j, (up, down) in enumerate(((up0, down0), (up1, down1))):
        d_pre = (dot_t(low, down[...]) * slope_ref[j]).astype(BF)
        dpre_ref[j] = d_pre
        half_ref[j] = dot_t(d_pre, up[...])
    part_ref[...] = (half_ref[0] + half_ref[1]).astype(BF)


def lead_mlp_body(
    message_ref, gains_ref, shifts_ref, up0, up1, ub0, ub1, down0, down1,
    resid_ref, hidden_ref, act_ref, slope_ref, part_ref, half_ref,
):
    model = resid_ref.shape[1]
    resid = message_ref[:, :model].astype(F32) + message_ref[:, model : 2 * model].astype(F32) + shifts_ref[0:1]
    resid_ref[...] = resid
    n1, _ = norm_parts(resid)
    hidden_low = (n1 * gains_ref[0:1] + shifts_ref[1:2]).astype(BF)
    hidden_ref[...] = hidden_low
    mlp_rows(hidden_low, up0, up1, ub0, ub1, down0, down1, act_ref, slope_ref, part_ref, half_ref)


def cls_attention_body(
    scalars, resid_ref, mine_ref, got_ref, sgains_ref, sshifts_ref, owner_row, owner_col, place_col, table_ref,
    own_ref, oth_ref, b_own, b_oth, wo_own, wo_oth,
    second_ref, value_ref, q_ref, k_ref, v_ref, att_ref, part_ref,
    w_ref, wo_ref,
):
    pair = q_ref.shape[1]
    pair_weights(scalars[0], own_ref, oth_ref, w_ref)
    pair_weights(scalars[0], wo_own, wo_oth, wo_ref)
    bias = pair_bias(scalars[0], b_own, b_oth)
    n1, _ = norm_parts(resid_ref[...])
    hidden = n1 * sgains_ref[0:1] + sshifts_ref[1:2]
    second = hidden + (mine_ref[...].astype(F32) + got_ref[...].astype(F32)) + sshifts_ref[2:3]
    second_ref[...] = second
    n2, _ = norm_parts(second)
    first = n2 * sgains_ref[1:2] + sshifts_ref[3:4]
    slots, places = resid_ref.shape[0], table_ref.shape[0]
    index = lax.broadcasted_iota(jnp.int32, (slots, places), 1).astype(F32)
    hot = (index == place_col[...]).astype(F32).astype(BF)
    value = first + dot(hot, table_ref[...])
    value_ref[...] = value
    low = value.astype(BF)
    q_ref[...] = (dot_t(low, w_ref[:pair]) + bias[0:1]).astype(BF)
    k_ref[...] = dot_t(low, w_ref[pair : 2 * pair]).astype(BF)
    v_ref[...] = (dot_t(low, w_ref[2 * pair :]) + bias[1:2]).astype(BF)
    allowed = owner_row[...] == owner_col[...]
    masks = head_masks(BF)
    for col in range(0, pair, LANES):
        at = slice(col, col + LANES)
        q, k, v = q_ref[:, at], k_ref[:, at], v_ref[:, at]
        tile = None
        for mask in masks:
            scores = jnp.where(allowed, dot_t(q * mask, k) * 0.125, -1000000000.0)
            one = dot(softmax(scores).astype(BF), v * mask)
            tile = one if tile is None else tile + one
        att_ref[:, at] = tile.astype(BF)
    part_ref[...] = dot(att_ref[...], wo_ref[...]).astype(BF)


def cls_mlp_body(
    value_ref, mine_ref, got_ref, gains_ref, shifts_ref, up0, up1, ub0, ub1, down0, down1,
    resid_ref, hidden_ref, act_ref, slope_ref, part_ref, half_ref,
):
    resid = value_ref[...] + (mine_ref[...].astype(F32) + got_ref[...].astype(F32)) + shifts_ref[0:1]
    resid_ref[...] = resid
    n1, _ = norm_parts(resid)
    hidden_low = (n1 * gains_ref[0:1] + shifts_ref[1:2]).astype(BF)
    hidden_ref[...] = hidden_low
    mlp_rows(hidden_low, up0, up1, ub0, ub1, down0, down1, act_ref, slope_ref, part_ref, half_ref)


def cls_mlp_back_body(
    resid_ref, mine_ref, got_ref, message_ref, slope_ref, gains_ref, shifts_ref, up0, up1, down0, down1,
    sides_ref, kept_down, came_down, kept_up, came_up,
    result_ref, dsec_ref, dpre_ref, part_ref, sums_ref, keep_down, send_down, keep_up, send_up,
    half_ref, down_ref, up_ref,
):
    add_cut(sides_ref, 2, (kept_down, came_down, keep_down, send_down, down_ref), (kept_up, came_up, keep_up, send_up, up_ref))
    n1, _ = norm_parts(resid_ref[...])
    hidden = n1 * gains_ref[0:1] + shifts_ref[1:2]
    second = hidden + (mine_ref[...].astype(F32) + got_ref[...].astype(F32)) + shifts_ref[2:3]
    n2, rstd2 = norm_parts(second)
    result_ref[...] = n2 * gains_ref[1:2] + shifts_ref[3:4]
    gy = message_ref[:, 2 * result_ref.shape[1] :].astype(F32)
    d_second = norm_back(gy, n2, rstd2, gains_ref[1:2])
    dsec_ref[...] = d_second
    mlp_rows_back(d_second.astype(BF), slope_ref, up0, up1, down0, down1, dpre_ref, part_ref, half_ref)
    sums_ref[...] = jnp.concatenate([column_sum(gy * n2), column_sum(d_second), column_sum(gy)], axis=0)


def cls_attention_back_body(
    scalars, resid_ref, mine_ref, got_ref, dsec_ref, gains_ref, q_ref, k_ref, v_ref, owner_row, owner_col,
    own_ref, oth_ref, wo_own, wo_oth,
    dres_ref, dres_low_ref, dmix_ref, part_ref, sums_ref,
    w_ref, wo_ref,
):
    pair = q_ref.shape[1]
    pair_weights(scalars[0], own_ref, oth_ref, w_ref)
    pair_weights(scalars[0], wo_own, wo_oth, wo_ref)
    n1, rstd1 = norm_parts(resid_ref[...])
    d_hidden = (mine_ref[...].astype(F32) + got_ref[...].astype(F32)) + dsec_ref[...]
    d_resid = norm_back(d_hidden, n1, rstd1, gains_ref[0:1])
    dres_ref[...] = d_resid
    low = d_resid.astype(BF)
    dres_low_ref[...] = low
    sums_ref[...] = jnp.concatenate(
        [column_sum(d_hidden * n1), column_sum(d_resid), column_sum(d_hidden)], axis=0
    )
    d_att = dot_t(low, wo_ref[...]).astype(BF)
    allowed = owner_row[...] == owner_col[...]
    masks = head_masks(BF)
    for col in range(0, pair, LANES):
        at = slice(col, col + LANES)
        q, k, v, g = q_ref[:, at], k_ref[:, at], v_ref[:, at], d_att[:, at]
        total = [None] * 3
        for mask in masks:
            qm, gm = q * mask, g * mask
            probs = softmax(jnp.where(allowed, dot_t(qm, k) * 0.125, -1000000000.0))
            d_prob = dot_t(gm, v)
            ds = (probs * (d_prob - jnp.sum(probs * d_prob, axis=-1, keepdims=True))).astype(BF)
            one = [dot(ds, k * mask), t_dot(ds, qm), t_dot(probs.astype(BF), gm)]
            total = [a if b is None else a + b for a, b in zip(one, total)]
        for j, scale in enumerate((0.125, 0.125, 1.0)):
            dmix_ref[:, j * pair + col : j * pair + col + LANES] = (total[j] * scale).astype(BF)
    part_ref[...] = dot(dmix_ref[...], w_ref[...]).astype(BF)


def lead_mlp_back_body(
    mine_ref, got_ref, dres_ref, second_ref, slope_ref, sgains_ref, place_row, up0, up1, down0, down1,
    sides_ref, kept_down, came_down, kept_up, came_up,
    dsec_ref, dsec_low_ref, dpre_ref, part_ref, sums_ref, pos_ref, keep_ref, send_ref,
    half_ref, down_ref, up_ref,
):
    cut_last(sides_ref[4], (kept_down, came_down, down_ref), (kept_up, came_up, up_ref), keep_ref, send_ref)
    gy = (mine_ref[...].astype(F32) + got_ref[...].astype(F32)) + dres_ref[...]
    n2, rstd2 = norm_parts(second_ref[...])
    d_second = norm_back(gy, n2, rstd2, sgains_ref[1:2])
    dsec_ref[...] = d_second
    low = d_second.astype(BF)
    dsec_low_ref[...] = low
    mlp_rows_back(low, slope_ref, up0, up1, down0, down1, dpre_ref, part_ref, half_ref)
    sums_ref[...] = jnp.concatenate([column_sum(gy * n2), column_sum(d_second), column_sum(gy)], axis=0)
    places, slots = pos_ref.shape[0], gy.shape[0]
    index = lax.broadcasted_iota(jnp.int32, (places, slots), 0).astype(F32)
    hot = (index == place_row[...]).astype(F32)
    pos_ref[...] = lax.dot_general(
        hot, gy, (((1,), (0,)), ((), ())), preferred_element_type=F32, precision=lax.Precision.HIGHEST
    )


def seg_attention_back_body(
    scalars, lresid_ref, lmine_ref, lgot_ref, ldsec_ref, gains_ref, wo_own, wo_oth, own_ref, oth_ref,
    q_ref, k_ref, v_ref, datt_ref, dres_ref, sums_a, sums_b, dpre_sums,
    part_ref, dres_out, dmix_ref, lsums_ref, rows_ref,
    lead_dres, lead_datt, datt_all, w_ref, wo_ref,
):
    rows, pair = q_ref.shape
    pair_weights(scalars[0], own_ref, oth_ref, w_ref)
    pair_weights(scalars[0], wo_own, wo_oth, wo_ref)
    n1, rstd1 = norm_parts(lresid_ref[...])
    d_hidden = (lmine_ref[...].astype(F32) + lgot_ref[...].astype(F32)) + ldsec_ref[...]
    d_resid = norm_back(d_hidden, n1, rstd1, gains_ref[0:1])
    lead_dres[...] = d_resid
    lead_datt[...] = dot_t(d_resid.astype(BF), wo_ref[...]).astype(BF).astype(F32)
    lsums_ref[...] = jnp.concatenate(
        [column_sum(d_hidden * n1), column_sum(d_resid), column_sum(d_hidden)], axis=0
    )
    masks = head_masks(BF)
    for row in range(0, rows, SEG):
        rs = slice(row, row + SEG)
        slot = scalars[1] + row // SEG
        dres_out[rs] = dres_ref[rs]
        dres_out[row : row + 1] = lead_dres[pl.ds(slot, 1)]
        datt_all[rs] = datt_ref[rs].astype(F32)
        datt_all[row : row + 1] = lead_datt[pl.ds(slot, 1)]
        ats = [(rs, slice(col, col + LANES)) for col in range(0, pair, LANES)]
        qs = [stacked(q_ref[at], masks) for at in ats]
        gs = [stacked(datt_all[at].astype(BF), masks) for at in ats]
        scores = [dot_t(q, k_ref[at]) * 0.125 for q, at in zip(qs, ats)]
        d_probs = [dot_t(g, v_ref[at]) for g, at in zip(gs, ats)]
        probs = [softmax(score) for score in scores]
        d_scores = [
            (p * (d - jnp.sum(p * d, axis=-1, keepdims=True))).astype(BF) for p, d in zip(probs, d_probs)
        ]
        for j, at in enumerate(ats):
            col = j * LANES
            both = jnp.concatenate([d_scores[j][:SEG], d_scores[j][SEG:]], axis=1)
            dmix_ref[rs, col : col + LANES] = (dot(both, stacked(k_ref[at], masks)) * 0.125).astype(BF)
            col += pair
            dmix_ref[rs, col : col + LANES] = (t_dot(d_scores[j], qs[j]) * 0.125).astype(BF)
            col += pair
            dmix_ref[rs, col : col + LANES] = t_dot(probs[j].astype(BF), gs[j]).astype(BF)
        if (row + SEG) % BLOCK == 0:
            at = slice(row + SEG - BLOCK, row + SEG)
            part_ref[at] = dot(dmix_ref[at], w_ref[...]).astype(BF)
    mixed = column_sum(dmix_ref[...].astype(F32))
    rows_ref[0:3] = sums_a[...]
    rows_ref[3:6] = sums_b[...]
    rows_ref[6:8] = jnp.zeros_like(rows_ref[6:8])
    rows_ref[6:7, :pair] = mixed[:, :pair]
    rows_ref[7:8, :pair] = mixed[:, 2 * pair :]
    rows_ref[8:10] = dpre_sums[...]


def attention_grads_body(
    scalars, dmix_ref, x_any, att_ref, dres_ref, kept_ref, came_ref,
    oth_a, oth_b, value_ref, own_a, own_b,
    full_ref, x_ref, x_sem,
):
    copy = own_copy(scalars, x_any, x_ref, x_sem)
    sum_body(kept_ref, came_ref, value_ref)
    core = scalars[0]
    d_mixed = dmix_ref[...]
    rows = d_mixed.shape[1]
    full_ref[rows:] = t_dot(att_ref[...], dres_ref[...].astype(BF)).astype(BF)
    copy.wait()
    full_ref[:rows] = t_dot(d_mixed, x_ref[...]).astype(BF)
    width = own_a.shape[0] // 2
    for part, (own_ref, oth_ref) in enumerate(((own_a, oth_a), (own_a, oth_a), (own_b, oth_b), (own_b, oth_b))):
        at = slice((part % 2) * width, (part % 2 + 1) * width)
        base = part * 2 * width
        own_ref[at] = full_ref[pl.ds(pl.multiple_of(base + core * width, width), width)]
        oth_ref[at] = full_ref[pl.ds(pl.multiple_of(base + (1 - core) * width, width), width)]


def two_cuts_body(at, sides_ref, a_mine, a_got, b_mine, b_got, keep_a, send_a, keep_b, send_b, a_ref, b_ref):
    add_cut(sides_ref, at, (a_mine, a_got, keep_a, send_a, a_ref), (b_mine, b_got, keep_b, send_b, b_ref))


def cut_last(side, first, second, keep_ref, send_ref):
    rows = keep_ref.shape[0] // 2
    for j, (mine, got, sum_ref) in enumerate((first, second)):
        sum_ref[...] = (mine[...].astype(F32) + got[...].astype(F32)).astype(BF)
        keep_ref[j * rows : (j + 1) * rows] = sum_ref[pl.ds(pl.multiple_of(side * rows, rows), rows)]
        send_ref[j * rows : (j + 1) * rows] = sum_ref[pl.ds(pl.multiple_of((1 - side) * rows, rows), rows)]


def last_cut_body(at, sides_ref, a_mine, a_got, b_mine, b_got, keep_ref, send_ref, a_ref, b_ref):
    cut_last(sides_ref[at], (a_mine, a_got, a_ref), (b_mine, b_got, b_ref), keep_ref, send_ref)


def sums_of(first, second, out_ref):
    rows = out_ref.shape[0] // 2
    for j, (mine, got) in enumerate((first, second)):
        out_ref[j * rows : (j + 1) * rows] = (mine[...].astype(F32) + got[...].astype(F32)).astype(BF)


def pieces_body(mine_ref, got_ref, a_ref, b_ref):
    rows = a_ref.shape[0]
    for j, out_ref in enumerate((a_ref, b_ref)):
        at = slice(j * rows, (j + 1) * rows)
        out_ref[...] = (mine_ref[at].astype(F32) + got_ref[at].astype(F32)).astype(BF)


def sums_join_body(step, sides_ref, a_mine, a_got, b_mine, b_got, c_mine, c_got, d_mine, d_got, out_ref, c_ref, d_ref):
    sums_of((a_mine, a_got), (b_mine, b_got), out_ref)
    join(sides_ref[step], c_mine, c_got, c_ref)
    join(sides_ref[step + 1], d_mine, d_got, d_ref)


def parts_join(side, mine_ref, got_ref, a_ref, b_ref):
    rows = mine_ref.shape[0] // 2
    for j, out_ref in enumerate((a_ref, b_ref)):
        out_ref[pl.ds(pl.multiple_of(side * rows, rows), rows)] = mine_ref[j * rows : (j + 1) * rows]
        out_ref[pl.ds(pl.multiple_of((1 - side) * rows, rows), rows)] = got_ref[j * rows : (j + 1) * rows]


def first_join_body(at, sides_ref, mine_ref, got_ref, a_ref, b_ref):
    parts_join(sides_ref[at], mine_ref, got_ref, a_ref, b_ref)


def cut_first_join_body(
    at, step, sides_ref, a_mine, a_got, b_mine, b_got, mine_ref, got_ref,
    keep_a, send_a, keep_b, send_b, c_ref, d_ref, a_ref, b_ref,
):
    add_cut(sides_ref, at, (a_mine, a_got, keep_a, send_a, a_ref), (b_mine, b_got, keep_b, send_b, b_ref))
    parts_join(sides_ref[step], mine_ref, got_ref, c_ref, d_ref)


def sum_body(a_ref, b_ref, out_ref):
    out_ref[...] = (a_ref[...].astype(F32) + b_ref[...].astype(F32)).astype(BF)


def join(side, a_ref, b_ref, out_ref):
    rows = a_ref.shape[0]
    out_ref[pl.ds(pl.multiple_of(side * rows, rows), rows)] = a_ref[...]
    out_ref[pl.ds(pl.multiple_of((1 - side) * rows, rows), rows)] = b_ref[...]


def two_joins_body(at, sides_ref, a_mine, a_got, b_mine, b_got, a_ref, b_ref):
    join(sides_ref[at], a_mine, a_got, a_ref)
    join(sides_ref[at + 1], b_mine, b_got, b_ref)


def attention_join_body(sides_ref, a_mine, a_got, b_mine, b_got, qkv_ref, out_ref):
    rows = a_mine.shape[0]
    for half_ref, which in ((a_mine, sides_ref[0]), (a_got, 1 - sides_ref[0])):
        qkv_ref[pl.ds(pl.multiple_of(which * rows, rows), rows)] = half_ref[...].astype(F32)
    low = sides_ref[1] == 0
    mine, got = b_mine[...].astype(F32), b_got[...].astype(F32)
    qkv_ref[2 * rows :] = jnp.where(low, mine, got)
    out_ref[...] = jnp.where(low, got, mine)


def layer_out_body(scalars, mine_ref, got_ref, result_mine, result_got, out_ref):
    step = pl.program_id(0)
    rows = out_ref.shape[0]
    steps = pl.num_programs(0) // 2
    value = jnp.where(step // steps == scalars[0], mine_ref[...].astype(F32), got_ref[...].astype(F32))
    row = lax.broadcasted_iota(jnp.int32, (rows, 1), 0)
    for j in range(rows // SEG):
        slot = scalars[2] + step * (rows // SEG) + j
        result = jnp.where(scalars[0] == 0, result_mine[pl.ds(slot, 1)], result_got[pl.ds(slot, 1)])
        value = jnp.where(row == j * SEG, result, value)
    out_ref[...] = value.astype(BF)


def tokens_grad_body(scalars, mine_ref, got_ref, out_ref):
    steps = pl.num_programs(0) // 2
    own = pl.program_id(0) // steps == scalars[0]

    @pl.when(own)
    def _():
        out_ref[...] = mine_ref[...]

    @pl.when(jnp.logical_not(own))
    def _():
        out_ref[...] = got_ref[...]


def tail_cores_body(mine_ref, got_ref, out_ref):
    out_ref[0:8] = mine_ref[0:8] + got_ref[0:8]
    out_ref[8:9] = mine_ref[8:9] + got_ref[9:10]


def finish_body(
    scalars, tail_ref, ub_ref, la_mine, lb_mine, ca_mine, cb_mine, pos_mine, la_got, lb_got, ca_got, cb_got, pos_got,
    gains_ref, shifts_ref, qv_ref, up_ref, cgains_ref, cshifts_ref, pos_ref,
):
    low = scalars[0] == 0

    def chosen(mine, got):
        return jnp.where(low, mine[...], got[...])

    def rows_of(a, b):
        return jnp.concatenate([b[0:1], a[0:1]], axis=0), jnp.concatenate([b[1:3], a[1:3]], axis=0)

    tail = tail_ref[...]
    la, lb = chosen(la_mine, la_got), chosen(lb_mine, lb_got)
    gains_ref[...], shifts_ref[...] = rows_of(tail[0:3] + la, tail[3:6] + lb)
    cgains_ref[...], cshifts_ref[...] = rows_of(chosen(ca_mine, ca_got), chosen(cb_mine, cb_got))
    pos_ref[...] = chosen(pos_mine, pos_got)
    width = qv_ref.shape[1]
    both = tail[6:8, : 2 * width]
    qv_ref[...] = jnp.where(low, both[:, :width], both[:, width:])
    up_ref[...] = tail[8:9] + ub_ref[...]


def add_rows_body(mine_ref, got_ref, dres_ref, out_ref):
    out_ref[...] = (mine_ref[...].astype(F32) + got_ref[...].astype(F32)) + dres_ref[...]


def cls_grads_body(
    scalars, mix_ref, low_ref, att_ref, dres_ref, hidden_ref, dpre_ref, act_ref, dsec_ref,
    qkv_out, bias_out, out_out, up_out, ub_out, down_out,
    full_ref,
):
    core = scalars[0]
    width = out_out.shape[0]
    pair = 2 * width

    def own(base):
        return full_ref[pl.ds(pl.multiple_of(base + core * width, width), width)]

    full_ref[...] = t_dot(mix_ref[...], low_ref[...].astype(BF))
    for part in range(3):
        qkv_out[part * width : (part + 1) * width] = own(part * pair)
    full_ref[:pair] = t_dot(att_ref[...], dres_ref[...])
    out_out[...] = own(0)
    sums = column_sum(mix_ref[...].astype(F32))
    for row, base in enumerate((0, 2 * pair)):
        bias_out[row : row + 1] = jnp.where(core == 0, sums[:, base : base + width], sums[:, base + width : base + pair])
    up_out[...] = t_dot(hidden_ref[...], dpre_ref[0])
    ub_out[...] = column_sum(dpre_ref[0].astype(F32))
    down_out[...] = t_dot(act_ref[0], dsec_ref[...].astype(BF))


def add_grads_body(sides_ref, hidden_ref, dpre_ref, act_ref, dsec_ref, down_a, down_b, up_a, up_b,
                   down_out, up_out, ub_out):
    for j, (a_ref, b_ref, out_ref) in enumerate(((down_a, down_b, down_out), (up_a, up_b, up_out))):
        rows = a_ref.shape[0]
        side = sides_ref[j]
        if j == 0:
            out_ref[...] = t_dot(act_ref[0], dsec_ref[...])
        else:
            out_ref[...] = t_dot(hidden_ref[...], dpre_ref[0])
        at = pl.ds(pl.multiple_of(side * rows, rows), rows)
        out_ref[at] = out_ref[at] + a_ref[...].astype(F32)
        at = pl.ds(pl.multiple_of((1 - side) * rows, rows), rows)
        out_ref[at] = out_ref[at] + b_ref[...].astype(F32)
    ub_out[...] = column_sum(dpre_ref[0].astype(F32))


def make_shards(n_dp):
    core_pairs = [(i, i ^ 1) for i in range(4)]
    x_pairs = [(i, i ^ 2) for i in range(4)]
    bits = [1 << k for k in range(n_dp.bit_length() - 1)]
    swapped = [bits[1], bits[0], *bits[2:]]

    def core_swap(value):
        return lax.ppermute(value, "mp", core_pairs)

    def x_swap(value):
        return lax.ppermute(value, "mp", x_pairs)

    def dp_swap(value, bit):
        return lax.ppermute(value, "dp", [(i, i ^ bit) for i in range(n_dp)])

    def shards(
        tokens,
        seg_counts,
        seg_order,
        seg_qkv,
        seg_qv_bias,
        seg_out,
        seg_up,
        seg_up_bias,
        seg_down,
        seg_gains,
        seg_shifts,
        cls_qkv,
        cls_qv_bias,
        cls_out,
        cls_up,
        cls_up_bias,
        cls_down,
        cls_gains,
        cls_shifts,
        pos_table,
        cotangent,
    ):
        outer = Outer()

        def run(*args, **options):
            if slots > 64:
                options["vmem"] = 56
            return call(outer, *args, **options)

        def tied(value, *others):
            result = tie(value, *others)
            if value in outer:
                outer.add(result)
            return result

        core = lax.axis_index("mp") % 2
        dp_index = lax.axis_index("dp")
        rows = tokens.shape[0] // 2
        own_segs = rows // SEG
        slots = seg_order.shape[0]
        width = seg_qkv.shape[2]
        pair = 2 * width
        model = tokens.shape[1]
        ff = seg_down.shape[0]
        places = pos_table.shape[0]

        def ordered(low_side, mine, other, axis):
            return jnp.where(
                low_side,
                jnp.concatenate([mine, other], axis=axis),
                jnp.concatenate([other, mine], axis=axis),
            )

        def paired(value, axis):
            return ordered(core == 0, value, core_swap(value), axis)

        def gather_slots(value, last_after):
            value = paired(value, 0)
            for bit in bits:
                if bit == bits[1]:
                    before = value
                    value = tied(value, last_after)
                value = ordered((dp_index & bit) == 0, value, dp_swap(value, bit), 0)
            return value, before

        def half(value, which, axis):
            size = value.shape[axis] // 2
            return lax.dynamic_slice_in_dim(value, which * size, size, axis)

        def own_half(value, axis):
            return half(value, core, axis)

        def side_of(bit):
            return jnp.where((dp_index & bit) == 0, 0, 1).astype(jnp.int32).reshape(1)

        def two_cuts(step, a, a_got, b, b_got):
            size = a.shape[0] // 2
            if size % 16 == 0:
                return run(
                    functools.partial(two_cuts_body, 2 * step),
                    [((size, model), BF)] * 4,
                    (sides, a, a_got, b, b_got),
                    "two_cuts",
                    far=(0, 2),
                    scratch=[pltpu.VMEM(a.shape, BF), pltpu.VMEM(b.shape, BF)],
                )
            out = []
            for mine, got, bit in ((a, a_got, bits[step]), (b, b_got, swapped[step])):
                value = (mine.astype(F32) + got.astype(F32)).astype(BF)
                side = side_of(bit)[0]
                out += [half(value, side, 0), half(value, 1 - side, 0)]
            return out

        last = len(bits) - 1

        def last_cut(a, a_got, b, b_got):
            size = a.shape[0] // 2
            if size % 16 == 0:
                return run(
                    functools.partial(last_cut_body, 2 * last),
                    [((2 * size, model), BF)] * 2,
                    (sides, a, a_got, b, b_got),
                    "last_cut",
                    far=(0,),
                    scratch=[pltpu.VMEM(a.shape, BF), pltpu.VMEM(b.shape, BF)],
                )
            keep_a, send_a, keep_b, send_b = two_cuts(last, a, a_got, b, b_got)
            return jnp.concatenate([keep_a, keep_b], axis=0), jnp.concatenate([send_a, send_b], axis=0)

        def last_sum(keep, send):
            return run(sum_body, [(keep.shape, BF)], (keep, dp_swap(send, bits[-1])), "last_sum")[0]

        def pieces_of(a, a_got, b, b_got):
            parts = [(mine.astype(F32) + got.astype(F32)).astype(BF) for mine, got in ((a, a_got), (b, b_got))]
            return jnp.concatenate(parts, axis=0)

        def last_sums(pieces, got):
            rows = pieces.shape[0] // 2
            if rows % 16 == 0:
                return run(pieces_body, [((rows, model), BF)] * 2, (pieces, got), "last_sums")
            value = (pieces.astype(F32) + got.astype(F32)).astype(BF)
            return value[:rows], value[rows:]

        def first_join(value, got):
            rows = value.shape[0] // 2
            if rows % 16 == 0:
                return run(
                    functools.partial(first_join_body, 2 * last),
                    [((2 * rows, model), BF)] * 2,
                    (sides, value, got),
                    "first_join",
                )
            low = (dp_index & bits[-1]) == 0
            return ordered(low, value[:rows], got[:rows], 0), ordered(low, value[rows:], got[rows:], 0)

        def two_joins(step, a, a_got, b, b_got):
            if a.shape[0] % 16 == 0:
                return run(
                    functools.partial(two_joins_body, 2 * step),
                    [((2 * a.shape[0], model), BF), ((2 * b.shape[0], model), BF)],
                    (sides, a, a_got, b, b_got),
                    "two_joins",
                )
            return (
                ordered((dp_index & bits[step]) == 0, a, a_got, 0),
                ordered((dp_index & swapped[step]) == 0, b, b_got, 0),
            )

        sides = jnp.concatenate([side_of(bit) for two in zip(bits, swapped) for bit in two])
        outer.add(seg_gains, seg_shifts, cls_gains, cls_shifts, pos_table)
        scalars = jnp.stack([core, (dp_index * 2 + core) * own_segs, dp_index * 2 * own_segs]).astype(jnp.int32)

        def weights(qkv, qv_bias, out, up, up_bias, down):
            flat = jnp.transpose(qkv, (1, 2, 0))
            bias = up_bias.reshape(1, ff)
            outs = out.reshape(1, width, model)
            heads = (flat, core_swap(flat), qv_bias, core_swap(qv_bias), outs, core_swap(outs))
            hidden = (up, core_swap(up), down, core_swap(down), bias, core_swap(bias))
            outer.add(heads[0], heads[4], *hidden)
            return heads, hidden

        s_heads, (s_up0, s_up1, s_down0, s_down1, *s_ub) = weights(
            seg_qkv, seg_qv_bias, seg_out, seg_up, seg_up_bias, seg_down
        )
        c_heads, (c_up0, c_up1, c_down0, c_down1, *c_ub) = weights(
            cls_qkv, cls_qv_bias, cls_out, cls_up, cls_up_bias, cls_down
        )

        c_swapped = (c_heads[1], c_heads[3], c_heads[5], c_up1, c_down1, c_ub[1])
        part1, lead_part, lead_rest, q, k, v, att = run(
            seg_attention_body,
            [((rows, model), BF), ((own_segs, model), F32), ((own_segs, 2 * model), F32)]
            + [((rows, pair), BF)] * 4,
            (scalars, tokens, cotangent, tied(s_heads[0], s_ub[1]), *s_heads[1:]),
            "seg_attention",
            far=(0, 3, 4, 5, 6),
            scratch=[
                pltpu.VMEM((3 * pair, model), BF),
                pltpu.VMEM((pair, model), BF),
                pltpu.VMEM((rows, model), BF),
                pltpu.VMEM((own_segs, 16, model), BF),
                pltpu.SemaphoreType.DMA,
                pltpu.SemaphoreType.DMA((own_segs,)),
            ],
            vmem=18,
            stay=(1, 2),
        )
        lead_sum = lead_part + x_swap(lead_part)
        got1 = x_swap(part1)
        message, before_last = gather_slots(jnp.concatenate([lead_sum.astype(BF), lead_rest.astype(BF)], axis=1), got1)

        owner_row, owner_col, place_row, place_col = run(
            layout_body,
            [((1, slots), F32), ((slots, 1), F32), ((1, slots), F32), ((slots, 1), F32)],
            (seg_counts.reshape(1, -1), seg_order.reshape(1, -1)),
            "layout",
            far=(0, 1, 2, 3),
        )
        mlp_weights = (s_up0, s_up1, s_down0, s_down1)
        l_resid, l_hidden, l_act, l_slope, l_part = run(
            lead_mlp_body,
            [((slots, model), F32), ((slots, model), BF), ((2, slots, ff), BF), ((2, slots, ff), F32),
             ((slots, model), BF)],
            (tied(message, owner_row, *c_swapped), seg_gains, seg_shifts, s_up0, s_up1, *s_ub, s_down0, s_down1),
            "lead_mlp",
            far=(0, 1, 2, 3),
            scratch=[pltpu.VMEM((2, slots, model), F32)],
        )
        got_l1 = x_swap(l_part)

        part2, resid, act, slope = run(
            seg_mlp_body,
            [((rows, model), BF), ((rows, model), F32), ((rows, 2 * ff), BF), ((rows, 2 * ff), F32)],
            (scalars, tokens, tied(part1, before_last), got1, seg_gains, seg_shifts, s_up0, s_up1, *s_ub, s_down0, s_down1),
            "seg_mlp",
            far=(0, 1, 2, 3),
            scratch=[pltpu.VMEM((rows, model), BF), pltpu.SemaphoreType.DMA],
            stay=(1,),
            vmem=18,
        )
        l_second, c_value, c_q, c_k, c_v, c_att, c_part1 = run(
            cls_attention_body,
            [((slots, model), F32)] * 2
            + [((slots, pair), BF)] * 4
            + [((slots, model), BF)],
            (scalars, l_resid, l_part, got_l1, seg_gains, seg_shifts, owner_row, owner_col, place_col,
             pos_table, *c_heads),
            "cls_attention",
            far=(0, 1, 2, 3, 4, 5),
            scratch=[pltpu.VMEM((3 * pair, model), BF), pltpu.VMEM((pair, model), BF)],
        )
        got2 = x_swap(part2)
        outer.add(got2)
        d_second_low, hidden_low, d_pre, first_low, d_second, part3, sums_a, d_pre_sum, down_oth, up_oth = run(
            seg_mlp_back_body,
            [((rows, model), BF), ((rows, model), BF), ((rows, 2 * ff), BF), ((rows, model), BF),
             ((rows, model), F32), ((rows, model), BF), ((3, model), F32), ((2, ff), F32),
             ((ff, model), BF), ((model, ff), BF)],
            (scalars, resid, tied(part2, l_part), got2, cotangent, slope, tied(act, got_l1), seg_gains,
             seg_shifts, *mlp_weights),
            "seg_mlp_back",
            far=(0, 1, 2, 3, 4, 5, 6, 7),
            scratch=[pltpu.VMEM((rows, model), BF), pltpu.SemaphoreType.DMA],
            stay=(4,),
            vmem=24,
        )
        got3 = x_swap(part3)
        keep_down, send_down, keep_up, send_up = run(
            own_mlp_grads_body,
            [((ff // 2, model), BF)] * 2 + [((model // 2, ff), BF)] * 2,
            (sides, tied(act, c_part1), d_second_low, hidden_low, d_pre, core_swap(down_oth), core_swap(up_oth)),
            "seg_own_mlp_grads",
            far=(0, 2),
            scratch=[pltpu.VMEM((ff, model), BF), pltpu.VMEM((model, ff), BF)],
        )
        got_c1 = tied(x_swap(c_part1), send_down, send_up, got3)
        c_resid, c_hidden, c_act, c_slope, c_part2 = run(
            cls_mlp_body,
            [((slots, model), F32), ((slots, model), BF), ((2, slots, ff), BF), ((2, slots, ff), F32),
             ((slots, model), BF)],
            (c_value, c_part1, got_c1, cls_gains, cls_shifts, c_up0, c_up1, *c_ub, c_down0, c_down1),
            "cls_mlp",
            far=(0, 1, 2, 3),
            scratch=[pltpu.VMEM((2, slots, model), F32)],
        )

        quarter = ff // 4
        c_result, c_d_second, c_d_pre, c_part3, c_sums_a, keep_down, send_down, keep_up, send_up = run(
            cls_mlp_back_body,
            [((slots, model), F32), ((slots, model), F32), ((2, slots, ff), BF), ((slots, model), BF),
             ((3, model), F32)] + [((quarter, model), BF)] * 4,
            (c_resid, c_part2, x_swap(c_part2), message, c_slope, cls_gains, cls_shifts, c_up0, c_up1, c_down0, c_down1,
             sides, keep_down, dp_swap(send_down, bits[0]), keep_up, dp_swap(send_up, swapped[0])),
            "cls_mlp_back",
            far=(0, 1, 2, 4, 5, 7),
            scratch=[pltpu.VMEM((2, slots, model), F32)] + [pltpu.VMEM((2 * quarter, model), BF)] * 2,
        )
        c_d_resid, c_d_resid_low, c_d_mixed, c_part4, c_sums_b = run(
            cls_attention_back_body,
            [((slots, model), F32), ((slots, model), BF), ((slots, 3 * pair), BF), ((slots, model), BF),
             ((3, model), F32)],
            (scalars, c_resid, c_part3, x_swap(c_part3), c_d_second, cls_gains, c_q, c_k, c_v,
             owner_row, owner_col, c_heads[0], c_heads[1], c_heads[4], c_heads[5]),
            "cls_attention_back",
            far=(0, 1, 2, 4),
            scratch=[pltpu.VMEM((3 * pair, model), BF), pltpu.VMEM((pair, model), BF)],
        )

        for step in range(2, last):
            keep_down, send_down, keep_up, send_up = two_cuts(
                step, keep_down, dp_swap(send_down, bits[step - 1]), keep_up, dp_swap(send_up, swapped[step - 1])
            )
        fused = last == 2
        kept = (keep_down, dp_swap(send_down, bits[last - 1]), keep_up, dp_swap(send_up, swapped[last - 1]))
        if not fused:
            keep_mlp, send_mlp = last_cut(*kept)
            kept = (down_oth[:32], down_oth[:32], down_oth[:32], down_oth[:32])
        eighth = kept[0].shape[0] // 2
        l_d_second, l_d_second_low, l_d_pre, l_part3, l_sums_a, pos_grad, *cuts = run(
            lead_mlp_back_body,
            [((slots, model), F32), ((slots, model), BF), ((2, slots, ff), BF), ((slots, model), BF),
             ((3, model), F32), ((places, model), F32)] + [((2 * eighth, model), BF)] * 2,
            (c_part4, x_swap(c_part4), c_d_resid, l_second, l_slope, seg_gains, place_row,
             *mlp_weights, sides, *kept),
            "lead_mlp_back",
            far=(0, 1, 2, 4, 5, 6),
            scratch=[pltpu.VMEM((2, slots, model), F32)] + [pltpu.VMEM((2 * eighth, model), BF)] * 2,
        )
        if fused:
            keep_mlp, send_mlp = cuts
        d_resid, d_att, sums_b = run(
            seg_out_back_body,
            [((rows, model), F32), ((rows, pair), BF), ((3, model), F32)],
            (scalars, resid, part3, tied(got3, l_part3), d_second, seg_gains, s_heads[4], s_heads[5]),
            "seg_out_back",
            far=(2,),
            scratch=[pltpu.VMEM((pair, model), BF)],
        )
        part4, d_resid, d_mixed, l_sums_b, tail = run(
            seg_attention_back_body,
            [((rows, model), BF), ((rows, model), F32), ((rows, 3 * pair), BF), ((3, model), F32), ((10, model), F32)],
            (scalars, l_resid, l_part3, x_swap(l_part3), l_d_second, seg_gains, s_heads[4], s_heads[5],
             s_heads[0], s_heads[1], q, k, v, d_att, d_resid, sums_a, sums_b, d_pre_sum),
            "seg_attention_back",
            far=(1, 3),
            scratch=[
                pltpu.VMEM((slots, model), F32),
                pltpu.VMEM((slots, pair), F32),
                pltpu.VMEM((rows, pair), F32),
                pltpu.VMEM((3 * pair, model), BF),
                pltpu.VMEM((pair, model), BF),
            ],
            vmem=18,
        )
        got4 = x_swap(part4)
        tail = run(tail_cores_body, [((9, model), F32)], (tail, core_swap(tail)), "tail_cores")[0]
        tails = [tail]
        for bit in bits:
            tails.append(tails[-1] + dp_swap(tails[-1], bit))
        tail = tails[-1]
        oth_a, oth_b, value_mlp, own_a, own_b = run(
            attention_grads_body,
            [((2 * width, model), BF)] * 2 + [(keep_mlp.shape, BF)] + [((2 * width, model), BF)] * 2,
            (scalars, d_mixed, tokens, att, d_resid, keep_mlp, dp_swap(send_mlp, bits[-1])),
            "seg_attention_grads",
            far=(3, 4),
            scratch=[pltpu.VMEM((8 * width, model), BF), pltpu.VMEM((rows, model), BF), pltpu.SemaphoreType.DMA],
            stay=(2,),
        )
        keep_a, send_a, keep_b, send_b = two_cuts(0, own_a, core_swap(oth_a), own_b, core_swap(oth_b))
        got_mlp = dp_swap(value_mlp, bits[-1])
        cg_qkv, cg_bias, cg_out, cg_up, cg_ub, cg_down = run(
            cls_grads_body,
            [((3 * width, model), F32), ((2, width), F32), ((width, model), F32), ((model, ff), F32),
             ((1, ff), F32), ((ff, model), F32)],
            (scalars, tied(c_d_mixed, send_a, send_b), c_value, c_att, c_d_resid_low, c_hidden, c_d_pre, c_act, c_d_second),
            "cls_grads",
            scratch=[pltpu.VMEM((3 * pair, model), F32)],
        )
        layer_out = call_blocks(
            layer_out_body,
            [((2 * rows, model), BF)],
            scalars,
            (tied(first_low, send_a, send_b), core_swap(first_low), c_result, core_swap(c_result)),
            "layer_out",
            2 * rows // BLOCK,
            BLOCK,
            "mmww",
        )[0]
        for step in range(last):
            if step > 0:
                if fused:
                    keep_a, send_a, keep_b, send_b, down, up = run(
                        functools.partial(cut_first_join_body, 2 * step, 2 * last),
                        [((width // 2, model), BF)] * 4 + [(value_mlp.shape, BF)] * 2,
                        (sides, *a_next, *b_next, value_mlp, got_mlp),
                        "cut_first_join",
                        far=(0, 2),
                        scratch=[pltpu.VMEM((width, model), BF)] * 2,
                    )
                else:
                    keep_a, send_a, keep_b, send_b = two_cuts(step, *a_next, *b_next)
            if step == 1:
                d_rows = run(add_rows_body, [((rows, model), F32)], (part4, tied(got4, send_a, send_b), d_resid), "add_rows")[0]
                tokens_grad = call_blocks(
                    tokens_grad_body,
                    [((2 * rows, model), F32)],
                    scalars,
                    (d_rows, core_swap(d_rows)),
                    "tokens_grad",
                    2 * rows // BLOCK,
                    BLOCK,
                    "mm",
                )[0]
            others = [tails[step]] + ([cg_bias, layer_out] if step == 0 else [])
            got_a, got_b = dp_swap(send_a, bits[step]), dp_swap(send_b, swapped[step])
            a_next, b_next = (keep_a, tied(got_a, *others)), (keep_b, got_b)
        if fused:
            size = a_next[0].shape[0]
            pieces, down, up = run(
                functools.partial(sums_join_body, 2),
                [((2 * size, model), BF)] + [((2 * down.shape[0], model), BF)] * 2,
                (sides, *a_next, *b_next, down, dp_swap(down, bits[1]), up, dp_swap(up, swapped[1])),
                "sums_join",
            )
        else:
            pieces = pieces_of(*a_next, *b_next)
            down, up = first_join(value_mlp, got_mlp)
            for at in range(last - 1, 0, -1):
                down, up = two_joins(at, down, dp_swap(down, bits[at]), up, dp_swap(up, swapped[at]))
        grad_down, grad_up, l_up_bias = run(
            add_grads_body,
            [((ff, model), F32), ((model, ff), F32), ((1, ff), F32)],
            (sides, l_hidden, l_d_pre, l_act, l_d_second_low,
             down, dp_swap(down, bits[0]), up, dp_swap(up, swapped[0])),
            "seg_add_grads",
        )
        value_a, value_b = last_sums(pieces, tied(dp_swap(pieces, bits[-1]), tokens_grad))
        for step in range(last - 1, 0, -1):
            got_a, got_b = dp_swap(value_a, bits[step]), dp_swap(value_b, swapped[step])
            if step == 1:
                got_a = tied(got_a, l_up_bias, tails[2])
            value_a, value_b = two_joins(step, value_a, got_a, value_b, got_b)
        a_parts = (value_a, dp_swap(value_a, bits[0]))
        b_parts = (value_b, dp_swap(value_b, swapped[0]))
        lead_sums = (l_sums_a, l_sums_b, c_sums_a, c_sums_b, pos_grad)
        m_gains, m_shifts, qv_total, up_total, cls_gains_grad, cls_shifts_grad, pos_grad = run(
            finish_body,
            [((2, model), F32), ((4, model), F32), ((2, width), F32), ((1, ff), F32), ((2, model), F32),
             ((4, model), F32), ((places, model), F32)],
            (scalars, tail, l_up_bias, *lead_sums, *[core_swap(part) for part in lead_sums]),
            "finish",
        )

        g_qkv, g_out = run(
            attention_join_body,
            [((3 * width, model), F32), ((width, model), F32)],
            (sides, tied(a_parts[0], m_gains), a_parts[1], *b_parts),
            "seg_attention_join",
        )
        def unflatten(flat):
            return jnp.transpose(flat.reshape(3, width, model), (2, 0, 1))

        seg_grads = (
            unflatten(g_qkv),
            qv_total,
            g_out,
            grad_up,
            up_total[0],
            grad_down,
            m_gains,
            m_shifts,
        )
        cls_grads = (
            unflatten(cg_qkv),
            cg_bias,
            cg_out,
            cg_up,
            cg_ub[0],
            cg_down,
            cls_gains_grad,
            cls_shifts_grad,
        )
        return (layer_out, tokens_grad, *seg_grads, *cls_grads, pos_grad)

    return shards


def solution(mesh):
    in_specs = (
        P("dp", None),
        P(),
        P(),
        P(None, None, "mp"),
        P(None, "mp"),
        P("mp", None),
        P(None, "mp"),
        P("mp"),
        P("mp", None),
        P(),
        P(),
        P(None, None, "mp"),
        P(None, "mp"),
        P("mp", None),
        P(None, "mp"),
        P("mp"),
        P("mp", None),
        P(),
        P(),
        P(),
        P("dp", None),
    )
    out_specs = (
        P("dp", None),
        P("dp", None),
        P(None, None, "mp"),
        P(None, "mp"),
        P("mp", None),
        P(None, "mp"),
        P("mp"),
        P("mp", None),
        P(),
        P(),
        P(None, None, "mp"),
        P(None, "mp"),
        P("mp", None),
        P(None, "mp"),
        P("mp"),
        P("mp", None),
        P(),
        P(),
        P(),
    )
    return jax.shard_map(
        make_shards(mesh.shape["dp"]), mesh=mesh, in_specs=in_specs, out_specs=out_specs, check_vma=False
    )
```

```python
import functools

import jax
import jax.numpy as jnp
from jax import lax
from jax.experimental import pallas as pl
from jax.experimental.pallas import tpu as pltpu
from jax.sharding import PartitionSpec as P

HEAD = 64
SEG = 128
LANES = 128
EPSILON = 1e-05
BF = jnp.bfloat16
F32 = jnp.float32


def dot(a, b):
    return lax.dot_general(a, b, (((1,), (0,)), ((), ())), preferred_element_type=F32)


def dot_t(a, b):
    return lax.dot_general(a, b, (((1,), (1,)), ((), ())), preferred_element_type=F32)


def t_dot(a, b):
    return lax.dot_general(a, b, (((0,), (0,)), ((), ())), preferred_element_type=F32)


def norm_parts(value):
    center = value - jnp.mean(value, axis=-1, keepdims=True)
    rstd = lax.rsqrt(jnp.mean(center * center, axis=-1, keepdims=True) + EPSILON)
    return center * rstd, rstd


def norm_back(grad, normed, rstd, gain):
    gy = grad * gain
    return rstd * (
        gy
        - jnp.mean(gy, axis=-1, keepdims=True)
        - normed * jnp.mean(gy * normed, axis=-1, keepdims=True)
    )


def gelu_both(pre):
    cdf = 0.5 * (1.0 + lax.erf(pre * 0.7071067811865476))
    pdf = 0.3989422804014327 * jnp.exp(-0.5 * pre * pre)
    return pre * cdf, cdf + pre * pdf


def column_sum(value):
    return jnp.sum(value, axis=0, keepdims=True)


def softmax(scores):
    powers = jnp.exp(scores - jnp.max(scores, axis=-1, keepdims=True))
    return powers * (1.0 / jnp.sum(powers, axis=-1, keepdims=True))


def head_masks(dtype):
    lane = lax.broadcasted_iota(jnp.int32, (1, LANES), 1)
    return [(lane < HEAD).astype(F32).astype(dtype), (lane >= HEAD).astype(F32).astype(dtype)]


def stacked(tile, masks):
    return jnp.concatenate([tile * masks[0], tile * masks[1]], axis=0)


class Outer:
    def __init__(self):
        self.held = {}

    def add(self, *values):
        for value in values:
            self.held[id(value)] = value
        return values

    def __contains__(self, value):
        return self.held.get(id(value)) is value


def call(outer, body, outs, args, name, far=(), scratch=(), vmem=16, stay=()):
    def spec(i, a):
        if i in stay:
            return pl.BlockSpec(memory_space=pltpu.HBM)
        return pl.BlockSpec(memory_space=pltpu.SMEM if a.dtype == jnp.int32 and a.ndim == 1 else pltpu.VMEM)

    results = pl.pallas_call(
        body,
        out_shape=tuple(
            pltpu.HBM(s, d) if i in far else jax.ShapeDtypeStruct(s, d) for i, (s, d) in enumerate(outs)
        ),
        in_specs=[spec(i, a) for i, a in enumerate(args)],
        out_specs=tuple(pl.BlockSpec(memory_space=pltpu.VMEM) for _ in outs),
        scratch_shapes=list(scratch),
        compiler_params=pltpu.CompilerParams(vmem_limit_bytes=vmem * 1024 * 1024),
        name=name,
    )(*[pltpu.with_memory_space_constraint(a, pltpu.HBM) if i in stay or a in outer else a for i, a in enumerate(args)])
    outer.add(*[result for i, result in enumerate(results) if i in far])
    return results


def call_blocks(body, outs, scalars, args, name, grid, rows, kinds, vmem=14):
    def spec(shape, kind):
        if kind == "w":
            return pl.BlockSpec(shape, lambda i, scalars: (0,) * len(shape))
        steps = shape[0] // rows
        return pl.BlockSpec((rows, *shape[1:]), lambda i, scalars: (i % steps, 0))

    return pl.pallas_call(
        body,
        out_shape=tuple(jax.ShapeDtypeStruct(s, d) for s, d in outs),
        grid_spec=pltpu.PrefetchScalarGridSpec(
            num_scalar_prefetch=1,
            grid=(grid,),
            in_specs=[spec(a.shape, k) for k, a in zip(kinds, args, strict=True)],
            out_specs=tuple(spec(s, "m") for s, _ in outs),
        ),
        compiler_params=pltpu.CompilerParams(vmem_limit_bytes=vmem * 1024 * 1024),
        name=name,
    )(scalars, *args)


def tie(value, *others):
    return lax.optimization_barrier((value, *others))[0]


BLOCK = 256


def blocks_of(rows):
    return [slice(at, at + BLOCK) for at in range(0, rows, BLOCK)]


def layout_body(counts_ref, order_ref, owner_row, owner_col, place_row, place_col):
    docs, slots = counts_ref.shape[1], order_ref.shape[1]
    counts = counts_ref[...].astype(F32)
    order = order_ref[...].astype(F32)

    def iotas(a, b):
        return [lax.broadcasted_iota(jnp.int32, (a, b), d).astype(F32) for d in (0, 1)]

    def to_column(row):
        size = row.shape[1]
        r, c = iotas(size, size)
        return jnp.sum(jnp.where(r == c, row, 0.0), axis=1, keepdims=True)

    def to_row(col):
        size = col.shape[0]
        r, c = iotas(size, size)
        return column_sum(jnp.where(r == c, col, 0.0))

    def total(row):
        return jnp.sum(row, axis=1, keepdims=True)

    r, c = iotas(docs, docs)
    ends_col = jnp.sum(jnp.where(c <= r, counts, 0.0), axis=1, keepdims=True)
    ends_row = to_row(ends_col)
    starts_col = ends_col - to_column(counts)
    starts_row = ends_row - counts
    index = lax.broadcasted_iota(jnp.int32, (1, docs), 1).astype(F32)
    top = jnp.max(counts, axis=1, keepdims=True)
    longest = jnp.min(jnp.where(counts == top, index, float(docs)), axis=1, keepdims=True)
    lead = total(jnp.where(index == longest, starts_row, 0.0))
    trail = total(jnp.where(index == longest, ends_row, 0.0)) - 1.0
    slot = lax.broadcasted_iota(jnp.int32, (1, slots), 1).astype(F32)
    head = total(jnp.where(slot == 0.0, order, 0.0))
    held = jnp.where(slot == 0.0, lead, jnp.where(order == lead, head, order))
    last = total(jnp.where(slot == slots - 1.0, held, 0.0))
    held = jnp.where(slot == slots - 1.0, trail, jnp.where(held == trail, last, held))
    owner = column_sum((held >= ends_col).astype(F32))
    r, _ = iotas(docs, slots)
    start = column_sum(jnp.where(r == owner, starts_col, 0.0))
    place = held - start
    owner_row[...] = owner
    owner_col[...] = to_column(owner)
    place_row[...] = place
    place_col[...] = to_column(place)


def pair_weights(core, own_ref, oth_ref, w_ref):
    parts, width = own_ref.shape[0], own_ref.shape[1]
    for part in range(parts):
        base = part * 2 * width
        w_ref[pl.ds(pl.multiple_of(base + core * width, width), width)] = own_ref[part]
        w_ref[pl.ds(pl.multiple_of(base + (1 - core) * width, width), width)] = oth_ref[part]


def pair_bias(core, own_ref, oth_ref):
    own, oth = own_ref[...], oth_ref[...]
    low = jnp.where(core == 0, own, oth)
    return jnp.concatenate([low, jnp.where(core == 0, oth, own)], axis=1)


def seg_attention_body(
    scalars, x_any, cot_any, own_ref, oth_ref, b_own, b_oth, wo_own, wo_oth,
    part_ref, lead_ref, rest_ref, q_ref, k_ref, v_ref, att_ref,
    w_ref, wo_ref, x_ref, cot_ref, x_sem, cot_sem,
):
    rows, pair = q_ref.shape
    model = x_any.shape[1]
    segs, packed = cot_ref.shape[0], cot_ref.shape[1]
    base = pl.multiple_of(scalars[0] * rows, rows)
    x_copy = pltpu.make_async_copy(x_any.at[pl.ds(base, rows)], x_ref, x_sem)
    x_copy.start()
    cot_copies = [
        pltpu.make_async_copy(cot_any.at[pl.ds(base + j * SEG, packed)], cot_ref.at[j], cot_sem.at[j])
        for j in range(segs)
    ]
    for copy in cot_copies:
        copy.start()
    pair_weights(scalars[0], own_ref, oth_ref, w_ref)
    pair_weights(scalars[0], wo_own, wo_oth, wo_ref)
    bias = pair_bias(scalars[0], b_own, b_oth)
    masks = head_masks(BF)
    x_copy.wait()
    for rs in blocks_of(rows):
        x = x_ref[rs]
        q_ref[rs] = (dot_t(x, w_ref[:pair]) + bias[0:1]).astype(BF)
        k_ref[rs] = dot_t(x, w_ref[pair : 2 * pair]).astype(BF)
        v_ref[rs] = (dot_t(x, w_ref[2 * pair :]) + bias[1:2]).astype(BF)
        for row in range(rs.start, rs.stop, SEG):
            ats = [(slice(row, row + SEG), slice(col, col + LANES)) for col in range(0, pair, LANES)]
            scores = [dot_t(stacked(q_ref[at], masks), k_ref[at]) * 0.125 for at in ats]
            probs = [softmax(score).astype(BF) for score in scores]
            both = [jnp.concatenate([p[:SEG], p[SEG:]], axis=1) for p in probs]
            for at, weight in zip(ats, both):
                att_ref[at] = dot(weight, stacked(v_ref[at], masks)).astype(BF)
        part = dot(att_ref[rs], wo_ref[...])
        part_ref[rs] = part.astype(BF)
        for row in range(0, BLOCK, SEG):
            j = (rs.start + row) // SEG
            lead_ref[j : j + 1] = part[row : row + 1]
            rest_ref[j : j + 1, :model] = x[row : row + 1].astype(F32)
    for j, copy in enumerate(cot_copies):
        copy.wait()
        rest_ref[j : j + 1, model:] = cot_ref[j, 0:1].astype(F32)


def own_copy(scalars, source, target, sem):
    rows = target.shape[0]
    copy = pltpu.make_async_copy(source.at[pl.ds(pl.multiple_of(scalars[0] * rows, rows), rows)], target, sem)
    copy.start()
    return copy


def seg_mlp_body(
    scalars, x_any, mine_ref, got_ref, gains_ref, shifts_ref, up0, up1, ub0, ub1, down0, down1,
    part_ref, resid_ref, act_ref, slope_ref,
    x_ref, x_sem,
):
    own_copy(scalars, x_any, x_ref, x_sem).wait()
    for rs in blocks_of(resid_ref.shape[0]):
        branch = mine_ref[rs].astype(F32) + got_ref[rs].astype(F32)
        resid = x_ref[rs].astype(F32) + branch + shifts_ref[0:1]
        resid_ref[rs] = resid
        normed, _ = norm_parts(resid)
        hidden_low = (normed * gains_ref[0:1] + shifts_ref[1:2]).astype(BF)
        parts = []
        for j, (up, ub, down) in enumerate(((up0, ub0, down0), (up1, ub1, down1))):
            at = (rs, slice(j * up.shape[1], (j + 1) * up.shape[1]))
            act, slope = gelu_both(dot(hidden_low, up[...]) + ub[...])
            low = act.astype(BF)
            act_ref[at] = low
            slope_ref[at] = slope
            parts.append(dot(low, down[...]))
        part_ref[rs] = (parts[0] + parts[1]).astype(BF)


def seg_mlp_back_body(
    scalars, resid_ref, mine_ref, got_ref, cot_any, slope_ref, act_ref, gains_ref, shifts_ref, up0, up1, down0, down1,
    dsec_low_ref, hidden_ref, dpre_ref, out_ref, dsec_ref, part_ref, sums_ref, dpre_sum_ref, down_ref, up_ref,
    cot_ref, cot_sem,
):
    copy = own_copy(scalars, cot_any, cot_ref, cot_sem)
    blocks = blocks_of(resid_ref.shape[0])
    for rs in blocks:
        normed, _ = norm_parts(resid_ref[rs])
        hidden = normed * gains_ref[0:1] + shifts_ref[1:2]
        hidden_ref[rs] = hidden.astype(BF)
        second = hidden + (mine_ref[rs].astype(F32) + got_ref[rs].astype(F32)) + shifts_ref[2:3]
        n2, rstd2 = norm_parts(second)
        out_ref[rs] = (n2 * gains_ref[1:2] + shifts_ref[3:4]).astype(BF)
        lead = lax.broadcasted_iota(jnp.int32, (BLOCK, 1), 0) % SEG == 0
        if rs.start == 0:
            copy.wait()
        gy = jnp.where(lead, 0.0, cot_ref[rs].astype(F32))
        d_second = norm_back(gy, n2, rstd2, gains_ref[1:2])
        dsec_ref[rs] = d_second
        low = d_second.astype(BF)
        dsec_low_ref[rs] = low
        parts, pre_sums = [], []
        for j, (up, down) in enumerate(((up0, down0), (up1, down1))):
            at = (rs, slice(j * up.shape[1], (j + 1) * up.shape[1]))
            d_pre = (dot_t(low, down[...]) * slope_ref[at]).astype(BF)
            dpre_ref[at] = d_pre
            pre_sums.append(column_sum(d_pre.astype(F32)))
            parts.append(dot_t(d_pre, up[...]))
        part_ref[rs] = (parts[0] + parts[1]).astype(BF)
        sums = jnp.concatenate([column_sum(gy * n2), column_sum(d_second), column_sum(gy)], axis=0)
        pre_sums = jnp.concatenate(pre_sums, axis=0)
        if rs.start == 0:
            sums_ref[...] = sums
            dpre_sum_ref[...] = pre_sums
        else:
            sums_ref[...] += sums
            dpre_sum_ref[...] += pre_sums
    size = down_ref.shape[0]
    down_ref[...] = t_dot(act_ref[:, size:], dsec_low_ref[...]).astype(BF)
    up_ref[...] = t_dot(hidden_ref[...], dpre_ref[:, size:]).astype(BF)


def cut(side, value_ref, keep_ref, send_ref):
    rows = keep_ref.shape[0]
    keep_ref[...] = value_ref[pl.ds(pl.multiple_of(side * rows, rows), rows)]
    send_ref[...] = value_ref[pl.ds(pl.multiple_of((1 - side) * rows, rows), rows)]


def own_mlp_grads_body(
    sides_ref, act_ref, low_ref, hidden_ref, dpre_ref, got_down, got_up,
    keep_down, send_down, keep_up, send_up, down_ref, up_ref,
):
    size = down_ref.shape[0]
    down_ref[...] = (t_dot(act_ref[:, :size], low_ref[...]) + got_down[...].astype(F32)).astype(BF)
    cut(sides_ref[0], down_ref, keep_down, send_down)
    up_ref[...] = (t_dot(hidden_ref[...], dpre_ref[:, :size]) + got_up[...].astype(F32)).astype(BF)
    cut(sides_ref[1], up_ref, keep_up, send_up)


def add_cut(sides_ref, at, first, second):
    for j, (a_ref, b_ref, keep_ref, send_ref, sum_ref) in enumerate((first, second)):
        sum_ref[...] = (a_ref[...].astype(F32) + b_ref[...].astype(F32)).astype(BF)
        cut(sides_ref[at + j], sum_ref, keep_ref, send_ref)


def seg_out_back_body(
    scalars, resid_ref, mine_ref, got_ref, dsec_ref, gains_ref, wo_own, wo_oth,
    dres_ref, datt_ref, sums_ref,
    wo_ref,
):
    pair_weights(scalars[0], wo_own, wo_oth, wo_ref)
    for rs in blocks_of(resid_ref.shape[0]):
        n1, rstd1 = norm_parts(resid_ref[rs])
        d_hidden = (mine_ref[rs].astype(F32) + got_ref[rs].astype(F32)) + dsec_ref[rs]
        d_resid = norm_back(d_hidden, n1, rstd1, gains_ref[0:1])
        dres_ref[rs] = d_resid
        datt_ref[rs] = dot_t(d_resid.astype(BF), wo_ref[...]).astype(BF)
        sums = jnp.concatenate([column_sum(d_hidden * n1), column_sum(d_resid), column_sum(d_hidden)], axis=0)
        if rs.start == 0:
            sums_ref[...] = sums
        else:
            sums_ref[...] += sums


def mlp_rows(hidden_low, up0, up1, ub0, ub1, down0, down1, act_ref, slope_ref, part_ref, half_ref):
    for j, (up, ub, down) in enumerate(((up0, ub0, down0), (up1, ub1, down1))):
        act, slope = gelu_both(dot(hidden_low, up[...]) + ub[...])
        low = act.astype(BF)
        act_ref[j] = low
        slope_ref[j] = slope
        half_ref[j] = dot(low, down[...])
    part_ref[...] = (half_ref[0] + half_ref[1]).astype(BF)


def mlp_rows_back(low, slope_ref, up0, up1, down0, down1, dpre_ref, part_ref, half_ref):
    for j, (up, down) in enumerate(((up0, down0), (up1, down1))):
        d_pre = (dot_t(low, down[...]) * slope_ref[j]).astype(BF)
        dpre_ref[j] = d_pre
        half_ref[j] = dot_t(d_pre, up[...])
    part_ref[...] = (half_ref[0] + half_ref[1]).astype(BF)


def lead_mlp_body(
    message_ref, gains_ref, shifts_ref, up0, up1, ub0, ub1, down0, down1,
    resid_ref, hidden_ref, act_ref, slope_ref, part_ref, half_ref,
):
    model = resid_ref.shape[1]
    resid = message_ref[:, :model].astype(F32) + message_ref[:, model : 2 * model].astype(F32) + shifts_ref[0:1]
    resid_ref[...] = resid
    n1, _ = norm_parts(resid)
    hidden_low = (n1 * gains_ref[0:1] + shifts_ref[1:2]).astype(BF)
    hidden_ref[...] = hidden_low
    mlp_rows(hidden_low, up0, up1, ub0, ub1, down0, down1, act_ref, slope_ref, part_ref, half_ref)


def cls_attention_body(
    scalars, resid_ref, mine_ref, got_ref, sgains_ref, sshifts_ref, owner_row, owner_col, place_col, table_ref,
    own_ref, oth_ref, b_own, b_oth, wo_own, wo_oth,
    second_ref, value_ref, q_ref, k_ref, v_ref, att_ref, part_ref,
    w_ref, wo_ref,
):
    pair = q_ref.shape[1]
    pair_weights(scalars[0], own_ref, oth_ref, w_ref)
    pair_weights(scalars[0], wo_own, wo_oth, wo_ref)
    bias = pair_bias(scalars[0], b_own, b_oth)
    n1, _ = norm_parts(resid_ref[...])
    hidden = n1 * sgains_ref[0:1] + sshifts_ref[1:2]
    second = hidden + (mine_ref[...].astype(F32) + got_ref[...].astype(F32)) + sshifts_ref[2:3]
    second_ref[...] = second
    n2, _ = norm_parts(second)
    first = n2 * sgains_ref[1:2] + sshifts_ref[3:4]
    slots, places = resid_ref.shape[0], table_ref.shape[0]
    index = lax.broadcasted_iota(jnp.int32, (slots, places), 1).astype(F32)
    hot = (index == place_col[...]).astype(F32).astype(BF)
    value = first + dot(hot, table_ref[...])
    value_ref[...] = value
    low = value.astype(BF)
    q_ref[...] = (dot_t(low, w_ref[:pair]) + bias[0:1]).astype(BF)
    k_ref[...] = dot_t(low, w_ref[pair : 2 * pair]).astype(BF)
    v_ref[...] = (dot_t(low, w_ref[2 * pair :]) + bias[1:2]).astype(BF)
    allowed = owner_row[...] == owner_col[...]
    masks = head_masks(BF)
    for col in range(0, pair, LANES):
        at = slice(col, col + LANES)
        q, k, v = q_ref[:, at], k_ref[:, at], v_ref[:, at]
        tile = None
        for mask in masks:
            scores = jnp.where(allowed, dot_t(q * mask, k) * 0.125, -1000000000.0)
            one = dot(softmax(scores).astype(BF), v * mask)
            tile = one if tile is None else tile + one
        att_ref[:, at] = tile.astype(BF)
    part_ref[...] = dot(att_ref[...], wo_ref[...]).astype(BF)


def cls_mlp_body(
    value_ref, mine_ref, got_ref, gains_ref, shifts_ref, up0, up1, ub0, ub1, down0, down1,
    resid_ref, hidden_ref, act_ref, slope_ref, part_ref, half_ref,
):
    resid = value_ref[...] + (mine_ref[...].astype(F32) + got_ref[...].astype(F32)) + shifts_ref[0:1]
    resid_ref[...] = resid
    n1, _ = norm_parts(resid)
    hidden_low = (n1 * gains_ref[0:1] + shifts_ref[1:2]).astype(BF)
    hidden_ref[...] = hidden_low
    mlp_rows(hidden_low, up0, up1, ub0, ub1, down0, down1, act_ref, slope_ref, part_ref, half_ref)


def cls_mlp_back_body(
    resid_ref, mine_ref, got_ref, message_ref, slope_ref, gains_ref, shifts_ref, up0, up1, down0, down1,
    sides_ref, kept_down, came_down, kept_up, came_up,
    result_ref, dsec_ref, dpre_ref, part_ref, sums_ref, keep_down, send_down, keep_up, send_up,
    half_ref, down_ref, up_ref,
):
    add_cut(sides_ref, 2, (kept_down, came_down, keep_down, send_down, down_ref), (kept_up, came_up, keep_up, send_up, up_ref))
    n1, _ = norm_parts(resid_ref[...])
    hidden = n1 * gains_ref[0:1] + shifts_ref[1:2]
    second = hidden + (mine_ref[...].astype(F32) + got_ref[...].astype(F32)) + shifts_ref[2:3]
    n2, rstd2 = norm_parts(second)
    result_ref[...] = n2 * gains_ref[1:2] + shifts_ref[3:4]
    gy = message_ref[:, 2 * result_ref.shape[1] :].astype(F32)
    d_second = norm_back(gy, n2, rstd2, gains_ref[1:2])
    dsec_ref[...] = d_second
    mlp_rows_back(d_second.astype(BF), slope_ref, up0, up1, down0, down1, dpre_ref, part_ref, half_ref)
    sums_ref[...] = jnp.concatenate([column_sum(gy * n2), column_sum(d_second), column_sum(gy)], axis=0)


def cls_attention_back_body(
    scalars, resid_ref, mine_ref, got_ref, dsec_ref, gains_ref, q_ref, k_ref, v_ref, owner_row, owner_col,
    own_ref, oth_ref, wo_own, wo_oth,
    dres_ref, dres_low_ref, dmix_ref, part_ref, sums_ref,
    w_ref, wo_ref,
):
    pair = q_ref.shape[1]
    pair_weights(scalars[0], own_ref, oth_ref, w_ref)
    pair_weights(scalars[0], wo_own, wo_oth, wo_ref)
    n1, rstd1 = norm_parts(resid_ref[...])
    d_hidden = (mine_ref[...].astype(F32) + got_ref[...].astype(F32)) + dsec_ref[...]
    d_resid = norm_back(d_hidden, n1, rstd1, gains_ref[0:1])
    dres_ref[...] = d_resid
    low = d_resid.astype(BF)
    dres_low_ref[...] = low
    sums_ref[...] = jnp.concatenate(
        [column_sum(d_hidden * n1), column_sum(d_resid), column_sum(d_hidden)], axis=0
    )
    d_att = dot_t(low, wo_ref[...]).astype(BF)
    allowed = owner_row[...] == owner_col[...]
    masks = head_masks(BF)
    for col in range(0, pair, LANES):
        at = slice(col, col + LANES)
        q, k, v, g = q_ref[:, at], k_ref[:, at], v_ref[:, at], d_att[:, at]
        total = [None] * 3
        for mask in masks:
            qm, gm = q * mask, g * mask
            probs = softmax(jnp.where(allowed, dot_t(qm, k) * 0.125, -1000000000.0))
            d_prob = dot_t(gm, v)
            ds = (probs * (d_prob - jnp.sum(probs * d_prob, axis=-1, keepdims=True))).astype(BF)
            one = [dot(ds, k * mask), t_dot(ds, qm), t_dot(probs.astype(BF), gm)]
            total = [a if b is None else a + b for a, b in zip(one, total)]
        for j, scale in enumerate((0.125, 0.125, 1.0)):
            dmix_ref[:, j * pair + col : j * pair + col + LANES] = (total[j] * scale).astype(BF)
    part_ref[...] = dot(dmix_ref[...], w_ref[...]).astype(BF)


def lead_mlp_back_body(
    mine_ref, got_ref, dres_ref, second_ref, slope_ref, sgains_ref, place_row, up0, up1, down0, down1,
    sides_ref, kept_down, came_down, kept_up, came_up,
    dsec_ref, dsec_low_ref, dpre_ref, part_ref, sums_ref, pos_ref, keep_ref, send_ref,
    half_ref, down_ref, up_ref,
):
    cut_last(sides_ref[4], (kept_down, came_down, down_ref), (kept_up, came_up, up_ref), keep_ref, send_ref)
    gy = (mine_ref[...].astype(F32) + got_ref[...].astype(F32)) + dres_ref[...]
    n2, rstd2 = norm_parts(second_ref[...])
    d_second = norm_back(gy, n2, rstd2, sgains_ref[1:2])
    dsec_ref[...] = d_second
    low = d_second.astype(BF)
    dsec_low_ref[...] = low
    mlp_rows_back(low, slope_ref, up0, up1, down0, down1, dpre_ref, part_ref, half_ref)
    sums_ref[...] = jnp.concatenate([column_sum(gy * n2), column_sum(d_second), column_sum(gy)], axis=0)
    places, slots = pos_ref.shape[0], gy.shape[0]
    index = lax.broadcasted_iota(jnp.int32, (places, slots), 0).astype(F32)
    hot = (index == place_row[...]).astype(F32)
    pos_ref[...] = lax.dot_general(
        hot, gy, (((1,), (0,)), ((), ())), preferred_element_type=F32, precision=lax.Precision.HIGHEST
    )


def seg_attention_back_body(
    scalars, lresid_ref, lmine_ref, lgot_ref, ldsec_ref, gains_ref, wo_own, wo_oth, own_ref, oth_ref,
    q_ref, k_ref, v_ref, datt_ref, dres_ref, sums_a, sums_b, dpre_sums,
    part_ref, dres_out, dmix_ref, lsums_ref, rows_ref,
    lead_dres, lead_datt, datt_all, w_ref, wo_ref,
):
    rows, pair = q_ref.shape
    pair_weights(scalars[0], own_ref, oth_ref, w_ref)
    pair_weights(scalars[0], wo_own, wo_oth, wo_ref)
    n1, rstd1 = norm_parts(lresid_ref[...])
    d_hidden = (lmine_ref[...].astype(F32) + lgot_ref[...].astype(F32)) + ldsec_ref[...]
    d_resid = norm_back(d_hidden, n1, rstd1, gains_ref[0:1])
    lead_dres[...] = d_resid
    lead_datt[...] = dot_t(d_resid.astype(BF), wo_ref[...]).astype(BF).astype(F32)
    lsums_ref[...] = jnp.concatenate(
        [column_sum(d_hidden * n1), column_sum(d_resid), column_sum(d_hidden)], axis=0
    )
    masks = head_masks(BF)
    for row in range(0, rows, SEG):
        rs = slice(row, row + SEG)
        slot = scalars[1] + row // SEG
        dres_out[rs] = dres_ref[rs]
        dres_out[row : row + 1] = lead_dres[pl.ds(slot, 1)]
        datt_all[rs] = datt_ref[rs].astype(F32)
        datt_all[row : row + 1] = lead_datt[pl.ds(slot, 1)]
        ats = [(rs, slice(col, col + LANES)) for col in range(0, pair, LANES)]
        qs = [stacked(q_ref[at], masks) for at in ats]
        gs = [stacked(datt_all[at].astype(BF), masks) for at in ats]
        scores = [dot_t(q, k_ref[at]) * 0.125 for q, at in zip(qs, ats)]
        d_probs = [dot_t(g, v_ref[at]) for g, at in zip(gs, ats)]
        probs = [softmax(score) for score in scores]
        d_scores = [
            (p * (d - jnp.sum(p * d, axis=-1, keepdims=True))).astype(BF) for p, d in zip(probs, d_probs)
        ]
        for j, at in enumerate(ats):
            col = j * LANES
            both = jnp.concatenate([d_scores[j][:SEG], d_scores[j][SEG:]], axis=1)
            dmix_ref[rs, col : col + LANES] = (dot(both, stacked(k_ref[at], masks)) * 0.125).astype(BF)
            col += pair
            dmix_ref[rs, col : col + LANES] = (t_dot(d_scores[j], qs[j]) * 0.125).astype(BF)
            col += pair
            dmix_ref[rs, col : col + LANES] = t_dot(probs[j].astype(BF), gs[j]).astype(BF)
        if (row + SEG) % BLOCK == 0:
            at = slice(row + SEG - BLOCK, row + SEG)
            part_ref[at] = dot(dmix_ref[at], w_ref[...]).astype(BF)
    mixed = column_sum(dmix_ref[...].astype(F32))
    rows_ref[0:3] = sums_a[...]
    rows_ref[3:6] = sums_b[...]
    rows_ref[6:8] = jnp.zeros_like(rows_ref[6:8])
    rows_ref[6:7, :pair] = mixed[:, :pair]
    rows_ref[7:8, :pair] = mixed[:, 2 * pair :]
    rows_ref[8:10] = dpre_sums[...]


def attention_grads_body(
    scalars, dmix_ref, x_any, att_ref, dres_ref, kept_ref, came_ref,
    oth_a, oth_b, value_ref, own_a, own_b,
    full_ref, x_ref, x_sem,
):
    copy = own_copy(scalars, x_any, x_ref, x_sem)
    sum_body(kept_ref, came_ref, value_ref)
    core = scalars[0]
    d_mixed = dmix_ref[...]
    rows = d_mixed.shape[1]
    full_ref[rows:] = t_dot(att_ref[...], dres_ref[...].astype(BF)).astype(BF)
    copy.wait()
    full_ref[:rows] = t_dot(d_mixed, x_ref[...]).astype(BF)
    width = own_a.shape[0] // 2
    for part, (own_ref, oth_ref) in enumerate(((own_a, oth_a), (own_a, oth_a), (own_b, oth_b), (own_b, oth_b))):
        at = slice((part % 2) * width, (part % 2 + 1) * width)
        base = part * 2 * width
        own_ref[at] = full_ref[pl.ds(pl.multiple_of(base + core * width, width), width)]
        oth_ref[at] = full_ref[pl.ds(pl.multiple_of(base + (1 - core) * width, width), width)]


def two_cuts_body(at, sides_ref, a_mine, a_got, b_mine, b_got, keep_a, send_a, keep_b, send_b, a_ref, b_ref):
    add_cut(sides_ref, at, (a_mine, a_got, keep_a, send_a, a_ref), (b_mine, b_got, keep_b, send_b, b_ref))


def cut_last(side, first, second, keep_ref, send_ref):
    rows = keep_ref.shape[0] // 2
    for j, (mine, got, sum_ref) in enumerate((first, second)):
        sum_ref[...] = (mine[...].astype(F32) + got[...].astype(F32)).astype(BF)
        keep_ref[j * rows : (j + 1) * rows] = sum_ref[pl.ds(pl.multiple_of(side * rows, rows), rows)]
        send_ref[j * rows : (j + 1) * rows] = sum_ref[pl.ds(pl.multiple_of((1 - side) * rows, rows), rows)]


def last_cut_body(at, sides_ref, a_mine, a_got, b_mine, b_got, keep_ref, send_ref, a_ref, b_ref):
    cut_last(sides_ref[at], (a_mine, a_got, a_ref), (b_mine, b_got, b_ref), keep_ref, send_ref)


def sums_of(first, second, out_ref):
    rows = out_ref.shape[0] // 2
    for j, (mine, got) in enumerate((first, second)):
        out_ref[j * rows : (j + 1) * rows] = (mine[...].astype(F32) + got[...].astype(F32)).astype(BF)


def pieces_body(mine_ref, got_ref, a_ref, b_ref):
    rows = a_ref.shape[0]
    for j, out_ref in enumerate((a_ref, b_ref)):
        at = slice(j * rows, (j + 1) * rows)
        out_ref[...] = (mine_ref[at].astype(F32) + got_ref[at].astype(F32)).astype(BF)


def sums_join_body(step, sides_ref, keep_a, keep_b, z_mine, z_got, y_mine, y_got, out_ref, c_ref, d_ref):
    rows, whole = keep_a.shape[0], z_mine.shape[0] - keep_a.shape[0]
    sums_of((keep_a, z_got.at[pl.ds(0, rows)]), (keep_b, y_got.at[pl.ds(0, rows)]), out_ref)
    at = pl.ds(rows, whole)
    join(sides_ref[step], z_mine.at[at], z_got.at[at], c_ref)
    join(sides_ref[step + 1], y_mine.at[at], y_got.at[at], d_ref)


def parts_join(side, mine_ref, got_ref, a_ref, b_ref):
    rows = mine_ref.shape[0] // 2
    for j, out_ref in enumerate((a_ref, b_ref)):
        out_ref[pl.ds(pl.multiple_of(side * rows, rows), rows)] = mine_ref[j * rows : (j + 1) * rows]
        out_ref[pl.ds(pl.multiple_of((1 - side) * rows, rows), rows)] = got_ref[j * rows : (j + 1) * rows]


def first_join_body(at, sides_ref, mine_ref, got_ref, a_ref, b_ref):
    parts_join(sides_ref[at], mine_ref, got_ref, a_ref, b_ref)


def cut_first_join_body(
    at, step, sides_ref, a_mine, a_got, b_mine, b_got, mine_ref, got_ref,
    keep_a, z_ref, keep_b, y_ref, a_ref, b_ref,
):
    rows, whole = keep_a.shape[0], z_ref.shape[0] - keep_a.shape[0]
    sends, wholes = [[ref.at[pl.ds(at_row, size)] for ref in (z_ref, y_ref)] for at_row, size in ((0, rows), (rows, whole))]
    add_cut(sides_ref, at, (a_mine, a_got, keep_a, sends[0], a_ref), (b_mine, b_got, keep_b, sends[1], b_ref))
    parts_join(sides_ref[step], mine_ref, got_ref, *wholes)


def sum_body(a_ref, b_ref, out_ref):
    out_ref[...] = (a_ref[...].astype(F32) + b_ref[...].astype(F32)).astype(BF)


def join(side, a_ref, b_ref, out_ref):
    rows = a_ref.shape[0]
    out_ref[pl.ds(pl.multiple_of(side * rows, rows), rows)] = a_ref[...]
    out_ref[pl.ds(pl.multiple_of((1 - side) * rows, rows), rows)] = b_ref[...]


def two_joins_body(at, sides_ref, a_mine, a_got, b_mine, b_got, a_ref, b_ref):
    join(sides_ref[at], a_mine, a_got, a_ref)
    join(sides_ref[at + 1], b_mine, b_got, b_ref)


def attention_join_body(sides_ref, a_mine, a_got, b_mine, b_got, qkv_ref, out_ref):
    rows = a_mine.shape[0]
    for half_ref, which in ((a_mine, sides_ref[0]), (a_got, 1 - sides_ref[0])):
        qkv_ref[pl.ds(pl.multiple_of(which * rows, rows), rows)] = half_ref[...].astype(F32)
    low = sides_ref[1] == 0
    mine, got = b_mine[...].astype(F32), b_got[...].astype(F32)
    qkv_ref[2 * rows :] = jnp.where(low, mine, got)
    out_ref[...] = jnp.where(low, got, mine)


def layer_out_body(scalars, mine_ref, got_ref, result_mine, result_got, out_ref):
    step = pl.program_id(0)
    rows = out_ref.shape[0]
    steps = pl.num_programs(0) // 2
    value = jnp.where(step // steps == scalars[0], mine_ref[...].astype(F32), got_ref[...].astype(F32))
    row = lax.broadcasted_iota(jnp.int32, (rows, 1), 0)
    for j in range(rows // SEG):
        slot = scalars[2] + step * (rows // SEG) + j
        result = jnp.where(scalars[0] == 0, result_mine[pl.ds(slot, 1)], result_got[pl.ds(slot, 1)])
        value = jnp.where(row == j * SEG, result, value)
    out_ref[...] = value.astype(BF)


def tokens_grad_body(scalars, mine_ref, got_ref, out_ref):
    steps = pl.num_programs(0) // 2
    own = pl.program_id(0) // steps == scalars[0]

    @pl.when(own)
    def _():
        out_ref[...] = mine_ref[...]

    @pl.when(jnp.logical_not(own))
    def _():
        out_ref[...] = got_ref[...]


def tail_cores_body(mine_ref, got_ref, out_ref):
    out_ref[0:8] = mine_ref[0:8] + got_ref[0:8]
    out_ref[8:9] = mine_ref[8:9] + got_ref[9:10]


def finish_body(
    scalars, tail_ref, ub_ref, la_mine, lb_mine, ca_mine, cb_mine, pos_mine, la_got, lb_got, ca_got, cb_got, pos_got,
    gains_ref, shifts_ref, qv_ref, up_ref, cgains_ref, cshifts_ref, pos_ref,
):
    low = scalars[0] == 0

    def chosen(mine, got):
        return jnp.where(low, mine[...], got[...])

    def rows_of(a, b):
        return jnp.concatenate([b[0:1], a[0:1]], axis=0), jnp.concatenate([b[1:3], a[1:3]], axis=0)

    tail = tail_ref[...]
    la, lb = chosen(la_mine, la_got), chosen(lb_mine, lb_got)
    gains_ref[...], shifts_ref[...] = rows_of(tail[0:3] + la, tail[3:6] + lb)
    cgains_ref[...], cshifts_ref[...] = rows_of(chosen(ca_mine, ca_got), chosen(cb_mine, cb_got))
    pos_ref[...] = chosen(pos_mine, pos_got)
    width = qv_ref.shape[1]
    both = tail[6:8, : 2 * width]
    qv_ref[...] = jnp.where(low, both[:, :width], both[:, width:])
    up_ref[...] = tail[8:9] + ub_ref[...]


def add_rows_body(mine_ref, got_ref, dres_ref, out_ref):
    out_ref[...] = (mine_ref[...].astype(F32) + got_ref[...].astype(F32)) + dres_ref[...]


def cls_grads_body(
    scalars, mix_ref, low_ref, att_ref, dres_ref, hidden_ref, dpre_ref, act_ref, dsec_ref,
    qkv_out, bias_out, out_out, up_out, ub_out, down_out,
    full_ref,
):
    core = scalars[0]
    width = out_out.shape[0]
    pair = 2 * width

    def own(base):
        return full_ref[pl.ds(pl.multiple_of(base + core * width, width), width)]

    full_ref[...] = t_dot(mix_ref[...], low_ref[...].astype(BF))
    for part in range(3):
        qkv_out[part * width : (part + 1) * width] = own(part * pair)
    full_ref[:pair] = t_dot(att_ref[...], dres_ref[...])
    out_out[...] = own(0)
    sums = column_sum(mix_ref[...].astype(F32))
    for row, base in enumerate((0, 2 * pair)):
        bias_out[row : row + 1] = jnp.where(core == 0, sums[:, base : base + width], sums[:, base + width : base + pair])
    up_out[...] = t_dot(hidden_ref[...], dpre_ref[0])
    ub_out[...] = column_sum(dpre_ref[0].astype(F32))
    down_out[...] = t_dot(act_ref[0], dsec_ref[...].astype(BF))


def add_grads_body(sides_ref, hidden_ref, dpre_ref, act_ref, dsec_ref, down_a, down_b, up_a, up_b,
                   down_out, up_out, ub_out):
    for j, (a_ref, b_ref, out_ref) in enumerate(((down_a, down_b, down_out), (up_a, up_b, up_out))):
        rows = a_ref.shape[0]
        side = sides_ref[j]
        if j == 0:
            out_ref[...] = t_dot(act_ref[0], dsec_ref[...])
        else:
            out_ref[...] = t_dot(hidden_ref[...], dpre_ref[0])
        at = pl.ds(pl.multiple_of(side * rows, rows), rows)
        out_ref[at] = out_ref[at] + a_ref[...].astype(F32)
        at = pl.ds(pl.multiple_of((1 - side) * rows, rows), rows)
        out_ref[at] = out_ref[at] + b_ref[...].astype(F32)
    ub_out[...] = column_sum(dpre_ref[0].astype(F32))


def make_shards(n_dp):
    core_pairs = [(i, i ^ 1) for i in range(4)]
    x_pairs = [(i, i ^ 2) for i in range(4)]
    bits = [1 << k for k in range(n_dp.bit_length() - 1)]
    swapped = [bits[1], bits[0], *bits[2:]]

    def core_swap(value):
        return lax.ppermute(value, "mp", core_pairs)

    def x_swap(value):
        return lax.ppermute(value, "mp", x_pairs)

    def dp_swap(value, bit):
        return lax.ppermute(value, "dp", [(i, i ^ bit) for i in range(n_dp)])

    def shards(
        tokens,
        seg_counts,
        seg_order,
        seg_qkv,
        seg_qv_bias,
        seg_out,
        seg_up,
        seg_up_bias,
        seg_down,
        seg_gains,
        seg_shifts,
        cls_qkv,
        cls_qv_bias,
        cls_out,
        cls_up,
        cls_up_bias,
        cls_down,
        cls_gains,
        cls_shifts,
        pos_table,
        cotangent,
    ):
        outer = Outer()

        def run(*args, **options):
            if slots > 64:
                options["vmem"] = 56
            return call(outer, *args, **options)

        def tied(value, *others):
            result = tie(value, *others)
            if value in outer:
                outer.add(result)
            return result

        core = lax.axis_index("mp") % 2
        dp_index = lax.axis_index("dp")
        rows = tokens.shape[0] // 2
        own_segs = rows // SEG
        slots = seg_order.shape[0]
        width = seg_qkv.shape[2]
        pair = 2 * width
        model = tokens.shape[1]
        ff = seg_down.shape[0]
        places = pos_table.shape[0]

        def ordered(low_side, mine, other, axis):
            return jnp.where(
                low_side,
                jnp.concatenate([mine, other], axis=axis),
                jnp.concatenate([other, mine], axis=axis),
            )

        def paired(value, axis):
            return ordered(core == 0, value, core_swap(value), axis)

        def gather_slots(value, last_after):
            value = paired(value, 0)
            for bit in bits:
                if bit == bits[1]:
                    before = value
                    value = tied(value, last_after)
                value = ordered((dp_index & bit) == 0, value, dp_swap(value, bit), 0)
            return value, before

        def half(value, which, axis):
            size = value.shape[axis] // 2
            return lax.dynamic_slice_in_dim(value, which * size, size, axis)

        def own_half(value, axis):
            return half(value, core, axis)

        def side_of(bit):
            return jnp.where((dp_index & bit) == 0, 0, 1).astype(jnp.int32).reshape(1)

        def two_cuts(step, a, a_got, b, b_got):
            size = a.shape[0] // 2
            if size % 16 == 0:
                return run(
                    functools.partial(two_cuts_body, 2 * step),
                    [((size, model), BF)] * 4,
                    (sides, a, a_got, b, b_got),
                    "two_cuts",
                    far=(0, 2),
                    scratch=[pltpu.VMEM(a.shape, BF), pltpu.VMEM(b.shape, BF)],
                )
            out = []
            for mine, got, bit in ((a, a_got, bits[step]), (b, b_got, swapped[step])):
                value = (mine.astype(F32) + got.astype(F32)).astype(BF)
                side = side_of(bit)[0]
                out += [half(value, side, 0), half(value, 1 - side, 0)]
            return out

        last = len(bits) - 1

        def last_cut(a, a_got, b, b_got):
            size = a.shape[0] // 2
            if size % 16 == 0:
                return run(
                    functools.partial(last_cut_body, 2 * last),
                    [((2 * size, model), BF)] * 2,
                    (sides, a, a_got, b, b_got),
                    "last_cut",
                    far=(0,),
                    scratch=[pltpu.VMEM(a.shape, BF), pltpu.VMEM(b.shape, BF)],
                )
            keep_a, send_a, keep_b, send_b = two_cuts(last, a, a_got, b, b_got)
            return jnp.concatenate([keep_a, keep_b], axis=0), jnp.concatenate([send_a, send_b], axis=0)

        def last_sum(keep, send):
            return run(sum_body, [(keep.shape, BF)], (keep, dp_swap(send, bits[-1])), "last_sum")[0]

        def pieces_of(a, a_got, b, b_got):
            parts = [(mine.astype(F32) + got.astype(F32)).astype(BF) for mine, got in ((a, a_got), (b, b_got))]
            return jnp.concatenate(parts, axis=0)

        def last_sums(pieces, got):
            rows = pieces.shape[0] // 2
            if rows % 16 == 0:
                return run(pieces_body, [((rows, model), BF)] * 2, (pieces, got), "last_sums")
            value = (pieces.astype(F32) + got.astype(F32)).astype(BF)
            return value[:rows], value[rows:]

        def first_join(value, got):
            rows = value.shape[0] // 2
            if rows % 16 == 0:
                return run(
                    functools.partial(first_join_body, 2 * last),
                    [((2 * rows, model), BF)] * 2,
                    (sides, value, got),
                    "first_join",
                )
            low = (dp_index & bits[-1]) == 0
            return ordered(low, value[:rows], got[:rows], 0), ordered(low, value[rows:], got[rows:], 0)

        def two_joins(step, a, a_got, b, b_got):
            if a.shape[0] % 16 == 0:
                return run(
                    functools.partial(two_joins_body, 2 * step),
                    [((2 * a.shape[0], model), BF), ((2 * b.shape[0], model), BF)],
                    (sides, a, a_got, b, b_got),
                    "two_joins",
                )
            return (
                ordered((dp_index & bits[step]) == 0, a, a_got, 0),
                ordered((dp_index & swapped[step]) == 0, b, b_got, 0),
            )

        sides = jnp.concatenate([side_of(bit) for two in zip(bits, swapped) for bit in two])
        outer.add(seg_gains, seg_shifts, cls_gains, cls_shifts, pos_table)
        scalars = jnp.stack([core, (dp_index * 2 + core) * own_segs, dp_index * 2 * own_segs]).astype(jnp.int32)

        def weights(qkv, qv_bias, out, up, up_bias, down):
            flat = jnp.transpose(qkv, (1, 2, 0))
            bias = up_bias.reshape(1, ff)
            outs = out.reshape(1, width, model)
            heads = (flat, core_swap(flat), qv_bias, core_swap(qv_bias), outs, core_swap(outs))
            hidden = (up, core_swap(up), down, core_swap(down), bias, core_swap(bias))
            outer.add(heads[0], heads[4], *hidden)
            return heads, hidden

        s_heads, (s_up0, s_up1, s_down0, s_down1, *s_ub) = weights(
            seg_qkv, seg_qv_bias, seg_out, seg_up, seg_up_bias, seg_down
        )
        c_heads, (c_up0, c_up1, c_down0, c_down1, *c_ub) = weights(
            cls_qkv, cls_qv_bias, cls_out, cls_up, cls_up_bias, cls_down
        )

        c_swapped = (c_heads[1], c_heads[3], c_heads[5], c_up1, c_down1, c_ub[1])
        part1, lead_part, lead_rest, q, k, v, att = run(
            seg_attention_body,
            [((rows, model), BF), ((own_segs, model), F32), ((own_segs, 2 * model), F32)]
            + [((rows, pair), BF)] * 4,
            (scalars, tokens, cotangent, tied(s_heads[0], s_ub[1]), *s_heads[1:]),
            "seg_attention",
            far=(0, 3, 4, 5, 6),
            scratch=[
                pltpu.VMEM((3 * pair, model), BF),
                pltpu.VMEM((pair, model), BF),
                pltpu.VMEM((rows, model), BF),
                pltpu.VMEM((own_segs, 16, model), BF),
                pltpu.SemaphoreType.DMA,
                pltpu.SemaphoreType.DMA((own_segs,)),
            ],
            vmem=18,
            stay=(1, 2),
        )
        lead_sum = lead_part + x_swap(lead_part)
        got1 = x_swap(part1)
        message, before_last = gather_slots(jnp.concatenate([lead_sum.astype(BF), lead_rest.astype(BF)], axis=1), got1)

        owner_row, owner_col, place_row, place_col = run(
            layout_body,
            [((1, slots), F32), ((slots, 1), F32), ((1, slots), F32), ((slots, 1), F32)],
            (seg_counts.reshape(1, -1), seg_order.reshape(1, -1)),
            "layout",
            far=(0, 1, 2, 3),
        )
        mlp_weights = (s_up0, s_up1, s_down0, s_down1)
        l_resid, l_hidden, l_act, l_slope, l_part = run(
            lead_mlp_body,
            [((slots, model), F32), ((slots, model), BF), ((2, slots, ff), BF), ((2, slots, ff), F32),
             ((slots, model), BF)],
            (tied(message, owner_row, *c_swapped), seg_gains, seg_shifts, s_up0, s_up1, *s_ub, s_down0, s_down1),
            "lead_mlp",
            far=(0, 1, 2, 3),
            scratch=[pltpu.VMEM((2, slots, model), F32)],
        )
        got_l1 = x_swap(l_part)

        part2, resid, act, slope = run(
            seg_mlp_body,
            [((rows, model), BF), ((rows, model), F32), ((rows, 2 * ff), BF), ((rows, 2 * ff), F32)],
            (scalars, tokens, tied(part1, before_last), got1, seg_gains, seg_shifts, s_up0, s_up1, *s_ub, s_down0, s_down1),
            "seg_mlp",
            far=(0, 1, 2, 3),
            scratch=[pltpu.VMEM((rows, model), BF), pltpu.SemaphoreType.DMA],
            stay=(1,),
            vmem=18,
        )
        l_second, c_value, c_q, c_k, c_v, c_att, c_part1 = run(
            cls_attention_body,
            [((slots, model), F32)] * 2
            + [((slots, pair), BF)] * 4
            + [((slots, model), BF)],
            (scalars, l_resid, l_part, got_l1, seg_gains, seg_shifts, owner_row, owner_col, place_col,
             pos_table, *c_heads),
            "cls_attention",
            far=(0, 1, 2, 3, 4, 5),
            scratch=[pltpu.VMEM((3 * pair, model), BF), pltpu.VMEM((pair, model), BF)],
        )
        got2 = x_swap(part2)
        outer.add(got2)
        d_second_low, hidden_low, d_pre, first_low, d_second, part3, sums_a, d_pre_sum, down_oth, up_oth = run(
            seg_mlp_back_body,
            [((rows, model), BF), ((rows, model), BF), ((rows, 2 * ff), BF), ((rows, model), BF),
             ((rows, model), F32), ((rows, model), BF), ((3, model), F32), ((2, ff), F32),
             ((ff, model), BF), ((model, ff), BF)],
            (scalars, resid, tied(part2, l_part), got2, cotangent, slope, tied(act, got_l1), seg_gains,
             seg_shifts, *mlp_weights),
            "seg_mlp_back",
            far=(0, 1, 2, 3, 4, 5, 6, 7),
            scratch=[pltpu.VMEM((rows, model), BF), pltpu.SemaphoreType.DMA],
            stay=(4,),
            vmem=24,
        )
        got3 = x_swap(part3)
        keep_down, send_down, keep_up, send_up = run(
            own_mlp_grads_body,
            [((ff // 2, model), BF)] * 2 + [((model // 2, ff), BF)] * 2,
            (sides, tied(act, c_part1), d_second_low, hidden_low, d_pre, core_swap(down_oth), core_swap(up_oth)),
            "seg_own_mlp_grads",
            far=(0, 2),
            scratch=[pltpu.VMEM((ff, model), BF), pltpu.VMEM((model, ff), BF)],
        )
        got_c1 = tied(x_swap(c_part1), send_down, send_up, got3)
        c_resid, c_hidden, c_act, c_slope, c_part2 = run(
            cls_mlp_body,
            [((slots, model), F32), ((slots, model), BF), ((2, slots, ff), BF), ((2, slots, ff), F32),
             ((slots, model), BF)],
            (c_value, c_part1, got_c1, cls_gains, cls_shifts, c_up0, c_up1, *c_ub, c_down0, c_down1),
            "cls_mlp",
            far=(0, 1, 2, 3),
            scratch=[pltpu.VMEM((2, slots, model), F32)],
        )

        quarter = ff // 4
        c_result, c_d_second, c_d_pre, c_part3, c_sums_a, keep_down, send_down, keep_up, send_up = run(
            cls_mlp_back_body,
            [((slots, model), F32), ((slots, model), F32), ((2, slots, ff), BF), ((slots, model), BF),
             ((3, model), F32)] + [((quarter, model), BF)] * 4,
            (c_resid, c_part2, x_swap(c_part2), message, c_slope, cls_gains, cls_shifts, c_up0, c_up1, c_down0, c_down1,
             sides, keep_down, dp_swap(send_down, bits[0]), keep_up, dp_swap(send_up, swapped[0])),
            "cls_mlp_back",
            far=(0, 1, 2, 4, 5, 7),
            scratch=[pltpu.VMEM((2, slots, model), F32)] + [pltpu.VMEM((2 * quarter, model), BF)] * 2,
        )
        c_d_resid, c_d_resid_low, c_d_mixed, c_part4, c_sums_b = run(
            cls_attention_back_body,
            [((slots, model), F32), ((slots, model), BF), ((slots, 3 * pair), BF), ((slots, model), BF),
             ((3, model), F32)],
            (scalars, c_resid, c_part3, x_swap(c_part3), c_d_second, cls_gains, c_q, c_k, c_v,
             owner_row, owner_col, c_heads[0], c_heads[1], c_heads[4], c_heads[5]),
            "cls_attention_back",
            far=(0, 1, 2, 4),
            scratch=[pltpu.VMEM((3 * pair, model), BF), pltpu.VMEM((pair, model), BF)],
        )

        for step in range(2, last):
            keep_down, send_down, keep_up, send_up = two_cuts(
                step, keep_down, dp_swap(send_down, bits[step - 1]), keep_up, dp_swap(send_up, swapped[step - 1])
            )
        fused = last == 2
        kept = (keep_down, dp_swap(send_down, bits[last - 1]), keep_up, dp_swap(send_up, swapped[last - 1]))
        if not fused:
            keep_mlp, send_mlp = last_cut(*kept)
            kept = (down_oth[:32], down_oth[:32], down_oth[:32], down_oth[:32])
        eighth = kept[0].shape[0] // 2
        l_d_second, l_d_second_low, l_d_pre, l_part3, l_sums_a, pos_grad, *cuts = run(
            lead_mlp_back_body,
            [((slots, model), F32), ((slots, model), BF), ((2, slots, ff), BF), ((slots, model), BF),
             ((3, model), F32), ((places, model), F32)] + [((2 * eighth, model), BF)] * 2,
            (c_part4, x_swap(c_part4), c_d_resid, l_second, l_slope, seg_gains, place_row,
             *mlp_weights, sides, *kept),
            "lead_mlp_back",
            far=(0, 1, 2, 4, 5, 6),
            scratch=[pltpu.VMEM((2, slots, model), F32)] + [pltpu.VMEM((2 * eighth, model), BF)] * 2,
        )
        if fused:
            keep_mlp, send_mlp = cuts
        d_resid, d_att, sums_b = run(
            seg_out_back_body,
            [((rows, model), F32), ((rows, pair), BF), ((3, model), F32)],
            (scalars, resid, part3, tied(got3, l_part3), d_second, seg_gains, s_heads[4], s_heads[5]),
            "seg_out_back",
            far=(2,),
            scratch=[pltpu.VMEM((pair, model), BF)],
        )
        part4, d_resid, d_mixed, l_sums_b, tail = run(
            seg_attention_back_body,
            [((rows, model), BF), ((rows, model), F32), ((rows, 3 * pair), BF), ((3, model), F32), ((10, model), F32)],
            (scalars, l_resid, l_part3, x_swap(l_part3), l_d_second, seg_gains, s_heads[4], s_heads[5],
             s_heads[0], s_heads[1], q, k, v, d_att, d_resid, sums_a, sums_b, d_pre_sum),
            "seg_attention_back",
            far=(1, 3),
            scratch=[
                pltpu.VMEM((slots, model), F32),
                pltpu.VMEM((slots, pair), F32),
                pltpu.VMEM((rows, pair), F32),
                pltpu.VMEM((3 * pair, model), BF),
                pltpu.VMEM((pair, model), BF),
            ],
            vmem=18,
        )
        got4 = x_swap(part4)
        tail = run(tail_cores_body, [((9, model), F32)], (tail, core_swap(tail)), "tail_cores")[0]
        tails = [tail]
        for bit in bits:
            tails.append(tails[-1] + dp_swap(tails[-1], bit))
        tail = tails[-1]
        oth_a, oth_b, value_mlp, own_a, own_b = run(
            attention_grads_body,
            [((2 * width, model), BF)] * 2 + [(keep_mlp.shape, BF)] + [((2 * width, model), BF)] * 2,
            (scalars, d_mixed, tokens, att, d_resid, keep_mlp, dp_swap(send_mlp, bits[-1])),
            "seg_attention_grads",
            far=(3, 4),
            scratch=[pltpu.VMEM((8 * width, model), BF), pltpu.VMEM((rows, model), BF), pltpu.SemaphoreType.DMA],
            stay=(2,),
        )
        keep_a, send_a, keep_b, send_b = two_cuts(0, own_a, core_swap(oth_a), own_b, core_swap(oth_b))
        got_mlp = dp_swap(value_mlp, bits[-1])
        cg_qkv, cg_bias, cg_out, cg_up, cg_ub, cg_down = run(
            cls_grads_body,
            [((3 * width, model), F32), ((2, width), F32), ((width, model), F32), ((model, ff), F32),
             ((1, ff), F32), ((ff, model), F32)],
            (scalars, tied(c_d_mixed, send_a, send_b), c_value, c_att, c_d_resid_low, c_hidden, c_d_pre, c_act, c_d_second),
            "cls_grads",
            scratch=[pltpu.VMEM((3 * pair, model), F32)],
        )
        layer_out = call_blocks(
            layer_out_body,
            [((2 * rows, model), BF)],
            scalars,
            (tied(first_low, send_a, send_b), core_swap(first_low), c_result, core_swap(c_result)),
            "layer_out",
            2 * rows // BLOCK,
            BLOCK,
            "mmww",
        )[0]
        for step in range(last):
            if step > 0:
                if fused:
                    both = (width // 2 + value_mlp.shape[0], model)
                    keep_a, send_a, keep_b, send_b = run(
                        functools.partial(cut_first_join_body, 2 * step, 2 * last),
                        [((width // 2, model), BF), (both, BF)] * 2,
                        (sides, *a_next, *b_next, value_mlp, got_mlp),
                        "cut_first_join",
                        far=(0, 2),
                        scratch=[pltpu.VMEM((width, model), BF)] * 2,
                    )
                else:
                    keep_a, send_a, keep_b, send_b = two_cuts(step, *a_next, *b_next)
            if step == 1:
                d_rows = run(add_rows_body, [((rows, model), F32)], (part4, tied(got4, send_a, send_b), d_resid), "add_rows")[0]
                tokens_grad = call_blocks(
                    tokens_grad_body,
                    [((2 * rows, model), F32)],
                    scalars,
                    (d_rows, core_swap(d_rows)),
                    "tokens_grad",
                    2 * rows // BLOCK,
                    BLOCK,
                    "mm",
                )[0]
            others = [tails[step]] + ([cg_bias, layer_out] if step == 0 else [])
            got_a, got_b = dp_swap(send_a, bits[step]), dp_swap(send_b, swapped[step])
            a_next, b_next = (keep_a, tied(got_a, *others)), (keep_b, got_b)
        if fused:
            size = a_next[0].shape[0]
            pieces, down, up = run(
                functools.partial(sums_join_body, 2),
                [((2 * size, model), BF)] + [((2 * value_mlp.shape[0], model), BF)] * 2,
                (sides, a_next[0], b_next[0], send_a, a_next[1], send_b, b_next[1]),
                "sums_join",
            )
        else:
            pieces = pieces_of(*a_next, *b_next)
            down, up = first_join(value_mlp, got_mlp)
            for at in range(last - 1, 0, -1):
                down, up = two_joins(at, down, dp_swap(down, bits[at]), up, dp_swap(up, swapped[at]))
        grad_down, grad_up, l_up_bias = run(
            add_grads_body,
            [((ff, model), F32), ((model, ff), F32), ((1, ff), F32)],
            (sides, l_hidden, l_d_pre, l_act, l_d_second_low,
             down, dp_swap(down, bits[0]), up, dp_swap(up, swapped[0])),
            "seg_add_grads",
        )
        value_a, value_b = last_sums(pieces, tied(dp_swap(pieces, bits[-1]), tokens_grad))
        for step in range(last - 1, 0, -1):
            got_a, got_b = dp_swap(value_a, bits[step]), dp_swap(value_b, swapped[step])
            if step == 1:
                got_a = tied(got_a, l_up_bias, tails[2])
            value_a, value_b = two_joins(step, value_a, got_a, value_b, got_b)
        a_parts = (value_a, dp_swap(value_a, bits[0]))
        b_parts = (value_b, dp_swap(value_b, swapped[0]))
        lead_sums = (l_sums_a, l_sums_b, c_sums_a, c_sums_b, pos_grad)
        m_gains, m_shifts, qv_total, up_total, cls_gains_grad, cls_shifts_grad, pos_grad = run(
            finish_body,
            [((2, model), F32), ((4, model), F32), ((2, width), F32), ((1, ff), F32), ((2, model), F32),
             ((4, model), F32), ((places, model), F32)],
            (scalars, tail, l_up_bias, *lead_sums, *[core_swap(part) for part in lead_sums]),
            "finish",
        )

        g_qkv, g_out = run(
            attention_join_body,
            [((3 * width, model), F32), ((width, model), F32)],
            (sides, tied(a_parts[0], m_gains), a_parts[1], *b_parts),
            "seg_attention_join",
        )
        def unflatten(flat):
            return jnp.transpose(flat.reshape(3, width, model), (2, 0, 1))

        seg_grads = (
            unflatten(g_qkv),
            qv_total,
            g_out,
            grad_up,
            up_total[0],
            grad_down,
            m_gains,
            m_shifts,
        )
        cls_grads = (
            unflatten(cg_qkv),
            cg_bias,
            cg_out,
            cg_up,
            cg_ub[0],
            cg_down,
            cls_gains_grad,
            cls_shifts_grad,
        )
        return (layer_out, tokens_grad, *seg_grads, *cls_grads, pos_grad)

    return shards


def solution(mesh):
    in_specs = (
        P("dp", None),
        P(),
        P(),
        P(None, None, "mp"),
        P(None, "mp"),
        P("mp", None),
        P(None, "mp"),
        P("mp"),
        P("mp", None),
        P(),
        P(),
        P(None, None, "mp"),
        P(None, "mp"),
        P("mp", None),
        P(None, "mp"),
        P("mp"),
        P("mp", None),
        P(),
        P(),
        P(),
        P("dp", None),
    )
    out_specs = (
        P("dp", None),
        P("dp", None),
        P(None, None, "mp"),
        P(None, "mp"),
        P("mp", None),
        P(None, "mp"),
        P("mp"),
        P("mp", None),
        P(),
        P(),
        P(None, None, "mp"),
        P(None, "mp"),
        P("mp", None),
        P(None, "mp"),
        P("mp"),
        P("mp", None),
        P(),
        P(),
        P(),
    )
    return jax.shard_map(
        make_shards(mesh.shape["dp"]), mesh=mesh, in_specs=in_specs, out_specs=out_specs, check_vma=False
    )
```
